32 devices in a mesh: cfg: 2 (over x), ta: 2 (over core), sa: 8 (over z, y).
Axes of the slice: x: 2, y: 2, z: 4, core: 2. Of those that a mesh axis runs over, the one named last changes fastest.
Arguments:
- links: float32 [4, 3, 2, 3, 3, 32, 1024], P(None, None, None, None, None, 'sa', 'ta'), may hold values from -2.5 to 2.5
- vectors: float32 [4, 16, 2, 3, 32, 1024], P('ta', None, None, None, 'sa'), may hold values from -6 to 6
Outputs:
- filtered: float32 [8, 16, 2, 3, 32, 1024], P(('cfg', 'ta'), None, None, None, 'sa'), parts along dimension 0
- grams: float32 [8, 2, 2, 16, 16], P(('cfg', 'ta')), parts along dimension 0
The draws below stay inside these ranges and needn't reach their ends.
There are 2 independent parts, one for each index of `cfg`. The reference program is written for one: setup_inputs(seed, part) draws one part's arguments, and reference() takes and returns one part's arrays. A program takes and returns all parts, laid end to end along the dimension named above; an argument that names none is the same for every part. Nothing has to cross between parts.
All inputs are finite; a program needn't handle non-finite values.
Results may differ from the reference program's by a relative error of at most 0.00011.
Values sent between devices are 32-bit elements; how exact they have to be, the bound alone decides.
No kernel may reach another device: no remote copies, remote signals or barrier semaphores. Data moves between devices by JAX's collectives and lax.ppermute only.
A program may use at most 256 MiB of HBM per device.

```python
import jax
import jax.numpy as jnp
from jax import lax

LX = 32
LY = 32
LZ = 32
NVEC = 16
DEG = 3
NT = 4


def block_levels(key, shape, pieces, smallest, largest):
    gain, own = 1.0, jax.random.fold_in(key, 6)
    for dim, blocks in pieces:
        draws = jnp.exp(jax.random.uniform(jax.random.fold_in(own, dim), (blocks,), jnp.float32, smallest / len(pieces), largest / len(pieces)))
        gain = gain * jnp.repeat(draws, shape[dim] // blocks).reshape([-1 if axis == dim else 1 for axis in range(len(shape))])
    return gain


def gaussian(own_key, extent, spread, bound, cuts=(), dtype=jnp.bfloat16):
    entries = spread * jax.random.normal(own_key, extent, jnp.float32)
    if cuts:
        entries = entries * block_levels(own_key, extent, cuts, -0.22, 0.18)
    return jnp.clip(entries, -bound, bound).astype(dtype)


def setup_inputs(seed: int = 0, part: int = 0) -> dict:
    key_list = jax.random.split(jax.random.key(seed), 3)
    return {
        "links": gaussian(key_list[0], (NT, 3, 2, 3, 3, LZ, LY * LX), 0.41, 2.5, ((5, 8), (6, 2)), jnp.float32),
        "vectors": gaussian(key_list[1], (NT, NVEC, 2, 3, LZ, LY * LX), 1.0, 6.0, ((0, 2), (4, 8)), jnp.float32),
    }


def mat_vec(matrix, field):
    mat_re = matrix[:, None, 0]
    mat_im = matrix[:, None, 1]
    vec_re = field[:, :, 0][:, :, None]
    vec_im = field[:, :, 1][:, :, None]
    real_part = lax.optimization_barrier(jnp.sum(mat_re * vec_re - mat_im * vec_im, axis=3))
    imag_part = lax.optimization_barrier(jnp.sum(mat_re * vec_im + mat_im * vec_re, axis=3))
    return jnp.stack([real_part, imag_part], axis=2)

def adjoint(matrix):
    return jnp.stack([jnp.swapaxes(matrix[:, 0], 1, 2), -jnp.swapaxes(matrix[:, 1], 1, 2)], axis=1)

def plane_roll(array, offset, direction):
    shape = array.shape
    grid = array.reshape(shape[:-1] + (-1, LX))
    rolled = jnp.roll(grid, offset, axis=-1 if direction == 0 else -2)
    return rolled.reshape(shape)

def site_shift(array, offset, direction):
    if direction == 2:
        return jnp.roll(array, offset, axis=4)
    return plane_roll(array, offset, direction)

def hopping(links, field):
    total = jnp.zeros(field.shape, jnp.float32)
    for direction in range(3):
        matrix = links[:, direction]
        forward = mat_vec(matrix, site_shift(field, -1, direction))
        backward = site_shift(mat_vec(adjoint(matrix), field), 1, direction)
        total = total + forward
        total = total + backward
    return total

def operator(links, field):
    return 6.0 * field - hopping(links, field)

def scaled_apply(links, field):
    return (operator(links, field) - 7.0 * field) / 5.5

def gram_pair(left, right):
    count_t, count_n = (left.shape[0], left.shape[1])
    left_flat = left.reshape(count_t, count_n, 2, -1)
    right_flat = right.reshape(count_t, count_n, 2, -1)

    def inner(first, second):
        return jnp.einsum('tik,tjk->tij', first, second, precision=lax.Precision.HIGHEST)
    real_part = inner(left_flat[:, :, 0], right_flat[:, :, 0]) + inner(left_flat[:, :, 1], right_flat[:, :, 1])
    imag_part = inner(left_flat[:, :, 0], right_flat[:, :, 1]) - inner(left_flat[:, :, 1], right_flat[:, :, 0])
    return (real_part, imag_part)

def reference(links, vectors):
    previous = vectors
    current = scaled_apply(links, vectors)

    def advance(turn, carry):
        older, newer = carry
        return (newer, 2.0 * scaled_apply(links, newer) - older)
    previous, current = lax.fori_loop(0, DEG - 1, advance, (previous, current))
    sumsq = lax.optimization_barrier(jnp.sum(current * current, axis=(2, 3, 4, 5)))
    inverse = lax.rsqrt(sumsq)
    filtered = current * inverse[:, :, None, None, None, None]
    image = operator(links, filtered)
    over_re, over_im = gram_pair(filtered, filtered)
    lap_re, lap_im = gram_pair(filtered, image)
    grams = jnp.stack([jnp.stack([over_re, over_im], axis=1), jnp.stack([lap_re, lap_im], axis=1)], axis=1)
    return (filtered, grams)
```

```python
import functools

import jax
import jax.numpy as jnp
from jax import lax
from jax.experimental import pallas as pl
from jax.experimental.pallas import tpu as pltpu
from jax.sharding import PartitionSpec as P

LX = 32
LANES = 128
SHIFT = 7.0
SCALE = 5.5
F32 = jnp.float32
BF16 = jnp.bfloat16
VMEM = pl.BlockSpec(memory_space=pltpu.VMEM)
SMEM = pl.BlockSpec(memory_space=pltpu.SMEM)


def shape_of(*dims, dtype=F32):
    return jax.ShapeDtypeStruct(dims, dtype)


def call(kernel, outs, *args, smem=0, ops=1e6, scratch=()):
    size = sum(a.size * 4 for a in args) + sum(4 * o.size for o in jax.tree.leaves(outs))
    return pl.pallas_call(
        kernel,
        out_shape=outs,
        in_specs=[SMEM] * smem + [VMEM] * (len(args) - smem),
        out_specs=jax.tree.map(lambda _: VMEM, outs),
        scratch_shapes=scratch,
        cost_estimate=pl.CostEstimate(flops=int(ops), bytes_accessed=int(size), transcendentals=0),
    )(*args)


def to_rows(x):
    depth, plane = x.shape[-2:]
    x = x.reshape(-1, depth, plane // LANES, LANES)
    return jnp.swapaxes(x, 1, 2).reshape(-1, LANES)


def from_rows(x, shape):
    depth, plane = shape[-2:]
    x = x.reshape(-1, plane // LANES, depth, LANES)
    return jnp.swapaxes(x, 1, 2).reshape(shape)


def pieces_of(depth):
    if depth == 1:
        return [[0]]
    if depth == 2:
        return [[0], [1]]
    return [[0], list(range(1, depth - 1)), [depth - 1]]


def plane_refs(refs, pieces):
    return {z: ref.at[k] for ref, planes in zip(refs, pieces) for k, z in enumerate(planes)}


def lane_index(shape):
    return lax.broadcasted_iota(jnp.int32, shape, len(shape) - 1)


def ahead_x(v, lane):
    wrap = (lane % LX) == LX - 1
    return jnp.where(wrap, pltpu.roll(v, LX - 1, v.ndim - 1), pltpu.roll(v, LANES - 1, v.ndim - 1))


def behind_x(v, lane):
    wrap = (lane % LX) == 0
    return jnp.where(wrap, pltpu.roll(v, LANES - LX + 1, v.ndim - 1), pltpu.roll(v, 1, v.ndim - 1))


def ahead_y(here, after, lane):
    ax = here.ndim - 1
    return jnp.where(lane < LANES - LX, pltpu.roll(here, LANES - LX, ax), pltpu.roll(after, LANES - LX, ax))


def behind_y(here, before, lane):
    ax = here.ndim - 1
    return jnp.where(lane < LX, pltpu.roll(before, LX, ax), pltpu.roll(here, LX, ax))


def split_kernel(depth, rows, vecs, pieces, which_ref, v_ref, *out_refs):
    out = plane_refs(out_refs, pieces)
    stride = 6 * rows * depth
    base = which_ref[0] * (vecs * stride)
    for z in range(depth):

        def body(c, _, z=z):
            for q in range(6):
                start = base + q * rows * depth + c * depth + z
                out[z][c, q] = v_ref[pl.ds(start, vecs, stride=stride), :]
            return 0

        lax.fori_loop(0, rows, body, 0)


def link_kernel(depth, half, core_ref, kept_ref, came_ref, out_ref, top_ref):
    rows = 2 * half
    core = core_ref[0]
    for ref, first in ((kept_ref, core * half), (came_ref, (1 - core) * half)):
        for z in range(depth):

            def body(c, _, z=z, ref=ref, first=first):
                out_ref[z, first + c, 0:54, :] = ref[pl.ds(c * depth + z, 54, stride=half * depth), :]
                return 0

            lax.fori_loop(0, half, body, 0)
    lane = lane_index((18, LANES))
    for z in range(depth):

        def shift(c, _, z=z):
            before = lax.rem(c + rows - 1, rows)
            out_ref[z, c, 54:72, :] = behind_x(out_ref[z, c, 0:18, :], lane)
            out_ref[z, c, 72:90, :] = behind_y(out_ref[z, c, 18:36, :], out_ref[z, before, 18:36, :], lane)
            return 0

        lax.fori_loop(0, rows, shift, 0)
    top_ref[:, 0:18, :] = out_ref[depth - 1, :, 36:54, :]


def multiply_into(total, field, link, adjoint):
    for col in range(3):
        re, im = field(col), field(3 + col)
        for row in range(3):
            entry = col * 3 + row if adjoint else row * 3 + col
            a, b = link(entry), link(9 + entry)
            if adjoint:
                total[row] = total[row] + a * re + b * im
                total[3 + row] = total[3 + row] + a * im - b * re
            else:
                total[row] = total[row] + a * re - b * im
                total[3 + row] = total[3 + row] + a * im + b * re


def link_rows(ref, c, first, vecs):
    def link(k):
        return jnp.broadcast_to(ref[c, first + k : first + k + 1, :], (vecs, LANES))

    return link


def forward_hops(total, cur, up, links, c, rows, lane):
    vecs = lane.shape[0]
    after = lax.rem(c + 1, rows)
    multiply_into(total, lambda q: ahead_x(cur[c, q], lane), link_rows(links, c, 0, vecs), False)
    multiply_into(total, lambda q: ahead_y(cur[c, q], cur[after, q], lane), link_rows(links, c, 18, vecs), False)
    multiply_into(total, lambda q: up[c, q], link_rows(links, c, 36, vecs), False)


def backward_hops(total, cur, down, links, down_links, first, c, rows, lane):
    vecs = lane.shape[0]
    before = lax.rem(c + rows - 1, rows)
    multiply_into(total, lambda q: behind_x(cur[c, q], lane), link_rows(links, c, 54, vecs), True)
    multiply_into(total, lambda q: behind_y(cur[c, q], cur[before, q], lane), link_rows(links, c, 72, vecs), True)
    multiply_into(total, lambda q: down[c, q], link_rows(down_links, c, first, vecs), True)


def step_kernel(depth, pieces, todo, halos, first, *refs):
    refs = list(refs)
    links_ref = refs.pop(0)
    cur = plane_refs([refs.pop(0) for _ in pieces], pieces)
    prior_ref = None
    if halos:
        prior_ref = refs.pop(0)
        cur[-1], cur[depth] = refs.pop(0).at[0], refs.pop(0).at[0]
    done = [pieces[k] for k in todo]
    old = None if first else plane_refs([refs.pop(0) for _ in todo], done)
    out = plane_refs(refs, done)
    rows, _, vecs, _ = out[done[0][0]].shape
    lane = lane_index((vecs, LANES))
    factor = -1.0 / SCALE if first else -2.0 / SCALE
    for z in out:
        links = links_ref.at[z]
        down_links, start = (prior_ref, 0) if z == 0 else (links_ref.at[z - 1], 36)

        def body(c, _, z=z, links=links, down_links=down_links, start=start):
            total = [cur[z][c, q] for q in range(6)]
            forward_hops(total, cur[z], cur[z + 1], links, c, rows, lane)
            backward_hops(total, cur[z], cur[z - 1], links, down_links, start, c, rows, lane)
            for q in range(6):
                value = total[q] * factor
                out[z][c, q] = value if first else value - old[z][c, q]
            return 0

        lax.fori_loop(0, rows, body, 0)


def halves(x):
    high = x.astype(BF16)
    return high, (x - high.astype(F32)).astype(BF16)


def gram_kernel(depth, pieces, planes, add, *refs):
    refs = list(refs)
    links_ref = refs.pop(0)
    cur = plane_refs([refs.pop(0) for _ in pieces], pieces)
    if add:
        cur[depth] = refs.pop(0).at[0]
        sofar_ref = refs.pop(0)
    out_ref, acc_ref = refs
    rows, _, vecs, _ = cur[0].shape
    lane = lane_index((vecs, LANES))
    acc_ref[...] = jnp.zeros_like(acc_ref)
    for z in planes:
        links = links_ref.at[z]

        def body(pair, _, z=z, links=links):
            left, right = [[], [], [], []], [[], [], [], []]
            for c in (2 * pair, 2 * pair + 1):
                total = [jnp.zeros((vecs, LANES), F32) for _ in range(6)]
                forward_hops(total, cur[z], cur[z + 1], links, c, rows, lane)
                for part in range(2):
                    for q in range(3 * part, 3 * part + 3):
                        for store, x in ((left, cur[z][c, q]), (right, total[q])):
                            high, low = halves(x)
                            store[part].append(high)
                            store[2 + part].append(low)
            left = [jnp.concatenate(x, axis=1) for x in left]
            right = [jnp.concatenate(x, axis=1) for x in right]
            a = jnp.concatenate(left, axis=0)
            b = jnp.concatenate(left + right, axis=0)
            acc_ref[...] += lax.dot_general(a, b, (((1,), (1,)), ((), ())), preferred_element_type=F32)
            return 0

        lax.fori_loop(0, rows // 2, body, 0)
    n = vecs
    acc = acc_ref[0 : 2 * n] + acc_ref[2 * n : 4 * n]
    acc = acc + pltpu.roll(acc, LANES - 2 * n, 1)
    re, im = acc[0:n], acc[n : 2 * n]
    real = re + pltpu.roll(im, LANES - n, 1)
    imag = re - pltpu.roll(im, n, 1)
    part = jnp.where((lane % (2 * n)) < n, real, imag)
    out_ref[...] = part + sofar_ref[...] if add else part


def final_kernel(depth, pieces, mine_ref, *refs):
    refs = list(refs)
    count = len(pieces)
    sets = []
    for _ in range(2):
        gram = refs.pop(0)
        sets.append((gram, plane_refs([refs.pop(0) for _ in range(count)], pieces)))
    out_ref, grams_ref = refs
    rows, _, vecs, _ = sets[0][1][0].shape
    n = vecs
    stride = 6 * rows * depth
    lane = lane_index((n, LANES))
    diag = lane == lax.broadcasted_iota(jnp.int32, (n, LANES), 0)
    for k, (gram_ref, planes) in enumerate(sets):
        slot = mine_ref[0] if k == 0 else 1 - mine_ref[0]
        packed = gram_ref[...]
        norm = jnp.where(diag, packed, 0.0)
        down = lax.rsqrt(jnp.sum(norm, axis=1, keepdims=True))
        across = lax.rsqrt(jnp.sum(norm, axis=0, keepdims=True))[:, 0:n]
        scale = down * across
        over_re, over_im = packed[:, 0:n], packed[:, n : 2 * n]
        hop_re, hop_im = packed[:, 4 * n : 5 * n], packed[:, 5 * n : 6 * n]
        lap_re = 6.0 * over_re - (hop_re + hop_re.T)
        lap_im = 6.0 * over_im - (hop_im - hop_im.T)
        grams_ref[slot, 0, 0] = over_re * scale
        grams_ref[slot, 0, 1] = over_im * scale
        grams_ref[slot, 1, 0] = lap_re * scale
        grams_ref[slot, 1, 1] = lap_im * scale
        inverse = jnp.broadcast_to(down, (n, LANES))
        base = slot * (n * stride)
        for z in range(depth):

            def body(c, _, z=z, planes=planes, base=base, inverse=inverse):
                for q in range(6):
                    start = base + q * rows * depth + c * depth + z
                    out_ref[pl.ds(start, n, stride=stride), :] = planes[z][c, q] * inverse
                return 0

            lax.fori_loop(0, rows, body, 0)


def shifted(x, axis, by):
    n = lax.axis_size(axis)
    return lax.ppermute(x, axis, [(i, (i + by) % n) for i in range(n)])


def flipped(x, axis, bit):
    return lax.ppermute(x, axis, [(i, i ^ bit) for i in range(lax.axis_size(axis))])


def all_sum(x, axis):
    bit = 1
    while bit < lax.axis_size(axis):
        x = x + flipped(x, axis, bit)
        bit *= 2
    return x


def on_device(links, vectors):
    slices, vecs, _, _, depth, plane = vectors.shape
    rows = plane // LANES
    assert slices == 2 and lax.axis_size("cfg") % 2 == 0 and lax.axis_size("ta") == 2
    pieces = pieces_of(depth)
    core = lax.axis_index("ta")
    mine = lax.axis_index("cfg") % 2
    mine_s = mine.astype(jnp.int32).reshape(1)
    core_s = core.astype(jnp.int32).reshape(1)
    field = [shape_of(len(p), rows, 6, vecs, LANES) for p in pieces]
    ops = 1000 * 128 * vecs * rows

    start = call(
        functools.partial(split_kernel, depth, rows, vecs, pieces), field, mine_s, to_rows(vectors), smem=1, ops=1e5
    )

    flat = links.reshape((links.shape[0], 54) + links.shape[-2:])
    kept = lax.dynamic_index_in_dim(flat, 2 * core + mine, 0, keepdims=False)
    given = lax.dynamic_index_in_dim(flat, 2 * (1 - core) + mine, 0, keepdims=False)
    came = flipped(given, "ta", 1)
    table, top_links = call(
        functools.partial(link_kernel, depth, rows // 2),
        [shape_of(depth, rows, 90, LANES), shape_of(rows, 18, LANES)],
        core_s, to_rows(kept), to_rows(came), smem=1, ops=1e6,
    )
    prior = shifted(top_links, "sa", 1)

    ends = [0] if len(pieces) == 1 else [0, len(pieces) - 1]
    inner = [1] if len(pieces) == 3 else []

    def advance(cur, old):
        low = shifted(cur[-1], "sa", 1)
        high = shifted(cur[0], "sa", -1)
        new = list(cur)
        for todo, extra in ((inner, []), (ends, [prior, low, high])):
            if not todo:
                continue
            outs = [field[k] for k in todo]
            olds = [] if old is None else [old[k] for k in todo]
            result = call(
                functools.partial(step_kernel, depth, pieces, todo, bool(extra), old is None),
                outs, table, *cur, *extra, *olds, ops=ops * sum(len(pieces[k]) for k in todo),
            )
            for k, x in zip(todo, result):
                new[k] = x
        return new

    one = advance(start, None)
    two = advance(one, start)
    three = advance(two, one)

    other = [flipped(x, "cfg", 1) for x in three]
    above = shifted(three[0], "sa", -1)
    packed = shape_of(vecs, LANES)
    acc = [pltpu.VMEM((4 * vecs, 8 * vecs), F32)]
    part = call(
        functools.partial(gram_kernel, depth, pieces, range(depth - 1), False),
        packed, table, *three, scratch=acc, ops=ops * depth,
    )
    part = call(
        functools.partial(gram_kernel, depth, pieces, [depth - 1], True),
        packed, table, *three, above, part, scratch=acc, ops=ops,
    )
    gram = all_sum(part, "sa")
    other_gram = flipped(gram, "cfg", 1)
    out, grams = call(
        functools.partial(final_kernel, depth, pieces),
        [shape_of(2 * vecs * 6 * rows * depth, LANES), shape_of(2, 2, 2, vecs, vecs)],
        mine_s, gram, *three, other_gram, *other, smem=1, ops=1e6,
    )
    return from_rows(out, vectors.shape), grams


def solution(mesh):
    in_specs = (P(None, None, None, None, None, "sa", "ta"), P("ta", None, None, None, "sa", None))
    out_specs = (
        P(("cfg", "ta"), None, None, None, "sa", None),
        P(("cfg", "ta"), None, None, None, None),
    )
    return jax.shard_map(
        on_device, mesh=mesh, in_specs=in_specs, out_specs=out_specs, check_vma=False
    )
```

```python
import functools

import jax
import jax.numpy as jnp
from jax import lax
from jax.experimental import pallas as pl
from jax.experimental.pallas import tpu as pltpu
from jax.sharding import PartitionSpec as P

LX = 32
LANES = 128
SHIFT = 7.0
SCALE = 5.5
F32 = jnp.float32
BF16 = jnp.bfloat16
VMEM = pl.BlockSpec(memory_space=pltpu.VMEM)
GRANT = 16 * 2**20


def shape_of(*dims, dtype=F32):
    return jax.ShapeDtypeStruct(dims, dtype)


def call(kernel, outs, *args, ops=1e6, scratch=(), pick=None, whole=None, grid=1):
    size = sum(a.size * 4 for a in args) + sum(4 * o.size for o in jax.tree.leaves(outs))
    several = isinstance(outs, (list, tuple))
    params = dict(
        out_shape=outs,
        compiler_params=pltpu.CompilerParams(vmem_limit_bytes=GRANT),
        cost_estimate=pl.CostEstimate(flops=int(ops), bytes_accessed=int(size), transcendentals=0),
    )
    if pick is None:
        specs = [VMEM] * len(outs) if several else VMEM
        return pl.pallas_call(
            kernel, in_specs=[VMEM] * len(args), out_specs=specs, scratch_shapes=scratch, **params
        )(*args)
    specs = [pl.BlockSpec(*whole[k]) if k in whole else VMEM for k in range(len(args) + len(outs))]
    spec = pltpu.PrefetchScalarGridSpec(
        num_scalar_prefetch=1, grid=(grid,), in_specs=specs[: len(args)], out_specs=specs[len(args) :]
    )
    return pl.pallas_call(kernel, grid_spec=spec, **params)(pick, *args)


def to_rows(x):
    depth, plane = x.shape[-2:]
    x = x.reshape(-1, depth, plane // LANES, LANES)
    return jnp.swapaxes(x, 1, 2).reshape(-1, LANES)


def from_rows(x, shape):
    depth, plane = shape[-2:]
    x = x.reshape(-1, plane // LANES, depth, LANES)
    return jnp.swapaxes(x, 1, 2).reshape(shape)


def pieces_of(depth):
    if depth == 1:
        return [[0]]
    if depth == 2:
        return [[0], [1]]
    return [[0], list(range(1, depth - 1)), [depth - 1]]


def plane_refs(refs, pieces):
    return {z: ref.at[k] for ref, planes in zip(refs, pieces) for k, z in enumerate(planes)}


def lane_index(shape):
    return lax.broadcasted_iota(jnp.int32, shape, len(shape) - 1)


def ahead_x(v, lane):
    wrap = (lane % LX) == LX - 1
    return jnp.where(wrap, pltpu.roll(v, LX - 1, v.ndim - 1), pltpu.roll(v, LANES - 1, v.ndim - 1))


def behind_x(v, lane):
    wrap = (lane % LX) == 0
    return jnp.where(wrap, pltpu.roll(v, LANES - LX + 1, v.ndim - 1), pltpu.roll(v, 1, v.ndim - 1))


def ahead_y(here, after, lane):
    ax = here.ndim - 1
    return jnp.where(lane < LANES - LX, pltpu.roll(here, LANES - LX, ax), pltpu.roll(after, LANES - LX, ax))


def behind_y(here, before, lane):
    ax = here.ndim - 1
    return jnp.where(lane < LX, pltpu.roll(before, LX, ax), pltpu.roll(here, LX, ax))


def split_kernel(depth, rows, vecs, pieces, _, v_ref, *out_refs):
    out = plane_refs(out_refs, pieces)
    stride = 6 * rows * depth

    def body(c, _):
        for z in out:
            for q in range(6):
                out[z][c, q] = v_ref[pl.ds(q * rows * depth + c * depth + z, vecs, stride=stride), :]
        return 0

    lax.fori_loop(0, rows, body, 0)


def link_kernel(depth, half, pick_ref, kept_ref, came_ref, out_ref, top_ref):
    rows = 2 * half
    core = pick_ref[1]

    def body(c, _):
        for ref, first in ((kept_ref, core * half), (came_ref, (1 - core) * half)):
            for z in range(depth):
                out_ref[z, first + c, 0:54, :] = ref[pl.ds(c * depth + z, 54, stride=half * depth), :]
        return 0

    lax.fori_loop(0, half, body, 0)
    lane = lane_index((18, LANES))

    def shift(c, _):
        before = lax.rem(c + rows - 1, rows)
        for z in range(depth):
            out_ref[z, c, 54:72, :] = behind_x(out_ref[z, c, 0:18, :], lane)
            out_ref[z, c, 72:90, :] = behind_y(out_ref[z, c, 18:36, :], out_ref[z, before, 18:36, :], lane)
        top_ref[c, 0:18, :] = out_ref[depth - 1, c, 36:54, :]
        return 0

    lax.fori_loop(0, rows, shift, 0)


def multiply_into(total, field, link, adjoint):
    for col in range(3):
        re, im = field(col), field(3 + col)
        for row in range(3):
            entry = col * 3 + row if adjoint else row * 3 + col
            a, b = link(entry), link(9 + entry)
            if adjoint:
                total[row] = total[row] + a * re + b * im
                total[3 + row] = total[3 + row] + a * im - b * re
            else:
                total[row] = total[row] + a * re - b * im
                total[3 + row] = total[3 + row] + a * im + b * re


def link_rows(ref, c, first, vecs):
    def link(k):
        return jnp.broadcast_to(ref[c, first + k : first + k + 1, :], (vecs, LANES))

    return link


def forward_hops(total, cur, up, links, c, rows, lane):
    vecs = lane.shape[0]
    after = lax.rem(c + 1, rows)
    multiply_into(total, lambda q: ahead_x(cur[c, q], lane), link_rows(links, c, 0, vecs), False)
    multiply_into(total, lambda q: ahead_y(cur[c, q], cur[after, q], lane), link_rows(links, c, 18, vecs), False)
    if up is not None:
        multiply_into(total, lambda q: up[c, q], link_rows(links, c, 36, vecs), False)


def backward_hops(total, cur, down, links, down_links, c, rows, lane):
    vecs = lane.shape[0]
    before = lax.rem(c + rows - 1, rows)
    multiply_into(total, lambda q: behind_x(cur[c, q], lane), link_rows(links, c, 54, vecs), True)
    multiply_into(total, lambda q: behind_y(cur[c, q], cur[before, q], lane), link_rows(links, c, 72, vecs), True)
    if down is not None:
        multiply_into(total, lambda q: down[c, q], link_rows(down_links, c, 36, vecs), True)


def part_kernel(depth, pieces, factor, first, links_ref, *refs):
    count = len(pieces)
    cur = plane_refs(refs[:count], pieces)
    old = None if first else plane_refs(refs[count : 2 * count], pieces)
    out = plane_refs(refs[-count:], pieces)
    rows, _, vecs, _ = out[0].shape
    lane = lane_index((vecs, LANES))
    for z in range(depth):

        def body(c, _, z=z):
            total = [cur[z][c, q] for q in range(6)]
            links = links_ref.at[z]
            forward_hops(total, cur[z], cur.get(z + 1), links, c, rows, lane)
            below = links_ref.at[z - 1] if z else None
            backward_hops(total, cur[z], cur.get(z - 1), links, below, c, rows, lane)
            for q in range(6):
                value = total[q] * factor
                out[z][c, q] = value if first else value - old[z][c, q]
            return 0

        lax.fori_loop(0, rows, body, 0)


def close_kernel(factor, top_ref, prior_ref, low_ref, high_ref, *refs):
    half = len(refs) // 2
    parts = [r.at[0] for r in refs[:half]]
    outs = [r.at[0] for r in refs[half:]]
    rows, _, vecs, _ = outs[0].shape

    def body(c, _):
        for k in range(half):
            total = [jnp.zeros((vecs, LANES), F32) for _ in range(6)]
            if k == 0:
                multiply_into(total, lambda q: low_ref[0, c, q], link_rows(prior_ref, c, 0, vecs), True)
            if k == half - 1:
                multiply_into(total, lambda q: high_ref[0, c, q], link_rows(top_ref, c, 0, vecs), False)
            for q in range(6):
                outs[k][c, q] = parts[k][c, q] + total[q] * factor
        return 0

    lax.fori_loop(0, rows, body, 0)


def halves(x):
    high = x.astype(BF16)
    return high, (x - high.astype(F32)).astype(BF16)


def high_low(tiles):
    pairs = [halves(jnp.concatenate(tiles[k : k + 3], axis=1)) for k in (0, 3)]
    return [pairs[0][0], pairs[1][0], pairs[0][1], pairs[1][1]]


def products(acc_ref, rows, sides):
    def body(pair, _):
        stacks = [[], []]
        for c in (2 * pair, 2 * pair + 1):
            for stack, tiles in zip(stacks, sides(c)):
                stack.append(jnp.concatenate(high_low(tiles), axis=0))
        left, right = [jnp.concatenate(s, axis=1) for s in stacks]
        right = jnp.concatenate([right, right], axis=0)
        acc_ref[...] += lax.dot_general(left, right, (((1,), (1,)), ((), ())), preferred_element_type=F32)
        return 0

    lax.fori_loop(0, rows // 2, body, 0)


def packed_product(acc, n):
    acc = acc[0 : 2 * n] + acc[2 * n : 4 * n]
    acc = acc + pltpu.roll(acc, LANES - 2 * n, 1)
    re, im = acc[0:n], acc[n : 2 * n]
    real = re + pltpu.roll(im, LANES - n, 1)
    imag = re - pltpu.roll(im, n, 1)
    return jnp.where(lane_index((n, LANES)) < n, real, imag)


def over_kernel(pieces, *refs):
    refs = list(refs)
    acc_ref, out_ref = refs.pop(), refs.pop()
    cur = plane_refs(refs, pieces)
    rows, _, vecs, _ = cur[0].shape
    acc_ref[...] = jnp.zeros_like(acc_ref)
    for z in cur:

        def sides(c, z=z):
            tiles = [cur[z][c, q] for q in range(6)]
            return tiles, tiles

        products(acc_ref, rows, sides)
    out_ref[...] = packed_product(acc_ref[...], vecs)


def hop_kernel(depth, pieces, links_ref, *refs):
    refs = list(refs)
    acc_ref, out_ref = refs.pop(), refs.pop()
    cur = plane_refs(refs, pieces)
    rows, _, vecs, _ = cur[0].shape
    lane = lane_index((vecs, LANES))
    acc_ref[...] = jnp.zeros_like(acc_ref)
    for z in range(depth):

        def sides(c, z=z):
            total = [jnp.zeros((vecs, LANES), F32) for _ in range(6)]
            forward_hops(total, cur[z], cur.get(z + 1), links_ref.at[z], c, rows, lane)
            return [cur[z][c, q] for q in range(6)], total

        products(acc_ref, rows, sides)
    out_ref[...] = packed_product(acc_ref[...], vecs)


def last_hop_kernel(links_ref, top_ref, above_ref, sofar_ref, out_ref, acc_ref):
    rows, _, vecs, _ = top_ref.shape[1:]
    acc_ref[...] = jnp.zeros_like(acc_ref)

    def sides(c):
        total = [jnp.zeros((vecs, LANES), F32) for _ in range(6)]
        multiply_into(total, lambda q: above_ref[0, c, q], link_rows(links_ref, c, 0, vecs), False)
        return [top_ref[0, c, q] for q in range(6)], total

    products(acc_ref, rows, sides)
    out_ref[...] = packed_product(acc_ref[...], vecs) + sofar_ref[...]


def norms_of(packed):
    n = packed.shape[0]
    diag = lane_index((n, LANES)) == lax.broadcasted_iota(jnp.int32, (n, LANES), 0)
    return jnp.where(diag, packed, 0.0)


def filtered_kernel(depth, pieces, _, *refs):
    refs = list(refs)
    out_ref = refs.pop()
    count = len(pieces)
    sets = []
    for _ in range(2):
        terms = (refs.pop(0), refs.pop(0))
        sets.append((terms, plane_refs([refs.pop(0) for _ in range(count)], pieces)))
    rows, _, vecs, _ = sets[0][1][0].shape
    stride = 6 * rows * depth
    for k, (terms, planes) in enumerate(sets):

        @pl.when(pl.program_id(0) == k)
        def _(terms=terms, planes=planes):
            norm = norms_of(terms[0][...] + terms[1][...])
            inverse = jnp.broadcast_to(lax.rsqrt(jnp.sum(norm, axis=1, keepdims=True)), (vecs, LANES))

            def body(c, _):
                for z in range(depth):
                    for q in range(6):
                        start = q * rows * depth + c * depth + z
                        out_ref[pl.ds(start, vecs, stride=stride), :] = planes[z][c, q] * inverse
                return 0

            lax.fori_loop(0, rows, body, 0)


def grams_kernel(slot_ref, *refs):
    out_ref = refs[-1]
    for k in range(2):
        slot = slot_ref[0] if k == 0 else 1 - slot_ref[0]
        over0, over1, hop0, hop1 = refs[4 * k : 4 * k + 4]
        over, hop = over0[...] + over1[...], hop0[...] + hop1[...]
        n = over.shape[0]
        norm = norms_of(over)
        down = lax.rsqrt(jnp.sum(norm, axis=1, keepdims=True))
        across = lax.rsqrt(jnp.sum(norm, axis=0, keepdims=True)[:, 0:n])
        scale = down * across
        over_re, over_im, hop_re, hop_im = over[:, 0:n], over[:, n : 2 * n], hop[:, 0:n], hop[:, n : 2 * n]
        out_ref[slot, 0, 0] = over_re * scale
        out_ref[slot, 0, 1] = over_im * scale
        out_ref[slot, 1, 0] = (6.0 * over_re - (hop_re + hop_re.T)) * scale
        out_ref[slot, 1, 1] = (6.0 * over_im - (hop_im - hop_im.T)) * scale


def shifted(x, axis, by):
    n = lax.axis_size(axis)
    return lax.ppermute(x, axis, [(i, (i + by) % n) for i in range(n)])


def flipped(x, axis, bit):
    return lax.ppermute(x, axis, [(i, i ^ bit) for i in range(lax.axis_size(axis))])


def summed(x):
    size = lax.axis_size("sa")
    count = size.bit_length() - 1
    assert size == 1 << count

    def across(x, cfg, bits):
        pairs = range(lax.axis_size("cfg") * size)
        return lax.ppermute(x, ("cfg", "sa"), [(i, i ^ (cfg * size + bits)) for i in pairs])

    bit = 1
    for _ in range((count - 1) // 2):
        x = x + flipped(x, "sa", bit) + flipped(x, "sa", 2 * bit) + flipped(x, "sa", 3 * bit)
        bit *= 4
    if count % 2 == 0:
        x = x + flipped(x, "sa", bit)
        bit *= 2
    return (x, flipped(x, "sa", bit)), (across(x, 1, 0), across(x, 1, bit))


def on_device(links, vectors):
    slices, vecs, _, _, depth, plane = vectors.shape
    rows = plane // LANES
    assert slices == 2 and lax.axis_size("cfg") % 2 == 0 and lax.axis_size("ta") == 2
    pieces = pieces_of(depth)
    ends = [0] if len(pieces) == 1 else [0, len(pieces) - 1]
    core = lax.axis_index("ta")
    mine = lax.axis_index("cfg") % 2
    pick = jnp.stack([mine, core, 2 * core + mine]).astype(jnp.int32)
    field = [shape_of(len(p), rows, 6, vecs, LANES) for p in pieces]
    work = 1000 * LANES * vecs * rows
    many = vecs * 6 * rows * depth
    mine_block = ((many, LANES), lambda step, pick: (pick[0], 0))

    view = to_rows(vectors)

    def split(todo):
        return call(
            functools.partial(split_kernel, depth, rows, vecs, [pieces[k] for k in todo]),
            [field[k] for k in todo], view, pick=pick, whole={0: mine_block}, ops=1e5,
        )

    start = [None] * len(pieces)
    for k, x in zip(ends, split(ends)):
        start[k] = x
    links, view, *late = lax.optimization_barrier((links, view, *[start[k] for k in ends]))

    flat = links.reshape((links.shape[0], 54) + links.shape[-2:])
    given = lax.dynamic_index_in_dim(flat, 2 * (1 - core) + mine, 0, keepdims=False)
    came = flipped(given, "ta", 1)
    inner = [k for k in range(len(pieces)) if k not in ends]
    if inner:
        for k, x in zip(inner, split(inner)):
            start[k] = x
    block = ((54 * (rows // 2) * depth, LANES), lambda step, pick: (pick[2], 0))
    table, top_links = call(
        functools.partial(link_kernel, depth, rows // 2),
        [shape_of(depth, rows, 90, LANES), shape_of(rows, 18, LANES)],
        to_rows(links), to_rows(came), pick=pick, whole={0: block}, ops=1e6,
    )
    prior = shifted(top_links, "sa", 1)

    def advance(cur, old):
        low = shifted(cur[-1], "sa", 1)
        high = shifted(cur[0], "sa", -1)
        factor = -(1.0 if old is None else 2.0) / SCALE
        new = list(call(
            functools.partial(part_kernel, depth, pieces, factor, old is None),
            field, table, *cur, *(old or []), ops=work * depth,
        ))
        closed = call(
            functools.partial(close_kernel, factor), [field[k] for k in ends],
            top_links, prior, low, high, *[new[k] for k in ends], ops=work / 3,
        )
        for k, x in zip(ends, closed):
            new[k] = x
        return new

    one = advance(start, None)
    two = advance(one, start)
    three = advance(two, one)

    above = shifted(three[0], "sa", -1)
    other = [flipped(x, "cfg", 1) for x in three]
    packed = shape_of(vecs, LANES)
    acc = [pltpu.VMEM((4 * vecs, 8 * vecs), F32)]
    over = call(functools.partial(over_kernel, pieces), packed, *three, scratch=acc, ops=work * depth / 4)
    over_mine, over_other = summed(over)
    hop = call(
        functools.partial(hop_kernel, depth, pieces), packed, table, *three, scratch=acc, ops=work * depth / 2
    )
    hop = call(last_hop_kernel, packed, top_links, three[-1], above, hop, scratch=acc, ops=work / 4)
    hop_mine, hop_other = summed(hop)
    place = ((many, LANES), lambda step, pick: (jnp.where(step == 0, pick[0], 1 - pick[0]), 0))
    given = [*over_mine, *three, *over_other, *other]
    (out,) = call(
        functools.partial(filtered_kernel, depth, pieces), [shape_of(2 * many, LANES)],
        *given, pick=pick, whole={len(given): place}, grid=2, ops=1e6,
    )
    (grams,) = call(
        grams_kernel, [shape_of(2, 2, 2, vecs, vecs)],
        *over_mine, *hop_mine, *over_other, *hop_other, pick=pick, whole={}, ops=1e4,
    )
    return from_rows(out, vectors.shape), grams


def solution(mesh):
    in_specs = (P(None, None, None, None, None, "sa", "ta"), P("ta", None, None, None, "sa", None))
    out_specs = (
        P(("cfg", "ta"), None, None, None, "sa", None),
        P(("cfg", "ta"), None, None, None, None),
    )
    return jax.shard_map(
        on_device, mesh=mesh, in_specs=in_specs, out_specs=out_specs, check_vma=False
    )
```

```python
import functools

import jax
import jax.numpy as jnp
from jax import lax
from jax.experimental import pallas as pl
from jax.experimental.pallas import tpu as pltpu
from jax.sharding import PartitionSpec as P

LX = 32
LANES = 128
SHIFT = 7.0
SCALE = 5.5
F32 = jnp.float32
BF16 = jnp.bfloat16
VMEM = pl.BlockSpec(memory_space=pltpu.VMEM)
GRANT = 16 * 2**20
CHUNKS = 2


def shape_of(*dims, dtype=F32):
    return jax.ShapeDtypeStruct(dims, dtype)


def call(kernel, outs, *args, ops=1e6, scratch=(), pick=None, whole=None, grid=1):
    size = sum(a.size * 4 for a in args) + sum(4 * o.size for o in jax.tree.leaves(outs))
    several = isinstance(outs, (list, tuple))
    params = dict(
        out_shape=outs,
        compiler_params=pltpu.CompilerParams(vmem_limit_bytes=GRANT),
        cost_estimate=pl.CostEstimate(flops=int(ops), bytes_accessed=int(size), transcendentals=0),
    )
    if pick is None:
        specs = [VMEM] * len(outs) if several else VMEM
        return pl.pallas_call(
            kernel, in_specs=[VMEM] * len(args), out_specs=specs, scratch_shapes=scratch, **params
        )(*args)
    specs = [pl.BlockSpec(*whole[k]) if k in whole else VMEM for k in range(len(args) + len(outs))]
    spec = pltpu.PrefetchScalarGridSpec(
        num_scalar_prefetch=1, grid=(grid,), in_specs=specs[: len(args)], out_specs=specs[len(args) :],
        scratch_shapes=scratch,
    )
    return pl.pallas_call(kernel, grid_spec=spec, **params)(pick, *args)


def to_rows(x):
    depth, plane = x.shape[-2:]
    x = x.reshape(-1, depth, plane // LANES, LANES)
    return jnp.swapaxes(x, 1, 2).reshape(-1, LANES)


def from_rows(x, shape):
    depth, plane = shape[-2:]
    x = x.reshape(-1, plane // LANES, depth, LANES)
    return jnp.swapaxes(x, 1, 2).reshape(shape)


def pieces_of(depth):
    if depth == 1:
        return [[0]]
    if depth == 2:
        return [[0], [1]]
    return [[0], list(range(1, depth - 1)), [depth - 1]]


def plane_refs(refs, pieces):
    return {z: ref.at[k] for ref, planes in zip(refs, pieces) for k, z in enumerate(planes)}


def lane_index(shape):
    return lax.broadcasted_iota(jnp.int32, shape, len(shape) - 1)


def ahead_x(v, lane):
    wrap = (lane % LX) == LX - 1
    return jnp.where(wrap, pltpu.roll(v, LX - 1, v.ndim - 1), pltpu.roll(v, LANES - 1, v.ndim - 1))


def behind_x(v, lane):
    wrap = (lane % LX) == 0
    return jnp.where(wrap, pltpu.roll(v, LANES - LX + 1, v.ndim - 1), pltpu.roll(v, 1, v.ndim - 1))


def ahead_y(here, after, lane):
    ax = here.ndim - 1
    return jnp.where(lane < LANES - LX, pltpu.roll(here, LANES - LX, ax), pltpu.roll(after, LANES - LX, ax))


def behind_y(here, before, lane):
    ax = here.ndim - 1
    return jnp.where(lane < LX, pltpu.roll(before, LX, ax), pltpu.roll(here, LX, ax))


def split_kernel(depth, rows, vecs, pieces, chunks, _, v_ref, *out_refs):
    out = plane_refs(out_refs[: len(pieces)], pieces)
    cut = out_refs[len(pieces) :]
    stride = 6 * rows * depth
    size = rows // max(chunks, 1)

    def body(c, _, base):
        row = base + c
        for k, z in enumerate(out):
            for q in range(6):
                tile = v_ref[pl.ds(q * rows * depth + row * depth + z, vecs, stride=stride), :]
                out[z][row, q] = tile
                if chunks:
                    cut[k * chunks + base // size][c, q] = tile
        return 0

    for base in range(0, rows, size):
        lax.fori_loop(0, size, functools.partial(body, base=base), 0)


def link_kernel(depth, half, pick_ref, kept_ref, came_ref, out_ref, top_ref):
    rows = 2 * half
    core = pick_ref[1]

    def body(c, _):
        for ref, first in ((kept_ref, core * half), (came_ref, (1 - core) * half)):
            for z in range(depth):
                out_ref[z, first + c, 0:54, :] = ref[pl.ds(c * depth + z, 54, stride=half * depth), :]
        return 0

    lax.fori_loop(0, half, body, 0)
    lane = lane_index((18, LANES))

    def shift(c, _):
        before = lax.rem(c + rows - 1, rows)
        for z in range(depth):
            out_ref[z, c, 54:72, :] = behind_x(out_ref[z, c, 0:18, :], lane)
            out_ref[z, c, 72:90, :] = behind_y(out_ref[z, c, 18:36, :], out_ref[z, before, 18:36, :], lane)
        top_ref[c, 0:18, :] = out_ref[depth - 1, c, 36:54, :]
        return 0

    lax.fori_loop(0, rows, shift, 0)


def multiply_into(total, field, link, adjoint):
    for col in range(3):
        re, im = field(col), field(3 + col)
        for row in range(3):
            entry = col * 3 + row if adjoint else row * 3 + col
            a, b = link(entry), link(9 + entry)
            if adjoint:
                total[row] = total[row] + a * re + b * im
                total[3 + row] = total[3 + row] + a * im - b * re
            else:
                total[row] = total[row] + a * re - b * im
                total[3 + row] = total[3 + row] + a * im + b * re


def link_rows(ref, c, first, vecs):
    def link(k):
        return jnp.broadcast_to(ref[c, first + k : first + k + 1, :], (vecs, LANES))

    return link


def forward_hops(total, cur, up, links, c, rows, lane):
    vecs = lane.shape[0]
    after = lax.rem(c + 1, rows)
    multiply_into(total, lambda q: ahead_x(cur[c, q], lane), link_rows(links, c, 0, vecs), False)
    multiply_into(total, lambda q: ahead_y(cur[c, q], cur[after, q], lane), link_rows(links, c, 18, vecs), False)
    if up is not None:
        multiply_into(total, lambda q: up[c, q], link_rows(links, c, 36, vecs), False)


def backward_hops(total, cur, down, links, down_links, c, rows, lane):
    vecs = lane.shape[0]
    before = lax.rem(c + rows - 1, rows)
    multiply_into(total, lambda q: behind_x(cur[c, q], lane), link_rows(links, c, 54, vecs), True)
    multiply_into(total, lambda q: behind_y(cur[c, q], cur[before, q], lane), link_rows(links, c, 72, vecs), True)
    if down is not None:
        multiply_into(total, lambda q: down[c, q], link_rows(down_links, c, 36, vecs), True)


def part_kernel(depth, pieces, factor, first, links_ref, *refs):
    count = len(pieces)
    cur = plane_refs(refs[:count], pieces)
    old = None if first else plane_refs(refs[count : 2 * count], pieces)
    out = plane_refs(refs[-count:], pieces)
    rows, _, vecs, _ = out[0].shape
    lane = lane_index((vecs, LANES))
    for z in range(depth):

        def body(c, _, z=z):
            total = [cur[z][c, q] for q in range(6)]
            links = links_ref.at[z]
            forward_hops(total, cur[z], cur.get(z + 1), links, c, rows, lane)
            below = links_ref.at[z - 1] if z else None
            backward_hops(total, cur[z], cur.get(z - 1), links, below, c, rows, lane)
            for q in range(6):
                value = total[q] * factor
                out[z][c, q] = value if first else value - old[z][c, q]
            return 0

        lax.fori_loop(0, rows, body, 0)


def close_kernel(factor, chunk, ends, top_ref, prior_ref, low_ref, high_ref, *refs):
    refs = list(refs)
    parts = [refs.pop(0).at[0] for _ in range(ends)]
    size, _, vecs, _ = low_ref.shape
    rows = parts[0].shape[0]
    first = chunk * size
    last = first + size == rows
    outs = [refs.pop(-1) for _ in range(ends)][::-1]
    whole = [refs.pop(-1).at[0] for _ in range(ends)][::-1] if last else []

    def body(c, _):
        row = first + c
        for k in range(ends):
            total = [jnp.zeros((vecs, LANES), F32) for _ in range(6)]
            if k == 0:
                multiply_into(total, lambda q: low_ref[c, q], link_rows(prior_ref, row, 0, vecs), True)
            if k == ends - 1:
                multiply_into(total, lambda q: high_ref[c, q], link_rows(top_ref, row, 0, vecs), False)
            for q in range(6):
                value = parts[k][row, q] + total[q] * factor
                outs[k][c, q] = value
                if last:
                    whole[k][row, q] = value
        return 0

    lax.fori_loop(0, size, body, 0)
    if last:
        for k in range(ends):
            for j in range(chunk):
                whole[k][j * size : (j + 1) * size] = refs[k * chunk + j][...]


def halves(x):
    high = x.astype(BF16)
    return high, (x - high.astype(F32)).astype(BF16)


def high_low(tiles):
    pairs = [halves(jnp.concatenate(tiles[k : k + 3], axis=1)) for k in (0, 3)]
    return [pairs[0][0], pairs[1][0], pairs[0][1], pairs[1][1]]


def products(acc_ref, rows, own, sides):
    def body(pair, _):
        stacks = [[], []]
        for c in (2 * pair, 2 * pair + 1):
            for stack, tiles in zip(stacks, sides(c)):
                stack.append(jnp.concatenate(high_low(tiles), axis=0))
        left, right = [jnp.concatenate(s, axis=1) for s in stacks]
        right = jnp.concatenate([left if own else jnp.zeros_like(left), right], axis=0)
        acc_ref[...] += lax.dot_general(left, right, (((1,), (1,)), ((), ())), preferred_element_type=F32)
        return 0

    lax.fori_loop(0, rows // 2, body, 0)


def packed_product(acc, n):
    acc = acc[0 : 2 * n] + acc[2 * n : 4 * n]
    acc = acc + pltpu.roll(acc, LANES - 2 * n, 1)
    re, im = acc[0:n], acc[n : 2 * n]
    real = re + pltpu.roll(im, LANES - n, 1)
    imag = re - pltpu.roll(im, n, 1)
    return jnp.where(lane_index((n, LANES)) % (2 * n) < n, real, imag)


def gram_kernel(pieces, tasks, more, links_ref, *refs):
    refs = list(refs)
    acc_ref, out_ref = refs.pop(), refs.pop()
    sofar_ref = refs.pop() if more else None
    cur = plane_refs(refs, pieces)
    rows, _, vecs, _ = out_shape_of(cur)
    lane = lane_index((vecs, LANES))
    acc_ref[...] = jnp.zeros_like(acc_ref)
    for z, own, depth_hop in tasks:

        def sides(c, z=z, own=own, depth_hop=depth_hop):
            total = [jnp.zeros((vecs, LANES), F32) for _ in range(6)]
            links = links_ref.at[z]
            if own:
                forward_hops(total, cur[z], cur[z + 1] if depth_hop else None, links, c, rows, lane)
            else:
                multiply_into(total, lambda q: cur[z + 1][c, q], link_rows(links, c, 36, vecs), False)
            return [cur[z][c, q] for q in range(6)], total

        products(acc_ref, rows, own, sides)
    part = packed_product(acc_ref[...], vecs)
    out_ref[...] = part + sofar_ref[...] if more else part


def out_shape_of(planes):
    return next(iter(planes.values())).shape


def last_hop_kernel(chunks, links_ref, top_ref, *refs):
    above = refs[:chunks]
    sofar_ref, out_ref, acc_ref = refs[chunks:]
    size, _, vecs, _ = above[0].shape
    acc_ref[...] = jnp.zeros_like(acc_ref)
    for k, ref in enumerate(above):

        def sides(c, ref=ref, first=k * size):
            total = [jnp.zeros((vecs, LANES), F32) for _ in range(6)]
            multiply_into(total, lambda q: ref[c, q], link_rows(links_ref, first + c, 0, vecs), False)
            return [top_ref[0, first + c, q] for q in range(6)], total

        products(acc_ref, size, False, sides)
    out_ref[...] = packed_product(acc_ref[...], vecs) + sofar_ref[...]


def norms_of(packed):
    n = packed.shape[0]
    diag = lane_index((n, LANES)) == lax.broadcasted_iota(jnp.int32, (n, LANES), 0)
    return jnp.where(diag, packed, 0.0)


def scatter_kernel(depth, pieces, *refs):
    out_ref = refs[-1]
    planes = plane_refs(refs[:-1], pieces)
    rows, _, vecs, _ = planes[0].shape
    stride = 6 * rows * depth

    def body(c, _):
        for z in range(depth):
            for q in range(6):
                start = q * rows * depth + c * depth + z
                out_ref[pl.ds(start, vecs, stride=stride), :] = planes[z][c, q]
        return 0

    lax.fori_loop(0, rows, body, 0)


def final_kernel(slot_ref, *refs):
    out_ref, grams_ref, scale_ref = refs[-3:]
    for k in range(2):
        term0, term1, field_ref = refs[3 * k : 3 * k + 3]
        n = term0.shape[0]

        @pl.when(pl.program_id(0) == k)
        def _(k=k, term0=term0, term1=term1, field_ref=field_ref):
            slot = slot_ref[0] if k == 0 else 1 - slot_ref[0]
            packed = term0[...] + term1[...]
            norm = norms_of(packed)
            down = lax.rsqrt(jnp.sum(norm, axis=1, keepdims=True))
            across = lax.rsqrt(jnp.sum(norm, axis=0, keepdims=True)[:, 0:n])
            scale = down * across
            over_re, over_im = packed[:, 0:n], packed[:, n : 2 * n]
            hop_re, hop_im = packed[:, 4 * n : 5 * n], packed[:, 5 * n : 6 * n]
            grams_ref[slot, 0, 0] = over_re * scale
            grams_ref[slot, 0, 1] = over_im * scale
            grams_ref[slot, 1, 0] = (6.0 * over_re - (hop_re + hop_re.T)) * scale
            grams_ref[slot, 1, 1] = (6.0 * over_im - (hop_im - hop_im.T)) * scale
            scale_ref[...] = jnp.broadcast_to(down, (n, LANES))
            size = out_ref.shape[0] // n

            def body(i, _):
                block = pl.ds(pl.multiple_of(i * size, 8), size)
                out_ref[block, :] = field_ref[block, :] * scale_ref[pl.ds(i, 1), :]
                return 0

            lax.fori_loop(0, n, body, 0)


def shifted(x, axis, by):
    n = lax.axis_size(axis)
    return lax.ppermute(x, axis, [(i, (i + by) % n) for i in range(n)])


def flipped(x, axis, bit):
    return lax.ppermute(x, axis, [(i, i ^ bit) for i in range(lax.axis_size(axis))])


def summed(x):
    size = lax.axis_size("sa")
    count = size.bit_length() - 1
    assert size == 1 << count

    def across(x, cfg, bits):
        pairs = range(lax.axis_size("cfg") * size)
        return lax.ppermute(x, ("cfg", "sa"), [(i, i ^ (cfg * size + bits)) for i in pairs])

    bit = 1
    for _ in range((count - 1) // 2):
        x = x + flipped(x, "sa", bit) + flipped(x, "sa", 2 * bit) + flipped(x, "sa", 3 * bit)
        bit *= 4
    if count % 2 == 0:
        x = x + flipped(x, "sa", bit)
        bit *= 2
    return (x, flipped(x, "sa", bit)), (across(x, 1, 0), across(x, 1, bit))


def on_device(links, vectors):
    slices, vecs, _, _, depth, plane = vectors.shape
    rows = plane // LANES
    assert slices == 2 and lax.axis_size("cfg") % 2 == 0 and lax.axis_size("ta") == 2
    pieces = pieces_of(depth)
    ends = [0] if len(pieces) == 1 else [0, len(pieces) - 1]
    inner = [k for k in range(len(pieces)) if k not in ends]
    core = lax.axis_index("ta")
    mine = lax.axis_index("cfg") % 2
    pick = jnp.stack([mine, core, 2 * core + mine]).astype(jnp.int32)
    field = [shape_of(len(p), rows, 6, vecs, LANES) for p in pieces]
    cut = [shape_of(rows // CHUNKS, 6, vecs, LANES)] * (len(ends) * CHUNKS)
    work = 1000 * LANES * vecs * rows
    many = vecs * 6 * rows * depth
    mine_block = ((many, LANES), lambda step, pick: (pick[0], 0))

    view = to_rows(vectors)

    def split(todo, chunks):
        outs = [field[k] for k in todo] + (cut if chunks else [])
        with jax.named_scope("split_ends" if chunks else "split_rest"):
            return call(
                functools.partial(split_kernel, depth, rows, vecs, [pieces[k] for k in todo], chunks),
                outs, view, pick=pick, whole={0: mine_block}, ops=1e5,
            )

    start = [None] * len(pieces)
    got = split(ends, CHUNKS)
    for k, x in zip(ends, got):
        start[k] = x
    sent = got[len(ends) :]
    links, view, *_ = lax.optimization_barrier((links, view, *sent))

    with jax.named_scope("links"):
        flat = links.reshape((links.shape[0], 54) + links.shape[-2:])
        given = lax.dynamic_index_in_dim(flat, 2 * (1 - core) + mine, 0, keepdims=False)
        came = flipped(given, "ta", 1)
    if inner:
        for k, x in zip(inner, split(inner, 0)):
            start[k] = x
    block = ((54 * (rows // 2) * depth, LANES), lambda step, pick: (pick[2], 0))
    table, top_links = call(
        functools.partial(link_kernel, depth, rows // 2),
        [shape_of(depth, rows, 90, LANES), shape_of(rows, 18, LANES)],
        to_rows(links), to_rows(came), pick=pick, whole={0: block}, ops=1e6,
    )
    prior = shifted(top_links, "sa", 1)

    def advance(step, cur, sent, old):
        factor = -(1.0 if old is None else 2.0) / SCALE
        with jax.named_scope(f"part_{step}"):
            new = list(call(
                functools.partial(part_kernel, depth, pieces, factor, old is None),
                field, table, *cur, *(old or []), ops=work * depth,
            ))
        given = []
        for j in range(CHUNKS):
            with jax.named_scope(f"halo_{step}_{j}"):
                low = shifted(sent[(len(ends) - 1) * CHUNKS + j], "sa", 1)
                high = shifted(sent[j], "sa", -1)
            last = j == CHUNKS - 1
            before = [given[i][k] for k in range(len(ends)) for i in range(j)] if last else []
            with jax.named_scope(f"close_{step}_{j}"):
                got = call(
                    functools.partial(close_kernel, factor, j, len(ends)),
                    ([field[k] for k in ends] if last else []) + cut[: len(ends)],
                    top_links, prior, low, high, *[new[k] for k in ends], *before, ops=work / 6,
                )
            given.append(got[-len(ends) :])
        for k, x in zip(ends, got):
            new[k] = x
        return new, [given[i][k] for k in range(len(ends)) for i in range(CHUNKS)]

    packed = shape_of(vecs, LANES)
    acc = [pltpu.VMEM((4 * vecs, 8 * vecs), F32)]

    def swapped(x, name):
        with jax.named_scope(name):
            return flipped(x, "cfg", 1)

    def grams_of(planes, tasks, sofar):
        return call(
            functools.partial(gram_kernel, [pieces[k] for k in planes], tasks, sofar is not None),
            packed, table, *[three[k] for k in planes], *([] if sofar is None else [sofar]),
            scratch=acc, ops=work * len(tasks) / 2,
        )

    one, sent_one = advance(0, start, sent, None)
    two, sent_two = advance(1, one, sent_one, start)
    three, sent_three = advance(2, two, sent_two, one)

    sofar = None
    if inner:
        middle = pieces[1]
        with jax.named_scope("gram_rest"):
            sofar = grams_of(inner, [(z, True, z + 1 in middle) for z in middle], None)
    above = []
    for j in range(CHUNKS):
        with jax.named_scope(f"above_{j}"):
            above.append(shifted(sent_three[j], "sa", -1))
    tasks = [(z, True, z + 1 < depth) for z in sorted({0, depth - 1})]
    if inner:
        tasks.append((depth - 2, False, True))
    with jax.named_scope("gram_ends"):
        sofar = grams_of(range(len(pieces)), tasks, sofar)
    with jax.named_scope("gram_last"):
        sofar = call(
            functools.partial(last_hop_kernel, CHUNKS), packed, top_links, three[-1], *above, sofar,
            scratch=acc, ops=work / 4,
        )
    with jax.named_scope("sum"):
        sum_mine, sum_other = summed(sofar)
    other = [swapped(x, f"swap_{k}") for k, x in enumerate(three)]

    def scattered(planes, name):
        with jax.named_scope(name):
            return call(functools.partial(scatter_kernel, depth, pieces), shape_of(many, LANES), *planes, ops=1e6)

    place = ((many, LANES), lambda step, pick: (jnp.where(step == 0, pick[0], 1 - pick[0]), 0))
    given = [*sum_mine, scattered(three, "scatter_mine"), *sum_other, scattered(other, "scatter_other")]
    with jax.named_scope("final"):
        out, grams = call(
            final_kernel, [shape_of(2 * many, LANES), shape_of(2, 2, 2, vecs, vecs)], *given,
            pick=pick, whole={len(given): place}, grid=2, ops=1e6, scratch=[pltpu.VMEM((vecs, LANES), F32)],
        )
    return from_rows(out, vectors.shape), grams


def solution(mesh):
    in_specs = (P(None, None, None, None, None, "sa", "ta"), P("ta", None, None, None, "sa", None))
    out_specs = (
        P(("cfg", "ta"), None, None, None, "sa", None),
        P(("cfg", "ta"), None, None, None, None),
    )
    return jax.shard_map(
        on_device, mesh=mesh, in_specs=in_specs, out_specs=out_specs, check_vma=False
    )
```

```python
import functools

import jax
import jax.numpy as jnp
from jax import lax
from jax.experimental import pallas as pl
from jax.experimental.pallas import tpu as pltpu
from jax.sharding import PartitionSpec as P


LX = 32
LANES = 128
SCALE = 5.5
F32 = jnp.float32
BF16 = jnp.bfloat16
VMEM = pl.BlockSpec(memory_space=pltpu.VMEM)
GRANT = 16 * 2**20


def shape_of(*dims, dtype=F32):
    return jax.ShapeDtypeStruct(dims, dtype)


def call(kernel, outs, *args, ops=1e6, scratch=(), pick=None, whole=None, grid=1):
    size = sum(a.size * 4 for a in args) + sum(4 * o.size for o in jax.tree.leaves(outs))
    several = isinstance(outs, (list, tuple))
    params = dict(
        out_shape=outs,
        compiler_params=pltpu.CompilerParams(vmem_limit_bytes=GRANT),
        cost_estimate=pl.CostEstimate(flops=int(ops), bytes_accessed=int(size), transcendentals=0),
    )
    if pick is None:
        specs = [VMEM] * len(outs) if several else VMEM
        return pl.pallas_call(
            kernel, in_specs=[VMEM] * len(args), out_specs=specs, scratch_shapes=scratch, **params
        )(*args)
    specs = [pl.BlockSpec(*whole[k]) if k in whole else VMEM for k in range(len(args) + len(outs))]
    spec = pltpu.PrefetchScalarGridSpec(
        num_scalar_prefetch=1, grid=(grid,), in_specs=specs[: len(args)], out_specs=specs[len(args) :],
        scratch_shapes=scratch,
    )
    return pl.pallas_call(kernel, grid_spec=spec, **params)(pick, *args)


def to_rows(x):
    depth, plane = x.shape[-2:]
    x = x.reshape(-1, depth, plane // LANES, LANES)
    return jnp.swapaxes(x, 1, 2).reshape(-1, LANES)


def from_rows(x, shape):
    depth, plane = shape[-2:]
    x = x.reshape(-1, plane // LANES, depth, LANES)
    return jnp.swapaxes(x, 1, 2).reshape(shape)


def pieces_of(depth):
    if depth == 1:
        return [[0]]
    if depth == 2:
        return [[0], [1]]
    return [[0], list(range(1, depth - 1)), [depth - 1]]


def plane_refs(refs, pieces):
    return {z: ref.at[k] for ref, planes in zip(refs, pieces) for k, z in enumerate(planes)}


def lane_index(shape):
    return lax.broadcasted_iota(jnp.int32, shape, len(shape) - 1)


def ahead_x(v, lane):
    wrap = (lane % LX) == LX - 1
    return jnp.where(wrap, pltpu.roll(v, LX - 1, v.ndim - 1), pltpu.roll(v, LANES - 1, v.ndim - 1))


def behind_x(v, lane):
    wrap = (lane % LX) == 0
    return jnp.where(wrap, pltpu.roll(v, LANES - LX + 1, v.ndim - 1), pltpu.roll(v, 1, v.ndim - 1))


def ahead_y(here, after, lane):
    ax = here.ndim - 1
    return jnp.where(lane < LANES - LX, pltpu.roll(here, LANES - LX, ax), pltpu.roll(after, LANES - LX, ax))


def behind_y(here, before, lane):
    ax = here.ndim - 1
    return jnp.where(lane < LX, pltpu.roll(before, LX, ax), pltpu.roll(here, LX, ax))


def split_kernel(depth, rows, vecs, pieces, _, v_ref, *out_refs):
    out = plane_refs(out_refs[: len(pieces)], pieces)
    stride = 6 * rows * depth

    def body(c, _):
        for z in out:
            for q in range(6):
                out[z][c, q] = v_ref[pl.ds(q * rows * depth + c * depth + z, vecs, stride=stride), :]
        return 0

    lax.fori_loop(0, rows, body, 0)
    if len(out_refs) > len(pieces):
        out_refs[-1][...] = v_ref[0:8, :]


def link_kernel(depth, half, pick_ref, kept_ref, came_ref, out_ref, top_ref):
    rows = 2 * half
    core = pick_ref[1]

    def body(c, _):
        for ref, first in ((kept_ref, core * half), (came_ref, (1 - core) * half)):
            for z in range(depth):
                out_ref[z, first + c, 0:54, :] = ref[pl.ds(c * depth + z, 54, stride=half * depth), :]
        return 0

    lax.fori_loop(0, half, body, 0)
    lane = lane_index((18, LANES))

    def shift(c, _):
        before = lax.rem(c + rows - 1, rows)
        for z in range(depth):
            out_ref[z, c, 54:72, :] = behind_x(out_ref[z, c, 0:18, :], lane)
            out_ref[z, c, 72:90, :] = behind_y(out_ref[z, c, 18:36, :], out_ref[z, before, 18:36, :], lane)
        top_ref[c, 0:18, :] = out_ref[depth - 1, c, 36:54, :]
        return 0

    lax.fori_loop(0, rows, shift, 0)


def multiply_into(total, field, link, adjoint):
    for col in range(3):
        re, im = field(col), field(3 + col)
        for row in range(3):
            entry = col * 3 + row if adjoint else row * 3 + col
            a, b = link(entry), link(9 + entry)
            if adjoint:
                total[row] = total[row] + a * re + b * im
                total[3 + row] = total[3 + row] + a * im - b * re
            else:
                total[row] = total[row] + a * re - b * im
                total[3 + row] = total[3 + row] + a * im + b * re


def link_rows(ref, c, first, vecs):
    def link(k):
        return jnp.broadcast_to(ref[c, first + k : first + k + 1, :], (vecs, LANES))

    return link


def forward_hops(total, cur, up, links, c, rows, lane):
    vecs = lane.shape[0]
    after = lax.rem(c + 1, rows)
    multiply_into(total, lambda q: ahead_x(cur[c, q], lane), link_rows(links, c, 0, vecs), False)
    multiply_into(total, lambda q: ahead_y(cur[c, q], cur[after, q], lane), link_rows(links, c, 18, vecs), False)
    if up is not None:
        multiply_into(total, lambda q: up[c, q], link_rows(links, c, 36, vecs), False)


def backward_hops(total, cur, down, links, down_links, c, rows, lane):
    vecs = lane.shape[0]
    before = lax.rem(c + rows - 1, rows)
    multiply_into(total, lambda q: behind_x(cur[c, q], lane), link_rows(links, c, 54, vecs), True)
    multiply_into(total, lambda q: behind_y(cur[c, q], cur[before, q], lane), link_rows(links, c, 72, vecs), True)
    if down is not None:
        multiply_into(total, lambda q: down[c, q], link_rows(down_links, c, 36, vecs), True)


def part_kernel(pieces, todo, factor, first, links_ref, *refs):
    refs = list(refs)
    cur = plane_refs([refs.pop(0) for _ in pieces], pieces)
    done = [pieces[k] for k in todo]
    old = None if first else plane_refs([refs.pop(0) for _ in todo], done)
    out = plane_refs(refs, done)
    rows, _, vecs, _ = cur[0].shape
    lane = lane_index((vecs, LANES))
    for z in out:

        def body(c, _, z=z):
            total = [cur[z][c, q] for q in range(6)]
            links = links_ref.at[z]
            forward_hops(total, cur[z], cur.get(z + 1), links, c, rows, lane)
            below = links_ref.at[z - 1] if z else None
            backward_hops(total, cur[z], cur.get(z - 1), links, below, c, rows, lane)
            for q in range(6):
                value = total[q] * factor
                out[z][c, q] = value if first else value - old[z][c, q]
            return 0

        lax.fori_loop(0, rows, body, 0)


def close_kernel(factor, behind, *refs):
    part_ref, out_ref = refs[-2].at[0], refs[-1].at[0]
    rows, _, vecs, _ = out_ref.shape

    def body(c, _):
        total = [jnp.zeros((vecs, LANES), F32) for _ in range(6)]
        for k, back in enumerate(behind):
            links_ref, halo_ref = refs[2 * k : 2 * k + 2]
            multiply_into(total, lambda q: halo_ref[0, c, q], link_rows(links_ref, c, 0, vecs), back)
        for q in range(6):
            out_ref[c, q] = part_ref[c, q] + total[q] * factor
        return 0

    lax.fori_loop(0, rows, body, 0)


def halves(x):
    high = x.astype(BF16)
    return high, (x - high.astype(F32)).astype(BF16)


def high_low(tiles):
    pairs = [halves(jnp.concatenate(tiles[k : k + 3], axis=1)) for k in (0, 3)]
    return [pairs[0][0], pairs[1][0], pairs[0][1], pairs[1][1]]


def products(acc_ref, rows, own, sides):
    def body(pair, _):
        stacks = [[], []]
        for c in (2 * pair, 2 * pair + 1):
            for stack, tiles in zip(stacks, sides(c)):
                stack.append(jnp.concatenate(high_low(tiles), axis=0))
        left, right = [jnp.concatenate(s, axis=1) for s in stacks]
        right = jnp.concatenate([left if own else jnp.zeros_like(left), right], axis=0)
        acc_ref[...] += lax.dot_general(left, right, (((1,), (1,)), ((), ())), preferred_element_type=F32)
        return 0

    lax.fori_loop(0, rows // 2, body, 0)


def packed_product(acc, n):
    acc = acc[0 : 2 * n] + acc[2 * n : 4 * n]
    acc = acc + pltpu.roll(acc, LANES - 2 * n, 1)
    re, im = acc[0:n], acc[n : 2 * n]
    real = re + pltpu.roll(im, LANES - n, 1)
    imag = re - pltpu.roll(im, n, 1)
    return jnp.where(lane_index((n, LANES)) % (2 * n) < n, real, imag)


def gram_kernel(pieces, tasks, more, links_ref, *refs):
    refs = list(refs)
    acc_ref, out_ref = refs.pop(), refs.pop()
    sofar_ref = refs.pop() if more else None
    cur = plane_refs(refs, pieces)
    rows, _, vecs, _ = out_shape_of(cur)
    lane = lane_index((vecs, LANES))
    acc_ref[...] = jnp.zeros_like(acc_ref)
    for z, own, depth_hop in tasks:

        def sides(c, z=z, own=own, depth_hop=depth_hop):
            total = [jnp.zeros((vecs, LANES), F32) for _ in range(6)]
            links = links_ref.at[z]
            if own:
                forward_hops(total, cur[z], cur[z + 1] if depth_hop else None, links, c, rows, lane)
            else:
                multiply_into(total, lambda q: cur[z + 1][c, q], link_rows(links, c, 36, vecs), False)
            return [cur[z][c, q] for q in range(6)], total

        products(acc_ref, rows, own, sides)
    part = packed_product(acc_ref[...], vecs)
    out_ref[...] = part + sofar_ref[...] if more else part


def out_shape_of(planes):
    return next(iter(planes.values())).shape


def last_hop_kernel(links_ref, top_ref, above_ref, sofar_ref, out_ref, acc_ref):
    rows, _, vecs, _ = top_ref.shape[1:]
    acc_ref[...] = jnp.zeros_like(acc_ref)

    def sides(c):
        total = [jnp.zeros((vecs, LANES), F32) for _ in range(6)]
        multiply_into(total, lambda q: above_ref[0, c, q], link_rows(links_ref, c, 0, vecs), False)
        return [top_ref[0, c, q] for q in range(6)], total

    products(acc_ref, rows, False, sides)
    out_ref[...] = packed_product(acc_ref[...], vecs) + sofar_ref[...]


def norms_of(packed):
    n = packed.shape[0]
    diag = lane_index((n, LANES)) == lax.broadcasted_iota(jnp.int32, (n, LANES), 0)
    return jnp.where(diag, packed, 0.0)


def scatter_kernel(depth, pieces, *refs):
    out_ref = refs[-1]
    planes = plane_refs(refs[:-1], pieces)
    rows, _, vecs, _ = planes[0].shape
    stride = 6 * rows * depth

    def body(c, _):
        for z in range(depth):
            for q in range(6):
                start = q * rows * depth + c * depth + z
                out_ref[pl.ds(start, vecs, stride=stride), :] = planes[z][c, q]
        return 0

    lax.fori_loop(0, rows, body, 0)


def final_kernel(slot_ref, *refs):
    out_ref, grams_ref, scale_ref = refs[-3:]
    for k in range(2):
        term0, term1, field_ref = refs[3 * k : 3 * k + 3]
        n = term0.shape[0]

        @pl.when(pl.program_id(0) == k)
        def _(k=k, term0=term0, term1=term1, field_ref=field_ref):
            slot = slot_ref[0] if k == 0 else 1 - slot_ref[0]
            packed = term0[...] + term1[...]
            norm = norms_of(packed)
            down = lax.rsqrt(jnp.sum(norm, axis=1, keepdims=True))
            across = lax.rsqrt(jnp.sum(norm, axis=0, keepdims=True)[:, 0:n])
            scale = down * across
            over_re, over_im = packed[:, 0:n], packed[:, n : 2 * n]
            hop_re, hop_im = packed[:, 4 * n : 5 * n], packed[:, 5 * n : 6 * n]
            grams_ref[slot, 0, 0] = over_re * scale
            grams_ref[slot, 0, 1] = over_im * scale
            grams_ref[slot, 1, 0] = (6.0 * over_re - (hop_re + hop_re.T)) * scale
            grams_ref[slot, 1, 1] = (6.0 * over_im - (hop_im - hop_im.T)) * scale
            scale_ref[...] = jnp.broadcast_to(down, (n, LANES))
            size = out_ref.shape[0] // n

            def body(i, _):
                block = pl.ds(pl.multiple_of(i * size, 8), size)
                out_ref[block, :] = field_ref[block, :] * scale_ref[pl.ds(i, 1), :]
                return 0

            lax.fori_loop(0, n, body, 0)


def shifted(x, axis, by):
    n = lax.axis_size(axis)
    return lax.ppermute(x, axis, [(i, (i + by) % n) for i in range(n)])


def flipped(x, axis, bit):
    return lax.ppermute(x, axis, [(i, i ^ bit) for i in range(lax.axis_size(axis))])


def summed(x):
    size = lax.axis_size("sa")
    count = size.bit_length() - 1
    assert size == 1 << count

    def across(x, cfg, bits):
        pairs = range(lax.axis_size("cfg") * size)
        return lax.ppermute(x, ("cfg", "sa"), [(i, i ^ (cfg * size + bits)) for i in pairs])

    bit = 1
    for _ in range((count - 1) // 2):
        x = x + flipped(x, "sa", bit) + flipped(x, "sa", 2 * bit) + flipped(x, "sa", 3 * bit)
        bit *= 4
    if count % 2 == 0:
        x = x + flipped(x, "sa", bit)
        bit *= 2
    return (x, flipped(x, "sa", bit)), (across(x, 1, 0), across(x, 1, bit))


def on_device(links, vectors):
    slices, vecs, _, _, depth, plane = vectors.shape
    rows = plane // LANES
    assert slices == 2 and lax.axis_size("cfg") % 2 == 0 and lax.axis_size("ta") == 2
    pieces = pieces_of(depth)
    ends = [0] if len(pieces) == 1 else [0, len(pieces) - 1]
    inner = [k for k in range(len(pieces)) if k not in ends]
    core = lax.axis_index("ta")
    mine = lax.axis_index("cfg") % 2
    pick = jnp.stack([mine, core, 2 * core + mine]).astype(jnp.int32)
    field = [shape_of(len(p), rows, 6, vecs, LANES) for p in pieces]
    work = 1000 * LANES * vecs * rows
    many = vecs * 6 * rows * depth
    mine_block = ((many, LANES), lambda step, pick: (pick[0], 0))

    view = to_rows(vectors)

    def split(todo, token):
        return call(
            functools.partial(split_kernel, depth, rows, vecs, [pieces[k] for k in todo]),
            [field[k] for k in todo] + token, view, pick=pick, whole={0: mine_block}, ops=1e5,
        )

    start = [None] * len(pieces)
    *got, token = split(ends, [shape_of(8, LANES)])
    for k, x in zip(ends, got):
        start[k] = x
    links, view, _ = lax.optimization_barrier((links, view, token))

    flat = links.reshape((links.shape[0], 54) + links.shape[-2:])
    given = lax.dynamic_index_in_dim(flat, 2 * (1 - core) + mine, 0, keepdims=False)
    came = flipped(given, "ta", 1)
    if inner:
        for k, x in zip(inner, split(inner, [])):
            start[k] = x
    block = ((54 * (rows // 2) * depth, LANES), lambda step, pick: (pick[2], 0))
    table, top_links = call(
        functools.partial(link_kernel, depth, rows // 2),
        [shape_of(depth, rows, 90, LANES), shape_of(rows, 18, LANES)],
        to_rows(links), to_rows(came), pick=pick, whole={0: block}, ops=1e6,
    )
    prior = shifted(top_links, "sa", 1)

    def advance(cur, old):
        factor = -(1.0 if old is None else 2.0) / SCALE
        low = shifted(cur[-1], "sa", 1)
        high = shifted(cur[0], "sa", -1)
        new = [None] * len(pieces)
        for todo in (inner, ends):
            if todo:
                got = call(
                    functools.partial(part_kernel, pieces, todo, factor, old is None),
                    [field[k] for k in todo], table, *cur, *([] if old is None else [old[k] for k in todo]),
                    ops=work * sum(len(pieces[k]) for k in todo),
                )
                for k, x in zip(todo, got):
                    new[k] = x
        sides = [(0, True, prior, low), (len(pieces) - 1, False, top_links, high)]
        for k in ends:
            used = [side for side in sides if side[0] == k]
            operands = [x for side in used for x in side[2:]]
            (new[k],) = call(
                functools.partial(close_kernel, factor, [side[1] for side in used]),
                [field[k]], *operands, new[k], ops=work / 6,
            )
        return new

    packed = shape_of(vecs, LANES)
    acc = [pltpu.VMEM((4 * vecs, 8 * vecs), F32)]

    def swapped(x):
        return flipped(x, "cfg", 1)

    def grams_of(planes, tasks, sofar):
        return call(
            functools.partial(gram_kernel, [pieces[k] for k in planes], tasks, sofar is not None),
            packed, table, *[three[k] for k in planes], *([] if sofar is None else [sofar]),
            scratch=acc, ops=work * len(tasks) / 2,
        )

    one = advance(start, None)
    two = advance(one, start)
    three = advance(two, one)

    sofar = None
    if inner:
        middle = pieces[1]
        sofar = grams_of(inner, [(z, True, z + 1 in middle) for z in middle], None)
    above = shifted(three[0], "sa", -1)
    tasks = [(z, True, z + 1 < depth) for z in sorted({0, depth - 1})]
    if inner:
        tasks.append((depth - 2, False, True))
    sofar = grams_of(range(len(pieces)), tasks, sofar)
    sofar = call(
        last_hop_kernel, packed, top_links, three[-1], above, sofar,
        scratch=acc, ops=work / 4,
    )
    sum_mine, sum_other = summed(sofar)
    other = [swapped(x) for x in three]

    def scattered(planes):
        return call(functools.partial(scatter_kernel, depth, pieces), shape_of(many, LANES), *planes, ops=1e6)

    place = ((many, LANES), lambda step, pick: (jnp.where(step == 0, pick[0], 1 - pick[0]), 0))
    given = [*sum_mine, scattered(three), *sum_other, scattered(other)]
    out, grams = call(
        final_kernel, [shape_of(2 * many, LANES), shape_of(2, 2, 2, vecs, vecs)], *given,
        pick=pick, whole={len(given): place}, grid=2, ops=1e6, scratch=[pltpu.VMEM((vecs, LANES), F32)],
    )
    return from_rows(out, vectors.shape), grams


def solution(mesh):
    in_specs = (P(None, None, None, None, None, "sa", "ta"), P("ta", None, None, None, "sa", None))
    out_specs = (
        P(("cfg", "ta"), None, None, None, "sa", None),
        P(("cfg", "ta"), None, None, None, None),
    )
    return jax.shard_map(on_device, mesh=mesh, in_specs=in_specs, out_specs=out_specs, check_vma=False)
```

```python
import functools

import jax
import jax.numpy as jnp
from jax import lax
from jax.experimental import pallas as pl
from jax.experimental.pallas import tpu as pltpu
from jax.sharding import PartitionSpec as P


LX = 32
LANES = 128
SCALE = 5.5
F32 = jnp.float32
BF16 = jnp.bfloat16
VMEM = pl.BlockSpec(memory_space=pltpu.VMEM)
FAR = pl.BlockSpec(memory_space=pltpu.HBM)
GRANT = 16 * 2**20


def shape_of(*dims, dtype=F32):
    return jax.ShapeDtypeStruct(dims, dtype)


def call(kernel, outs, *args, ops=1e6, scratch=(), pick=None, far=(), place=None, grid=1, alias=None):
    size = sum(a.size * 4 for a in args) + sum(4 * o.size for o in jax.tree.leaves(outs))
    several = isinstance(outs, (list, tuple))
    params = dict(
        out_shape=outs,
        compiler_params=pltpu.CompilerParams(vmem_limit_bytes=GRANT),
        cost_estimate=pl.CostEstimate(flops=int(ops), bytes_accessed=int(size), transcendentals=0),
        input_output_aliases=alias or {},
    )
    in_specs = [FAR if k in far else VMEM for k in range(len(args))]
    out_specs = [VMEM] * len(outs) if several else VMEM
    if pick is None:
        return pl.pallas_call(
            kernel, in_specs=in_specs, out_specs=out_specs, scratch_shapes=scratch, **params
        )(*args)
    if place is not None:
        out_specs = [pl.BlockSpec(*place)] + out_specs[1:]
    spec = pltpu.PrefetchScalarGridSpec(
        num_scalar_prefetch=1, grid=(grid,), in_specs=in_specs, out_specs=out_specs, scratch_shapes=scratch
    )
    return pl.pallas_call(kernel, grid_spec=spec, **params)(pick, *args)


def to_rows(x):
    depth, plane = x.shape[-2:]
    x = x.reshape(-1, depth, plane // LANES, LANES)
    return jnp.swapaxes(x, 1, 2).reshape(-1, LANES)


def from_rows(x, shape):
    depth, plane = shape[-2:]
    x = x.reshape(-1, plane // LANES, depth, LANES)
    return jnp.swapaxes(x, 1, 2).reshape(shape)


def pieces_of(depth):
    if depth == 1:
        return [[0]]
    if depth == 2:
        return [[0], [1]]
    return [[0], list(range(1, depth - 1)), [depth - 1]]


def plane_refs(refs, pieces):
    return {z: ref.at[k] for ref, planes in zip(refs, pieces) for k, z in enumerate(planes)}


def lane_index(shape):
    return lax.broadcasted_iota(jnp.int32, shape, len(shape) - 1)


def ahead_x(v, lane):
    wrap = (lane % LX) == LX - 1
    return jnp.where(wrap, pltpu.roll(v, LX - 1, v.ndim - 1), pltpu.roll(v, LANES - 1, v.ndim - 1))


def behind_x(v, lane):
    wrap = (lane % LX) == 0
    return jnp.where(wrap, pltpu.roll(v, LANES - LX + 1, v.ndim - 1), pltpu.roll(v, 1, v.ndim - 1))


def ahead_y(here, after, lane):
    ax = here.ndim - 1
    return jnp.where(lane < LANES - LX, pltpu.roll(here, LANES - LX, ax), pltpu.roll(after, LANES - LX, ax))


def behind_y(here, before, lane):
    ax = here.ndim - 1
    return jnp.where(lane < LX, pltpu.roll(before, LX, ax), pltpu.roll(here, LX, ax))


def take_planes(out, raw_ref, first, count, rows, depth):
    stride = 6 * rows * depth

    def body(c, _):
        for z in out:
            for q in range(6):
                start = first * stride + q * rows * depth + c * depth + z
                out[z][c, q, first : first + count, :] = raw_ref[pl.ds(start, count, stride=stride), :]
        return 0

    lax.fori_loop(0, rows, body, 0)


def ends_kernel(depth, pieces, pick_ref, far_ref, raw_ref, *refs):
    *out_refs, sems = refs
    out = plane_refs(out_refs, pieces)
    rows, _, vecs, _ = out[0].shape
    size = raw_ref.shape[0]
    parts = 2
    copies = []
    for k in range(parts):
        block = pl.ds(k * (size // parts), size // parts)
        source = pl.ds(pick_ref[0] * size + k * (size // parts), size // parts)
        copies.append(pltpu.make_async_copy(far_ref.at[source], raw_ref.at[block], sems.at[k]))
        copies[-1].start()
    for k in range(parts):
        copies[k].wait()
        take_planes(out, raw_ref, k * (vecs // parts), vecs // parts, rows, depth)


def rest_kernel(depth, pieces, raw_ref, *out_refs):
    out = plane_refs(out_refs, pieces)
    rows, _, vecs, _ = out[pieces[0][0]].shape
    take_planes(out, raw_ref, 0, vecs, rows, depth)


def link_kernel(depth, half, pick_ref, far_ref, came_ref, table_ref, behind_ref, top_ref, sem):
    core = pick_ref[1]
    copy = pltpu.make_async_copy(far_ref.at[pick_ref[2]], table_ref.at[core], sem)
    copy.start()
    table_ref[1 - core] = came_ref[...]
    copy.wait()
    count = half * depth
    lane = lane_index((count, LANES))

    def shift(d, _):
        for h in range(2):
            behind_ref[h, d] = behind_x(table_ref[h, d], lane)
        low, high = table_ref[0, 18 + d], table_ref[1, 18 + d]
        for h, here, wrap in ((0, low, high), (1, high, low)):
            before = wrap[count - depth :]
            if half > 1:
                before = jnp.concatenate([before, here[: count - depth]], axis=0)
            behind_ref[h, 18 + d] = behind_y(here, before, lane)
        for h in range(2):
            top_ref[d, h * half : (h + 1) * half, :] = table_ref[h, 36 + d, pl.ds(depth - 1, half, stride=depth), :]
        return 0

    lax.fori_loop(0, 18, shift, 0)


def multiply_into(total, field, link, adjoint):
    for col in range(3):
        re, im = field(col), field(3 + col)
        for row in range(3):
            entry = col * 3 + row if adjoint else row * 3 + col
            a, b = link(entry), link(9 + entry)
            if adjoint:
                total[row] = total[row] + a * re + b * im
                total[3 + row] = total[3 + row] + a * im - b * re
            else:
                total[row] = total[row] + a * re - b * im
                total[3 + row] = total[3 + row] + a * im + b * re


def rows_of(ref, c, z, depth, first, vecs):
    half = ref.shape[2] // depth
    row = lax.rem(c, half) * depth + z

    def link(k):
        return jnp.broadcast_to(ref[c // half, first + k, pl.ds(row, 1), :], (vecs, LANES))

    return link


def edge_rows(ref, c, vecs):
    def link(k):
        return jnp.broadcast_to(ref[k, pl.ds(c, 1), :], (vecs, LANES))

    return link


def forward_hops(total, cur, up, table, c, z, depth, lane):
    rows, _, vecs, _ = cur.shape
    after = lax.rem(c + 1, rows)
    multiply_into(total, lambda q: ahead_x(cur[c, q], lane), rows_of(table, c, z, depth, 0, vecs), False)
    multiply_into(
        total, lambda q: ahead_y(cur[c, q], cur[after, q], lane), rows_of(table, c, z, depth, 18, vecs), False
    )
    if up is not None:
        multiply_into(total, lambda q: up[c, q], rows_of(table, c, z, depth, 36, vecs), False)


def backward_hops(total, cur, down, table, behind, c, z, depth, lane):
    rows, _, vecs, _ = cur.shape
    before = lax.rem(c + rows - 1, rows)
    multiply_into(total, lambda q: behind_x(cur[c, q], lane), rows_of(behind, c, z, depth, 0, vecs), True)
    multiply_into(
        total, lambda q: behind_y(cur[c, q], cur[before, q], lane), rows_of(behind, c, z, depth, 18, vecs), True
    )
    if down is not None:
        multiply_into(total, lambda q: down[c, q], rows_of(table, c, z - 1, depth, 36, vecs), True)


def part_kernel(depth, pieces, todo, factor, first, table_ref, behind_ref, *refs):
    refs = list(refs)
    cur = plane_refs([refs.pop(0) for _ in pieces], pieces)
    done = [pieces[k] for k in todo]
    old = None if first else plane_refs([refs.pop(0) for _ in todo], done)
    out = plane_refs(refs, done)
    rows, _, vecs, _ = cur[0].shape
    lane = lane_index((vecs, LANES))
    for z in out:

        def body(c, _, z=z):
            total = [cur[z][c, q] for q in range(6)]
            forward_hops(total, cur[z], cur.get(z + 1), table_ref, c, z, depth, lane)
            backward_hops(total, cur[z], cur.get(z - 1), table_ref, behind_ref, c, z, depth, lane)
            for q in range(6):
                value = total[q] * factor
                out[z][c, q] = value if first else value - old[z][c, q]
            return 0

        lax.fori_loop(0, rows, body, 0)


def close_kernel(factor, behind, *refs):
    part_ref, out_ref = refs[-2].at[0], refs[-1].at[0]
    rows, _, vecs, _ = out_ref.shape

    def body(c, _):
        total = [jnp.zeros((vecs, LANES), F32) for _ in range(6)]
        for k, back in enumerate(behind):
            links_ref, halo_ref = refs[2 * k : 2 * k + 2]
            multiply_into(total, lambda q: halo_ref[0, c, q], edge_rows(links_ref, c, vecs), back)
        for q in range(6):
            out_ref[c, q] = part_ref[c, q] + total[q] * factor
        return 0

    lax.fori_loop(0, rows, body, 0)


def halves(x):
    high = x.astype(BF16)
    return high, (x - high.astype(F32)).astype(BF16)


def high_low(tiles):
    pairs = [halves(jnp.concatenate(tiles[k : k + 3], axis=1)) for k in (0, 3)]
    return [pairs[0][0], pairs[1][0], pairs[0][1], pairs[1][1]]


def products(acc_ref, rows, own, sides):
    def body(pair, _):
        stacks = [[], []]
        for c in (2 * pair, 2 * pair + 1):
            for stack, tiles in zip(stacks, sides(c)):
                stack.append(jnp.concatenate(high_low(tiles), axis=0))
        left, right = [jnp.concatenate(s, axis=1) for s in stacks]
        right = jnp.concatenate([left if own else jnp.zeros_like(left), right], axis=0)
        acc_ref[...] += lax.dot_general(left, right, (((1,), (1,)), ((), ())), preferred_element_type=F32)
        return 0

    lax.fori_loop(0, rows // 2, body, 0)


def packed_product(acc, n):
    acc = acc[0 : 2 * n] + acc[2 * n : 4 * n]
    acc = acc + pltpu.roll(acc, LANES - 2 * n, 1)
    re, im = acc[0:n], acc[n : 2 * n]
    real = re + pltpu.roll(im, LANES - n, 1)
    imag = re - pltpu.roll(im, n, 1)
    return jnp.where(lane_index((n, LANES)) % (2 * n) < n, real, imag)


def gram_kernel(depth, pieces, tasks, more, table_ref, *refs):
    refs = list(refs)
    acc_ref, out_ref = refs.pop(), refs.pop()
    sofar_ref = refs.pop() if more else None
    cur = plane_refs(refs, pieces)
    rows, _, vecs, _ = cur[tasks[0][0]].shape
    lane = lane_index((vecs, LANES))
    acc_ref[...] = jnp.zeros_like(acc_ref)
    for z, own, depth_hop in tasks:

        def sides(c, z=z, own=own, depth_hop=depth_hop):
            total = [jnp.zeros((vecs, LANES), F32) for _ in range(6)]
            if own:
                forward_hops(total, cur[z], cur[z + 1] if depth_hop else None, table_ref, c, z, depth, lane)
            else:
                up = cur[z + 1]
                multiply_into(total, lambda q: up[c, q], rows_of(table_ref, c, z, depth, 36, vecs), False)
            return [cur[z][c, q] for q in range(6)], total

        products(acc_ref, rows, own, sides)
    part = packed_product(acc_ref[...], vecs)
    out_ref[...] = part + sofar_ref[...] if more else part


def last_hop_kernel(links_ref, top_ref, above_ref, sofar_ref, out_ref, acc_ref):
    rows, _, vecs, _ = top_ref.shape[1:]
    acc_ref[...] = jnp.zeros_like(acc_ref)

    def sides(c):
        total = [jnp.zeros((vecs, LANES), F32) for _ in range(6)]
        multiply_into(total, lambda q: above_ref[0, c, q], edge_rows(links_ref, c, vecs), False)
        return [top_ref[0, c, q] for q in range(6)], total

    products(acc_ref, rows, False, sides)
    out_ref[...] = packed_product(acc_ref[...], vecs) + sofar_ref[...]


def norms_of(packed):
    n = packed.shape[0]
    diag = lane_index((n, LANES)) == lax.broadcasted_iota(jnp.int32, (n, LANES), 0)
    return jnp.where(diag, packed, 0.0)


def scatter_kernel(depth, planes, piece_ref, *refs):
    out_ref = refs[-1]
    rows, _, vecs, _ = piece_ref.shape[1:]
    stride = 6 * rows * depth

    def body(c, _):
        for k, z in enumerate(planes):
            for q in range(6):
                start = q * rows * depth + c * depth + z
                out_ref[pl.ds(start, vecs, stride=stride), :] = piece_ref[k, c, q]
        return 0

    lax.fori_loop(0, rows, body, 0)


def final_kernel(steps, slot_ref, *refs):
    out_ref, grams_ref, scale_ref = refs[-3:]
    step = pl.program_id(0)
    for k in range(2):
        term0, term1, field_ref = refs[3 * k : 3 * k + 3]
        n = term0.shape[0]
        slot = slot_ref[0] if k == 0 else 1 - slot_ref[0]

        def normalised(term0=term0, term1=term1):
            packed = term0[...] + term1[...]
            norm = norms_of(packed)
            return packed, norm, lax.rsqrt(jnp.sum(norm, axis=1, keepdims=True))

        @pl.when(step == k * steps)
        def _(n=n, normalised=normalised):
            scale_ref[...] = jnp.broadcast_to(normalised()[2], (n, LANES))

        @pl.when((step >= k * steps) & (step < (k + 1) * steps))
        def _(k=k, n=n, field_ref=field_ref):
            size = field_ref.shape[0] // n
            each = n // steps

            def body(i, _):
                vec = (step - k * steps) * each + i
                source = pl.ds(pl.multiple_of(vec * size, 8), size)
                target = pl.ds(pl.multiple_of(i * size, 8), size)
                out_ref[target, :] = field_ref[source, :] * scale_ref[pl.ds(vec, 1), :]
                return 0

            lax.fori_loop(0, each, body, 0)

        @pl.when(step == (k + 1) * steps - 2)
        def _(n=n, slot=slot, normalised=normalised):
            packed, norm, down = normalised()
            across = lax.rsqrt(jnp.sum(norm, axis=0, keepdims=True)[:, 0:n])
            scale = down * across
            over_re, over_im = packed[:, 0:n], packed[:, n : 2 * n]
            hop_re, hop_im = packed[:, 4 * n : 5 * n], packed[:, 5 * n : 6 * n]
            grams_ref[slot, 0, 0] = over_re * scale
            grams_ref[slot, 0, 1] = over_im * scale
            grams_ref[slot, 1, 0] = (6.0 * over_re - (hop_re + hop_re.T)) * scale
            grams_ref[slot, 1, 1] = (6.0 * over_im - (hop_im - hop_im.T)) * scale


def shifted(x, axis, by):
    n = lax.axis_size(axis)
    return lax.ppermute(x, axis, [(i, (i + by) % n) for i in range(n)])


def flipped(x, axis, bit):
    return lax.ppermute(x, axis, [(i, i ^ bit) for i in range(lax.axis_size(axis))])


def summed(x):
    size = lax.axis_size("sa")
    count = size.bit_length() - 1
    assert size == 1 << count

    def across(x, cfg, bits):
        pairs = range(lax.axis_size("cfg") * size)
        return lax.ppermute(x, ("cfg", "sa"), [(i, i ^ (cfg * size + bits)) for i in pairs])

    bit = 1
    for _ in range((count - 1) // 2):
        x = x + flipped(x, "sa", bit) + flipped(x, "sa", 2 * bit) + flipped(x, "sa", 3 * bit)
        bit *= 4
    if count % 2 == 0:
        x = x + flipped(x, "sa", bit)
        bit *= 2
    return (x, flipped(x, "sa", bit)), (across(x, 1, 0), across(x, 1, bit))


def on_device(links, vectors):
    slices, vecs, _, _, depth, plane = vectors.shape
    rows = plane // LANES
    assert slices == 2 and lax.axis_size("cfg") % 2 == 0 and lax.axis_size("ta") == 2
    pieces = pieces_of(depth)
    ends = [0] if len(pieces) == 1 else [0, len(pieces) - 1]
    inner = [k for k in range(len(pieces)) if k not in ends]
    core = lax.axis_index("ta")
    mine = lax.axis_index("cfg") % 2
    pick = jnp.stack([mine, core, 2 * core + mine]).astype(jnp.int32)
    field = [shape_of(len(p), rows, 6, vecs, LANES) for p in pieces]
    work = 1000 * LANES * vecs * rows
    many = vecs * 6 * rows * depth
    half = rows // 2
    sem = pltpu.SemaphoreType.DMA

    raw, *got = call(
        functools.partial(ends_kernel, depth, [pieces[k] for k in ends]),
        [shape_of(many, LANES)] + [field[k] for k in ends],
        to_rows(vectors), pick=pick, far=(0,), scratch=[sem((2,))], ops=1e5,
    )
    start = [None] * len(pieces)
    for k, x in zip(ends, got):
        start[k] = x
    flat = links.reshape((links.shape[0], 54) + links.shape[-2:])
    given = lax.dynamic_index_in_dim(flat, 2 * (1 - core) + mine, 0, keepdims=False)
    came = flipped(given, "ta", 1)
    if inner:
        got = call(
            functools.partial(rest_kernel, depth, [pieces[k] for k in inner]),
            [field[k] for k in inner], raw, ops=1e5,
        )
        for k, x in zip(inner, got):
            start[k] = x
    table, behind, top_links = call(
        functools.partial(link_kernel, depth, half),
        [shape_of(2, 54, half * depth, LANES), shape_of(2, 36, half * depth, LANES), shape_of(18, rows, LANES)],
        to_rows(links).reshape(-1, 54, half * depth, LANES),
        to_rows(came).reshape(54, half * depth, LANES),
        pick=pick, far=(0,), scratch=[sem], ops=1e6,
    )
    prior = shifted(top_links, "sa", 1)

    def advance(cur, old):
        factor = -(1.0 if old is None else 2.0) / SCALE
        low = shifted(cur[-1], "sa", 1)
        high = shifted(cur[0], "sa", -1)
        new = [None] * len(pieces)
        for todo in (inner, ends):
            if todo:
                got = call(
                    functools.partial(part_kernel, depth, pieces, todo, factor, old is None),
                    [field[k] for k in todo], table, behind, *cur, *([] if old is None else [old[k] for k in todo]),
                    ops=work * sum(len(pieces[k]) for k in todo),
                )
                for k, x in zip(todo, got):
                    new[k] = x
        sides = [(0, True, prior, low), (len(pieces) - 1, False, top_links, high)]
        for k in ends:
            used = [side for side in sides if side[0] == k]
            operands = [x for side in used for x in side[2:]]
            (new[k],) = call(
                functools.partial(close_kernel, factor, [side[1] for side in used]),
                [field[k]], *operands, new[k], ops=work / 6,
            )
        return new

    packed = shape_of(vecs, LANES)
    acc = [pltpu.VMEM((4 * vecs, 8 * vecs), F32)]

    def swapped(x):
        return flipped(x, "cfg", 1)

    def grams_of(planes, tasks, sofar):
        return call(
            functools.partial(gram_kernel, depth, [pieces[k] for k in planes], tasks, sofar is not None),
            packed, table, *[three[k] for k in planes], *([] if sofar is None else [sofar]),
            scratch=acc, ops=work * len(tasks) / 2,
        )

    one = advance(start, None)
    two = advance(one, start)
    three = advance(two, one)

    sofar = None
    if inner:
        middle = pieces[1]
        sofar = grams_of(inner, [(z, True, z + 1 in middle) for z in middle], None)
    above = shifted(three[0], "sa", -1)
    tasks = [(z, True, z + 1 < depth) for z in sorted({0, depth - 1})]
    if inner:
        tasks.append((depth - 2, False, True))
    sofar = grams_of(range(len(pieces)), tasks, sofar)
    sofar = call(
        last_hop_kernel, packed, top_links, three[-1], above, sofar,
        scratch=acc, ops=work / 4,
    )
    sum_mine, sum_other = summed(sofar)
    other = [swapped(x) for x in three]

    def scattered(planes):
        out = None
        for k in inner + ends:
            out = call(
                functools.partial(scatter_kernel, depth, pieces[k]), shape_of(many, LANES),
                planes[k], *([] if out is None else [out]), alias={} if out is None else {1: 0}, ops=1e5,
            )
        return out

    steps = 4
    assert vecs % steps == 0

    def target(step, pick):
        slot = jnp.where(step < steps, pick[0], 1 - pick[0])
        return slot * steps + lax.rem(step, steps), 0

    out, grams = call(
        functools.partial(final_kernel, steps), [shape_of(2 * many, LANES), shape_of(2, 2, 2, vecs, vecs)],
        *sum_mine, scattered(three), *sum_other, scattered(other),
        pick=pick, place=((many // steps, LANES), target), grid=2 * steps, ops=1e6,
        scratch=[pltpu.VMEM((vecs, LANES), F32)],
    )
    return from_rows(out, vectors.shape), grams


def solution(mesh):
    in_specs = (P(None, None, None, None, None, "sa", "ta"), P("ta", None, None, None, "sa", None))
    out_specs = (
        P(("cfg", "ta"), None, None, None, "sa", None),
        P(("cfg", "ta"), None, None, None, None),
    )
    return jax.shard_map(on_device, mesh=mesh, in_specs=in_specs, out_specs=out_specs, check_vma=False)
```

```python
import functools

import jax
import jax.numpy as jnp
from jax import lax
from jax.experimental import pallas as pl
from jax.experimental.pallas import tpu as pltpu
from jax.sharding import PartitionSpec as P


LX = 32
LANES = 128
SCALE = 5.5
F32 = jnp.float32
BF16 = jnp.bfloat16
VMEM = pl.BlockSpec(memory_space=pltpu.VMEM)
FAR = pl.BlockSpec(memory_space=pltpu.HBM)
GRANT = 16 * 2**20


def shape_of(*dims, dtype=F32):
    return jax.ShapeDtypeStruct(dims, dtype)


def call(kernel, outs, *args, ops=1e6, scratch=(), pick=None, far=(), place=None, grid=1, alias=None):
    size = sum(a.size * 4 for a in args) + sum(4 * o.size for o in jax.tree.leaves(outs))
    several = isinstance(outs, (list, tuple))
    params = dict(
        out_shape=outs,
        compiler_params=pltpu.CompilerParams(vmem_limit_bytes=GRANT),
        cost_estimate=pl.CostEstimate(flops=int(ops), bytes_accessed=int(size), transcendentals=0),
        input_output_aliases=alias or {},
    )
    in_specs = [FAR if k in far else VMEM for k in range(len(args))]
    out_specs = [VMEM] * len(outs) if several else VMEM
    if pick is None:
        return pl.pallas_call(
            kernel, in_specs=in_specs, out_specs=out_specs, scratch_shapes=scratch, **params
        )(*args)
    if place is not None:
        out_specs = [pl.BlockSpec(*place)] + out_specs[1:]
    spec = pltpu.PrefetchScalarGridSpec(
        num_scalar_prefetch=1, grid=(grid,), in_specs=in_specs, out_specs=out_specs, scratch_shapes=scratch
    )
    return pl.pallas_call(kernel, grid_spec=spec, **params)(pick, *args)


def to_rows(x):
    depth, plane = x.shape[-2:]
    x = x.reshape(-1, depth, plane // LANES, LANES)
    return jnp.swapaxes(x, 1, 2).reshape(-1, LANES)


def from_rows(x, shape):
    depth, plane = shape[-2:]
    x = x.reshape(-1, plane // LANES, depth, LANES)
    return jnp.swapaxes(x, 1, 2).reshape(shape)


def pieces_of(depth):
    if depth == 1:
        return [[0]]
    if depth == 2:
        return [[0], [1]]
    return [[0], list(range(1, depth - 1)), [depth - 1]]


def plane_refs(refs, pieces):
    return {z: ref.at[k] for ref, planes in zip(refs, pieces) for k, z in enumerate(planes)}


def lane_index(shape):
    return lax.broadcasted_iota(jnp.int32, shape, len(shape) - 1)


def ahead_x(v, lane):
    wrap = (lane % LX) == LX - 1
    return jnp.where(wrap, pltpu.roll(v, LX - 1, v.ndim - 1), pltpu.roll(v, LANES - 1, v.ndim - 1))


def behind_x(v, lane):
    wrap = (lane % LX) == 0
    return jnp.where(wrap, pltpu.roll(v, LANES - LX + 1, v.ndim - 1), pltpu.roll(v, 1, v.ndim - 1))


def ahead_y(here, after, lane):
    ax = here.ndim - 1
    return jnp.where(lane < LANES - LX, pltpu.roll(here, LANES - LX, ax), pltpu.roll(after, LANES - LX, ax))


def behind_y(here, before, lane):
    ax = here.ndim - 1
    return jnp.where(lane < LX, pltpu.roll(before, LX, ax), pltpu.roll(here, LX, ax))


def take_planes(out, raw_ref, first, count, rows, depth):
    stride = 6 * rows * depth

    def body(c, _):
        for z in out:
            for q in range(6):
                start = first * stride + q * rows * depth + c * depth + z
                out[z][c, q, first : first + count, :] = raw_ref[pl.ds(start, count, stride=stride), :]
        return 0

    lax.fori_loop(0, rows, body, 0)


def planes_kernel(depth, pieces, pick_ref, far_ref, *refs):
    *out_refs, raw_ref, sems = refs
    out = plane_refs(out_refs, pieces)
    rows, _, vecs, _ = out[pieces[0][0]].shape
    size = raw_ref.shape[0]
    parts = 2
    copies = []
    for k in range(parts):
        block = pl.ds(k * (size // parts), size // parts)
        source = pl.ds(pick_ref[0] * size + k * (size // parts), size // parts)
        copies.append(pltpu.make_async_copy(far_ref.at[source], raw_ref.at[block], sems.at[k]))
        copies[-1].start()
    for k in range(parts):
        copies[k].wait()
        take_planes(out, raw_ref, k * (vecs // parts), vecs // parts, rows, depth)


def link_kernel(depth, half, pick_ref, far_ref, came_ref, table_ref, behind_ref, top_ref, sem):
    core = pick_ref[1]
    copy = pltpu.make_async_copy(far_ref.at[pick_ref[2]], table_ref.at[core], sem)
    copy.start()
    table_ref[1 - core] = came_ref[...]
    copy.wait()
    count = half * depth
    lane = lane_index((count, LANES))

    def shift(d, _):
        for h in range(2):
            behind_ref[h, d] = behind_x(table_ref[h, d], lane)
        low, high = table_ref[0, 18 + d], table_ref[1, 18 + d]
        for h, here, wrap in ((0, low, high), (1, high, low)):
            before = wrap[count - depth :]
            if half > 1:
                before = jnp.concatenate([before, here[: count - depth]], axis=0)
            behind_ref[h, 18 + d] = behind_y(here, before, lane)
        for h in range(2):
            top_ref[d, h * half : (h + 1) * half, :] = table_ref[h, 36 + d, pl.ds(depth - 1, half, stride=depth), :]
        return 0

    lax.fori_loop(0, 18, shift, 0)


def multiply_into(total, field, link, adjoint):
    for col in range(3):
        re, im = field(col), field(3 + col)
        for row in range(3):
            entry = col * 3 + row if adjoint else row * 3 + col
            a, b = link(entry), link(9 + entry)
            if adjoint:
                total[row] = total[row] + a * re + b * im
                total[3 + row] = total[3 + row] + a * im - b * re
            else:
                total[row] = total[row] + a * re - b * im
                total[3 + row] = total[3 + row] + a * im + b * re


def rows_of(ref, c, z, depth, first, vecs):
    half = ref.shape[2] // depth
    row = lax.rem(c, half) * depth + z

    def link(k):
        return jnp.broadcast_to(ref[c // half, first + k, pl.ds(row, 1), :], (vecs, LANES))

    return link


def edge_rows(ref, c, vecs):
    def link(k):
        return jnp.broadcast_to(ref[k, pl.ds(c, 1), :], (vecs, LANES))

    return link


def forward_hops(total, cur, up, table, c, z, depth, lane):
    rows, _, vecs, _ = cur.shape
    after = lax.rem(c + 1, rows)
    multiply_into(total, lambda q: ahead_x(cur[c, q], lane), rows_of(table, c, z, depth, 0, vecs), False)
    multiply_into(
        total, lambda q: ahead_y(cur[c, q], cur[after, q], lane), rows_of(table, c, z, depth, 18, vecs), False
    )
    if up is not None:
        multiply_into(total, lambda q: up[c, q], rows_of(table, c, z, depth, 36, vecs), False)


def backward_hops(total, cur, down, table, behind, c, z, depth, lane):
    rows, _, vecs, _ = cur.shape
    before = lax.rem(c + rows - 1, rows)
    multiply_into(total, lambda q: behind_x(cur[c, q], lane), rows_of(behind, c, z, depth, 0, vecs), True)
    multiply_into(
        total, lambda q: behind_y(cur[c, q], cur[before, q], lane), rows_of(behind, c, z, depth, 18, vecs), True
    )
    if down is not None:
        multiply_into(total, lambda q: down[c, q], rows_of(table, c, z - 1, depth, 36, vecs), True)


def part_kernel(depth, pieces, todo, factor, first, table_ref, behind_ref, *refs):
    refs = list(refs)
    cur = plane_refs([refs.pop(0) for _ in pieces], pieces)
    done = [pieces[k] for k in todo]
    old = None if first else plane_refs([refs.pop(0) for _ in todo], done)
    out = plane_refs(refs, done)
    rows, _, vecs, _ = cur[0].shape
    lane = lane_index((vecs, LANES))
    for z in out:

        def body(c, _, z=z):
            total = [cur[z][c, q] for q in range(6)]
            forward_hops(total, cur[z], cur.get(z + 1), table_ref, c, z, depth, lane)
            backward_hops(total, cur[z], cur.get(z - 1), table_ref, behind_ref, c, z, depth, lane)
            for q in range(6):
                value = total[q] * factor
                out[z][c, q] = value if first else value - old[z][c, q]
            return 0

        lax.fori_loop(0, rows, body, 0)


def close_kernel(factor, behind, *refs):
    part_ref, out_ref = refs[-2].at[0], refs[-1].at[0]
    rows, _, vecs, _ = out_ref.shape

    def body(c, _):
        total = [jnp.zeros((vecs, LANES), F32) for _ in range(6)]
        for k, back in enumerate(behind):
            links_ref, halo_ref = refs[2 * k : 2 * k + 2]
            multiply_into(total, lambda q: halo_ref[0, c, q], edge_rows(links_ref, c, vecs), back)
        for q in range(6):
            out_ref[c, q] = part_ref[c, q] + total[q] * factor
        return 0

    lax.fori_loop(0, rows, body, 0)


def halves(x):
    high = x.astype(BF16)
    return high, (x - high.astype(F32)).astype(BF16)


def high_low(tiles):
    pairs = [halves(jnp.concatenate(tiles[k : k + 3], axis=1)) for k in (0, 3)]
    return [pairs[0][0], pairs[1][0], pairs[0][1], pairs[1][1]]


def products(acc_ref, rows, own, sides):
    def body(pair, _):
        stacks = [[], []]
        for c in (2 * pair, 2 * pair + 1):
            for stack, tiles in zip(stacks, sides(c)):
                stack.append(jnp.concatenate(high_low(tiles), axis=0))
        left, right = [jnp.concatenate(s, axis=1) for s in stacks]
        right = jnp.concatenate([left if own else jnp.zeros_like(left), right], axis=0)
        acc_ref[...] += lax.dot_general(left, right, (((1,), (1,)), ((), ())), preferred_element_type=F32)
        return 0

    lax.fori_loop(0, rows // 2, body, 0)


def packed_product(acc, n):
    acc = acc[0 : 2 * n] + acc[2 * n : 4 * n]
    acc = acc + pltpu.roll(acc, LANES - 2 * n, 1)
    re, im = acc[0:n], acc[n : 2 * n]
    real = re + pltpu.roll(im, LANES - n, 1)
    imag = re - pltpu.roll(im, n, 1)
    return jnp.where(lane_index((n, LANES)) % (2 * n) < n, real, imag)


def gram_kernel(depth, pieces, tasks, more, table_ref, *refs):
    refs = list(refs)
    acc_ref, out_ref = refs.pop(), refs.pop()
    sofar_ref = refs.pop() if more else None
    cur = plane_refs(refs, pieces)
    rows, _, vecs, _ = cur[tasks[0][0]].shape
    lane = lane_index((vecs, LANES))
    acc_ref[...] = jnp.zeros_like(acc_ref)
    for z, own, depth_hop in tasks:

        def sides(c, z=z, own=own, depth_hop=depth_hop):
            total = [jnp.zeros((vecs, LANES), F32) for _ in range(6)]
            if own:
                forward_hops(total, cur[z], cur[z + 1] if depth_hop else None, table_ref, c, z, depth, lane)
            else:
                up = cur[z + 1]
                multiply_into(total, lambda q: up[c, q], rows_of(table_ref, c, z, depth, 36, vecs), False)
            return [cur[z][c, q] for q in range(6)], total

        products(acc_ref, rows, own, sides)
    part = packed_product(acc_ref[...], vecs)
    out_ref[...] = part + sofar_ref[...] if more else part


def last_hop_kernel(links_ref, top_ref, above_ref, sofar_ref, out_ref, acc_ref):
    rows, _, vecs, _ = top_ref.shape[1:]
    acc_ref[...] = jnp.zeros_like(acc_ref)

    def sides(c):
        total = [jnp.zeros((vecs, LANES), F32) for _ in range(6)]
        multiply_into(total, lambda q: above_ref[0, c, q], edge_rows(links_ref, c, vecs), False)
        return [top_ref[0, c, q] for q in range(6)], total

    products(acc_ref, rows, False, sides)
    out_ref[...] = packed_product(acc_ref[...], vecs) + sofar_ref[...]


def norms_of(packed):
    n = packed.shape[0]
    diag = lane_index((n, LANES)) == lax.broadcasted_iota(jnp.int32, (n, LANES), 0)
    return jnp.where(diag, packed, 0.0)


def scatter_kernel(depth, planes, piece_ref, *refs):
    out_ref = refs[-1]
    rows, _, vecs, _ = piece_ref.shape[1:]
    stride = 6 * rows * depth

    def body(c, _):
        for k, z in enumerate(planes):
            for q in range(6):
                start = q * rows * depth + c * depth + z
                out_ref[pl.ds(start, vecs, stride=stride), :] = piece_ref[k, c, q]
        return 0

    lax.fori_loop(0, rows, body, 0)


def final_kernel(steps, slot_ref, *refs):
    out_ref, grams_ref, scale_ref = refs[-3:]
    step = pl.program_id(0)
    for k in range(2):
        term0, term1, field_ref = refs[3 * k : 3 * k + 3]
        n = term0.shape[0]
        slot = slot_ref[0] if k == 0 else 1 - slot_ref[0]

        def normalised(term0=term0, term1=term1):
            packed = term0[...] + term1[...]
            norm = norms_of(packed)
            return packed, norm, lax.rsqrt(jnp.sum(norm, axis=1, keepdims=True))

        @pl.when(step == k * steps)
        def _(n=n, normalised=normalised):
            scale_ref[...] = jnp.broadcast_to(normalised()[2], (n, LANES))

        @pl.when((step >= k * steps) & (step < (k + 1) * steps))
        def _(k=k, n=n, field_ref=field_ref):
            size = field_ref.shape[0] // n
            each = n // steps

            def body(i, _):
                vec = (step - k * steps) * each + i
                source = pl.ds(pl.multiple_of(vec * size, 8), size)
                target = pl.ds(pl.multiple_of(i * size, 8), size)
                out_ref[target, :] = field_ref[source, :] * scale_ref[pl.ds(vec, 1), :]
                return 0

            lax.fori_loop(0, each, body, 0)

        @pl.when(step == k * steps)
        def _(n=n, slot=slot, normalised=normalised):
            packed, norm, down = normalised()
            across = lax.rsqrt(jnp.sum(norm, axis=0, keepdims=True)[:, 0:n])
            scale = down * across
            over_re, over_im = packed[:, 0:n], packed[:, n : 2 * n]
            hop_re, hop_im = packed[:, 4 * n : 5 * n], packed[:, 5 * n : 6 * n]
            grams_ref[slot, 0, 0] = over_re * scale
            grams_ref[slot, 0, 1] = over_im * scale
            grams_ref[slot, 1, 0] = (6.0 * over_re - (hop_re + hop_re.T)) * scale
            grams_ref[slot, 1, 1] = (6.0 * over_im - (hop_im - hop_im.T)) * scale


def shifted(x, axis, by):
    n = lax.axis_size(axis)
    return lax.ppermute(x, axis, [(i, (i + by) % n) for i in range(n)])


def flipped(x, axis, bit):
    return lax.ppermute(x, axis, [(i, i ^ bit) for i in range(lax.axis_size(axis))])


def summed(x):
    size = lax.axis_size("sa")
    count = size.bit_length() - 1
    assert size == 1 << count

    def across(x, cfg, bits):
        pairs = range(lax.axis_size("cfg") * size)
        return lax.ppermute(x, ("cfg", "sa"), [(i, i ^ (cfg * size + bits)) for i in pairs])

    bit = 1
    for _ in range((count - 1) // 2):
        x = x + flipped(x, "sa", bit) + flipped(x, "sa", 2 * bit) + flipped(x, "sa", 3 * bit)
        bit *= 4
    if count % 2 == 0:
        x = x + flipped(x, "sa", bit)
        bit *= 2
    return (x, flipped(x, "sa", bit)), (across(x, 1, 0), across(x, 1, bit))


def on_device(links, vectors):
    slices, vecs, _, _, depth, plane = vectors.shape
    rows = plane // LANES
    assert slices == 2 and lax.axis_size("cfg") % 2 == 0 and lax.axis_size("ta") == 2
    pieces = pieces_of(depth)
    ends = [0] if len(pieces) == 1 else [0, len(pieces) - 1]
    inner = [k for k in range(len(pieces)) if k not in ends]
    core = lax.axis_index("ta")
    mine = lax.axis_index("cfg") % 2
    pick = jnp.stack([mine, core, 2 * core + mine]).astype(jnp.int32)
    field = [shape_of(len(p), rows, 6, vecs, LANES) for p in pieces]
    work = 1000 * LANES * vecs * rows
    many = vecs * 6 * rows * depth
    half = rows // 2
    sem = pltpu.SemaphoreType.DMA

    view = pltpu.with_memory_space_constraint(to_rows(vectors), pltpu.HBM)

    def taken(todo):
        return call(
            functools.partial(planes_kernel, depth, [pieces[k] for k in todo]), [field[k] for k in todo],
            view, pick=pick, far=(0,), scratch=[pltpu.VMEM((many, LANES), F32), sem((2,))], ops=1e5,
        )

    start = [None] * len(pieces)
    for k, x in zip(ends, taken(ends)):
        start[k] = x
    flat = links.reshape((links.shape[0], 54) + links.shape[-2:])
    given = lax.dynamic_index_in_dim(flat, 2 * (1 - core) + mine, 0, keepdims=False)
    came = flipped(given, "ta", 1)
    if inner:
        for k, x in zip(inner, taken(inner)):
            start[k] = x
    table, behind, top_links = call(
        functools.partial(link_kernel, depth, half),
        [shape_of(2, 54, half * depth, LANES), shape_of(2, 36, half * depth, LANES), shape_of(18, rows, LANES)],
        pltpu.with_memory_space_constraint(to_rows(links).reshape(-1, 54, half * depth, LANES), pltpu.HBM),
        to_rows(came).reshape(54, half * depth, LANES),
        pick=pick, far=(0,), scratch=[sem], ops=1e6,
    )
    prior = shifted(top_links, "sa", 1)

    def advance(cur, old):
        factor = -(1.0 if old is None else 2.0) / SCALE
        low = shifted(cur[-1], "sa", 1)
        high = shifted(cur[0], "sa", -1)
        new = [None] * len(pieces)
        for todo in (inner, ends):
            if todo:
                got = call(
                    functools.partial(part_kernel, depth, pieces, todo, factor, old is None),
                    [field[k] for k in todo], table, behind, *cur, *([] if old is None else [old[k] for k in todo]),
                    ops=work * sum(len(pieces[k]) for k in todo),
                )
                for k, x in zip(todo, got):
                    new[k] = x
        sides = [(0, True, prior, low), (len(pieces) - 1, False, top_links, high)]
        for k in ends:
            used = [side for side in sides if side[0] == k]
            operands = [x for side in used for x in side[2:]]
            (new[k],) = call(
                functools.partial(close_kernel, factor, [side[1] for side in used]),
                [field[k]], *operands, new[k], ops=work / 6,
            )
        return new

    packed = shape_of(vecs, LANES)
    acc = [pltpu.VMEM((4 * vecs, 8 * vecs), F32)]

    def swapped(x):
        return flipped(x, "cfg", 1)

    def grams_of(planes, tasks, sofar):
        return call(
            functools.partial(gram_kernel, depth, [pieces[k] for k in planes], tasks, sofar is not None),
            packed, table, *[three[k] for k in planes], *([] if sofar is None else [sofar]),
            scratch=acc, ops=work * len(tasks) / 2,
        )

    one = advance(start, None)
    two = advance(one, start)
    three = advance(two, one)

    sofar = None
    if inner:
        middle = pieces[1]
        sofar = grams_of(inner, [(z, True, z + 1 in middle) for z in middle], None)
    above = shifted(three[0], "sa", -1)
    tasks = [(z, True, z + 1 < depth) for z in sorted({0, depth - 1})]
    if inner:
        tasks.append((depth - 2, False, True))
    sofar = grams_of(range(len(pieces)), tasks, sofar)
    sofar = call(
        last_hop_kernel, packed, top_links, three[-1], above, sofar,
        scratch=acc, ops=work / 4,
    )
    sum_mine, sum_other = summed(sofar)
    other = [swapped(x) for x in three]

    def scattered(planes):
        out = None
        for k in inner + ends:
            out = call(
                functools.partial(scatter_kernel, depth, pieces[k]), shape_of(many, LANES),
                planes[k], *([] if out is None else [out]), alias={} if out is None else {1: 0}, ops=1e5,
            )
        return out

    steps = 1
    assert vecs % steps == 0

    def target(step, pick):
        slot = jnp.where(step < steps, pick[0], 1 - pick[0])
        return slot * steps + lax.rem(step, steps), 0

    out, grams = call(
        functools.partial(final_kernel, steps), [shape_of(2 * many, LANES), shape_of(2, 2, 2, vecs, vecs)],
        *sum_mine, scattered(three), *sum_other, scattered(other),
        pick=pick, place=((many // steps, LANES), target), grid=2 * steps, ops=1e6,
        scratch=[pltpu.VMEM((vecs, LANES), F32)],
    )
    return from_rows(out, vectors.shape), grams


def solution(mesh):
    in_specs = (P(None, None, None, None, None, "sa", "ta"), P("ta", None, None, None, "sa", None))
    out_specs = (
        P(("cfg", "ta"), None, None, None, "sa", None),
        P(("cfg", "ta"), None, None, None, None),
    )
    return jax.shard_map(on_device, mesh=mesh, in_specs=in_specs, out_specs=out_specs, check_vma=False)
```

```python
import functools

import jax
import jax.numpy as jnp
from jax import lax
from jax.experimental import pallas as pl
from jax.experimental.pallas import tpu as pltpu
from jax.sharding import PartitionSpec as P


LX = 32
LANES = 128
SCALE = 5.5
F32 = jnp.float32
BF16 = jnp.bfloat16
VMEM = pl.BlockSpec(memory_space=pltpu.VMEM)
FAR = pl.BlockSpec(memory_space=pltpu.HBM)
GRANT = 16 * 2**20


def shape_of(*dims, dtype=F32):
    return jax.ShapeDtypeStruct(dims, dtype)


def call(kernel, outs, *args, ops=1e6, scratch=(), pick=None, far=(), far_out=(), alias=None):
    size = sum(a.size * 4 for a in args) + sum(4 * o.size for o in jax.tree.leaves(outs))
    several = isinstance(outs, (list, tuple))
    params = dict(
        out_shape=outs,
        compiler_params=pltpu.CompilerParams(vmem_limit_bytes=GRANT),
        cost_estimate=pl.CostEstimate(flops=int(ops), bytes_accessed=int(size), transcendentals=0),
        input_output_aliases=alias or {},
    )
    in_specs = [FAR if k in far else VMEM for k in range(len(args))]
    out_specs = [VMEM] * len(outs) if several else VMEM
    if pick is None:
        return pl.pallas_call(
            kernel, in_specs=in_specs, out_specs=out_specs, scratch_shapes=scratch, **params
        )(*args)
    out_specs = [FAR if k in far_out else VMEM for k in range(len(outs))]
    spec = pltpu.PrefetchScalarGridSpec(
        num_scalar_prefetch=1, grid=(1,), in_specs=in_specs, out_specs=out_specs, scratch_shapes=scratch
    )
    return pl.pallas_call(kernel, grid_spec=spec, **params)(pick, *args)


def to_rows(x):
    depth, plane = x.shape[-2:]
    x = x.reshape(-1, depth, plane // LANES, LANES)
    return jnp.swapaxes(x, 1, 2).reshape(-1, LANES)


def from_rows(x, shape):
    depth, plane = shape[-2:]
    x = x.reshape(-1, plane // LANES, depth, LANES)
    return jnp.swapaxes(x, 1, 2).reshape(shape)


def pieces_of(depth):
    if depth == 1:
        return [[0]]
    if depth == 2:
        return [[0], [1]]
    return [[0], list(range(1, depth - 1)), [depth - 1]]


def plane_refs(refs, pieces):
    return {z: ref.at[k] for ref, planes in zip(refs, pieces) for k, z in enumerate(planes)}


def lane_index(shape):
    return lax.broadcasted_iota(jnp.int32, shape, len(shape) - 1)


def ahead_x(v, lane):
    wrap = (lane % LX) == LX - 1
    return jnp.where(wrap, pltpu.roll(v, LX - 1, v.ndim - 1), pltpu.roll(v, LANES - 1, v.ndim - 1))


def behind_x(v, lane):
    wrap = (lane % LX) == 0
    return jnp.where(wrap, pltpu.roll(v, LANES - LX + 1, v.ndim - 1), pltpu.roll(v, 1, v.ndim - 1))


def ahead_y(here, after, lane):
    ax = here.ndim - 1
    return jnp.where(lane < LANES - LX, pltpu.roll(here, LANES - LX, ax), pltpu.roll(after, LANES - LX, ax))


def behind_y(here, before, lane):
    ax = here.ndim - 1
    return jnp.where(lane < LX, pltpu.roll(before, LX, ax), pltpu.roll(here, LX, ax))


def take_planes(out, raw_ref, first, count, rows, depth):
    stride = 6 * rows * depth

    def body(c, _):
        for z in out:
            for q in range(6):
                start = first * stride + q * rows * depth + c * depth + z
                out[z][c, q, first : first + count, :] = raw_ref[pl.ds(start, count, stride=stride), :]
        return 0

    lax.fori_loop(0, rows, body, 0)


def planes_kernel(depth, pieces, pick_ref, far_ref, *refs):
    *out_refs, raw_ref, sems = refs
    out = plane_refs(out_refs, pieces)
    rows, _, vecs, _ = out[pieces[0][0]].shape
    size = raw_ref.shape[0]
    parts = 2
    copies = []
    for k in range(parts):
        block = pl.ds(k * (size // parts), size // parts)
        source = pl.ds(pick_ref[0] * size + k * (size // parts), size // parts)
        copies.append(pltpu.make_async_copy(far_ref.at[source], raw_ref.at[block], sems.at[k]))
        copies[-1].start()
    for k in range(parts):
        copies[k].wait()
        take_planes(out, raw_ref, k * (vecs // parts), vecs // parts, rows, depth)


def link_kernel(depth, half, pick_ref, far_ref, came_ref, table_ref, behind_ref, top_ref, sem):
    core = pick_ref[1]
    copy = pltpu.make_async_copy(far_ref.at[pick_ref[2]], table_ref.at[core], sem)
    copy.start()
    table_ref[1 - core] = came_ref[...]
    copy.wait()
    count = half * depth
    lane = lane_index((count, LANES))

    def shift(d, _):
        for h in range(2):
            behind_ref[h, d] = behind_x(table_ref[h, d], lane)
        low, high = table_ref[0, 18 + d], table_ref[1, 18 + d]
        for h, here, wrap in ((0, low, high), (1, high, low)):
            before = wrap[count - depth :]
            if half > 1:
                before = jnp.concatenate([before, here[: count - depth]], axis=0)
            behind_ref[h, 18 + d] = behind_y(here, before, lane)
        for h in range(2):
            top_ref[d, h * half : (h + 1) * half, :] = table_ref[h, 36 + d, pl.ds(depth - 1, half, stride=depth), :]
        return 0

    lax.fori_loop(0, 18, shift, 0)


def multiply_into(total, field, link, adjoint):
    for col in range(3):
        re, im = field(col), field(3 + col)
        for row in range(3):
            entry = col * 3 + row if adjoint else row * 3 + col
            a, b = link(entry), link(9 + entry)
            if adjoint:
                total[row] = total[row] + a * re + b * im
                total[3 + row] = total[3 + row] + a * im - b * re
            else:
                total[row] = total[row] + a * re - b * im
                total[3 + row] = total[3 + row] + a * im + b * re


def rows_of(ref, c, z, depth, first, vecs):
    half = ref.shape[2] // depth
    row = lax.rem(c, half) * depth + z

    def link(k):
        return jnp.broadcast_to(ref[c // half, first + k, pl.ds(row, 1), :], (vecs, LANES))

    return link


def edge_rows(ref, c, vecs):
    def link(k):
        return jnp.broadcast_to(ref[k, pl.ds(c, 1), :], (vecs, LANES))

    return link


def forward_hops(total, cur, up, table, c, z, depth, lane):
    rows, _, vecs, _ = cur.shape
    after = lax.rem(c + 1, rows)
    multiply_into(total, lambda q: ahead_x(cur[c, q], lane), rows_of(table, c, z, depth, 0, vecs), False)
    multiply_into(
        total, lambda q: ahead_y(cur[c, q], cur[after, q], lane), rows_of(table, c, z, depth, 18, vecs), False
    )
    if up is not None:
        multiply_into(total, lambda q: up[c, q], rows_of(table, c, z, depth, 36, vecs), False)


def backward_hops(total, cur, down, table, behind, c, z, depth, lane):
    rows, _, vecs, _ = cur.shape
    before = lax.rem(c + rows - 1, rows)
    multiply_into(total, lambda q: behind_x(cur[c, q], lane), rows_of(behind, c, z, depth, 0, vecs), True)
    multiply_into(
        total, lambda q: behind_y(cur[c, q], cur[before, q], lane), rows_of(behind, c, z, depth, 18, vecs), True
    )
    if down is not None:
        multiply_into(total, lambda q: down[c, q], rows_of(table, c, z - 1, depth, 36, vecs), True)


def part_kernel(depth, pieces, todo, factor, first, table_ref, behind_ref, *refs):
    refs = list(refs)
    cur = plane_refs([refs.pop(0) for _ in pieces], pieces)
    done = [pieces[k] for k in todo]
    old = None if first else plane_refs([refs.pop(0) for _ in todo], done)
    out = plane_refs(refs, done)
    rows, _, vecs, _ = cur[0].shape
    lane = lane_index((vecs, LANES))
    for z in out:

        def body(c, _, z=z):
            total = [cur[z][c, q] for q in range(6)]
            forward_hops(total, cur[z], cur.get(z + 1), table_ref, c, z, depth, lane)
            backward_hops(total, cur[z], cur.get(z - 1), table_ref, behind_ref, c, z, depth, lane)
            for q in range(6):
                value = total[q] * factor
                out[z][c, q] = value if first else value - old[z][c, q]
            return 0

        lax.fori_loop(0, rows, body, 0)


def close_kernel(factor, behind, *refs):
    part_ref, out_ref = refs[-2].at[0], refs[-1].at[0]
    rows, _, vecs, _ = out_ref.shape

    def body(c, _):
        total = [jnp.zeros((vecs, LANES), F32) for _ in range(6)]
        for k, back in enumerate(behind):
            links_ref, halo_ref = refs[2 * k : 2 * k + 2]
            multiply_into(total, lambda q: halo_ref[0, c, q], edge_rows(links_ref, c, vecs), back)
        for q in range(6):
            out_ref[c, q] = part_ref[c, q] + total[q] * factor
        return 0

    lax.fori_loop(0, rows, body, 0)


def halves(x):
    high = x.astype(BF16)
    return high, (x - high.astype(F32)).astype(BF16)


def high_low(tiles):
    pairs = [halves(jnp.concatenate(tiles[k : k + 3], axis=1)) for k in (0, 3)]
    return [pairs[0][0], pairs[1][0], pairs[0][1], pairs[1][1]]


def products(acc_ref, rows, own, sides):
    def body(pair, _):
        stacks = [[], []]
        for c in (2 * pair, 2 * pair + 1):
            for stack, tiles in zip(stacks, sides(c)):
                stack.append(jnp.concatenate(high_low(tiles), axis=0))
        left, right = [jnp.concatenate(s, axis=1) for s in stacks]
        right = jnp.concatenate([left if own else jnp.zeros_like(left), right], axis=0)
        acc_ref[...] += lax.dot_general(left, right, (((1,), (1,)), ((), ())), preferred_element_type=F32)
        return 0

    lax.fori_loop(0, rows // 2, body, 0)


def packed_product(acc, n):
    acc = acc[0 : 2 * n] + acc[2 * n : 4 * n]
    acc = acc + pltpu.roll(acc, LANES - 2 * n, 1)
    re, im = acc[0:n], acc[n : 2 * n]
    real = re + pltpu.roll(im, LANES - n, 1)
    imag = re - pltpu.roll(im, n, 1)
    return jnp.where(lane_index((n, LANES)) % (2 * n) < n, real, imag)


def gram_kernel(depth, pieces, tasks, more, table_ref, *refs):
    refs = list(refs)
    acc_ref, out_ref = refs.pop(), refs.pop()
    sofar_ref = refs.pop() if more else None
    cur = plane_refs(refs, pieces)
    rows, _, vecs, _ = cur[tasks[0][0]].shape
    lane = lane_index((vecs, LANES))
    acc_ref[...] = jnp.zeros_like(acc_ref)
    for z, own, depth_hop in tasks:

        def sides(c, z=z, own=own, depth_hop=depth_hop):
            total = [jnp.zeros((vecs, LANES), F32) for _ in range(6)]
            if own:
                forward_hops(total, cur[z], cur[z + 1] if depth_hop else None, table_ref, c, z, depth, lane)
            else:
                up = cur[z + 1]
                multiply_into(total, lambda q: up[c, q], rows_of(table_ref, c, z, depth, 36, vecs), False)
            return [cur[z][c, q] for q in range(6)], total

        products(acc_ref, rows, own, sides)
    part = packed_product(acc_ref[...], vecs)
    out_ref[...] = part + sofar_ref[...] if more else part


def last_hop_kernel(links_ref, top_ref, above_ref, sofar_ref, out_ref, acc_ref):
    rows, _, vecs, _ = top_ref.shape[1:]
    acc_ref[...] = jnp.zeros_like(acc_ref)

    def sides(c):
        total = [jnp.zeros((vecs, LANES), F32) for _ in range(6)]
        multiply_into(total, lambda q: above_ref[0, c, q], edge_rows(links_ref, c, vecs), False)
        return [top_ref[0, c, q] for q in range(6)], total

    products(acc_ref, rows, False, sides)
    out_ref[...] = packed_product(acc_ref[...], vecs) + sofar_ref[...]


def norms_of(packed):
    n = packed.shape[0]
    diag = lane_index((n, LANES)) == lax.broadcasted_iota(jnp.int32, (n, LANES), 0)
    return jnp.where(diag, packed, 0.0)


def scatter_kernel(depth, planes, piece_ref, *refs):
    out_ref = refs[-1]
    rows, _, vecs, _ = piece_ref.shape[1:]
    stride = 6 * rows * depth

    def body(c, _):
        for k, z in enumerate(planes):
            for q in range(6):
                start = q * rows * depth + c * depth + z
                out_ref[pl.ds(start, vecs, stride=stride), :] = piece_ref[k, c, q]
        return 0

    lax.fori_loop(0, rows, body, 0)


def final_kernel(chunks, slot_ref, *refs):
    far_ref, grams_ref, scale_ref, ready_ref, sems = refs[-5:]
    copies = []
    for k in range(2):
        term0, term1, field_ref = refs[3 * k : 3 * k + 3]
        n = term0.shape[0]
        size = field_ref.shape[0] // n
        each = n // chunks
        slot = slot_ref[0] if k == 0 else 1 - slot_ref[0]
        packed = term0[...] + term1[...]
        norm = norms_of(packed)
        down = lax.rsqrt(jnp.sum(norm, axis=1, keepdims=True))
        scale_ref[...] = jnp.broadcast_to(down, (n, LANES))
        for j in range(chunks):

            def body(i, _, field_ref=field_ref, j=j, k=k):
                vec = j * each + i
                block = pl.ds(pl.multiple_of(vec * size, 8), size)
                ready_ref[k, block, :] = field_ref[block, :] * scale_ref[pl.ds(vec, 1), :]
                return 0

            lax.fori_loop(0, each, body, 0)
            part = pl.ds(j * each * size, each * size)
            target = pl.ds(slot * (n * size) + j * each * size, each * size)
            copies.append(pltpu.make_async_copy(ready_ref.at[k, part], far_ref.at[target], sems.at[k, j]))
            copies[-1].start()
        across = lax.rsqrt(jnp.sum(norm, axis=0, keepdims=True)[:, 0:n])
        scale = down * across
        over_re, over_im = packed[:, 0:n], packed[:, n : 2 * n]
        hop_re, hop_im = packed[:, 4 * n : 5 * n], packed[:, 5 * n : 6 * n]
        grams_ref[slot, 0, 0] = over_re * scale
        grams_ref[slot, 0, 1] = over_im * scale
        grams_ref[slot, 1, 0] = (6.0 * over_re - (hop_re + hop_re.T)) * scale
        grams_ref[slot, 1, 1] = (6.0 * over_im - (hop_im - hop_im.T)) * scale
    for copy in copies:
        copy.wait()


def shifted(x, axis, by):
    n = lax.axis_size(axis)
    return lax.ppermute(x, axis, [(i, (i + by) % n) for i in range(n)])


def flipped(x, axis, bit):
    return lax.ppermute(x, axis, [(i, i ^ bit) for i in range(lax.axis_size(axis))])


def summed(x):
    size = lax.axis_size("sa")
    count = size.bit_length() - 1
    assert size == 1 << count

    def across(x, cfg, bits):
        pairs = range(lax.axis_size("cfg") * size)
        return lax.ppermute(x, ("cfg", "sa"), [(i, i ^ (cfg * size + bits)) for i in pairs])

    bit = 1
    for _ in range((count - 1) // 2):
        x = x + flipped(x, "sa", bit) + flipped(x, "sa", 2 * bit) + flipped(x, "sa", 3 * bit)
        bit *= 4
    if count % 2 == 0:
        x = x + flipped(x, "sa", bit)
        bit *= 2
    return (x, flipped(x, "sa", bit)), (across(x, 1, 0), across(x, 1, bit))


def on_device(links, vectors):
    slices, vecs, _, _, depth, plane = vectors.shape
    rows = plane // LANES
    assert slices == 2 and lax.axis_size("cfg") % 2 == 0 and lax.axis_size("ta") == 2
    pieces = pieces_of(depth)
    ends = [0] if len(pieces) == 1 else [0, len(pieces) - 1]
    inner = [k for k in range(len(pieces)) if k not in ends]
    core = lax.axis_index("ta")
    mine = lax.axis_index("cfg") % 2
    pick = jnp.stack([mine, core, 2 * core + mine]).astype(jnp.int32)
    field = [shape_of(len(p), rows, 6, vecs, LANES) for p in pieces]
    work = 1000 * LANES * vecs * rows
    many = vecs * 6 * rows * depth
    half = rows // 2
    sem = pltpu.SemaphoreType.DMA

    view = pltpu.with_memory_space_constraint(to_rows(vectors), pltpu.HBM)

    def taken(todo):
        return call(
            functools.partial(planes_kernel, depth, [pieces[k] for k in todo]), [field[k] for k in todo],
            view, pick=pick, far=(0,), scratch=[pltpu.VMEM((many, LANES), F32), sem((2,))], ops=1e5,
        )

    first, rest = ends[-1:], [k for k in range(len(pieces)) if k != ends[-1]]
    start = [None] * len(pieces)
    for k, x in zip(first, taken(first)):
        start[k] = x
    flat = links.reshape((links.shape[0], 54) + links.shape[-2:])
    given = lax.dynamic_index_in_dim(flat, 2 * (1 - core) + mine, 0, keepdims=False)
    came = flipped(given, "ta", 1)
    if rest:
        for k, x in zip(rest, taken(rest)):
            start[k] = x
    table, behind, top_links = call(
        functools.partial(link_kernel, depth, half),
        [shape_of(2, 54, half * depth, LANES), shape_of(2, 36, half * depth, LANES), shape_of(18, rows, LANES)],
        pltpu.with_memory_space_constraint(to_rows(links).reshape(-1, 54, half * depth, LANES), pltpu.HBM),
        to_rows(came).reshape(54, half * depth, LANES),
        pick=pick, far=(0,), scratch=[sem], ops=1e6,
    )
    prior = shifted(top_links, "sa", 1)

    def advance(cur, old):
        factor = -(1.0 if old is None else 2.0) / SCALE
        low = shifted(cur[-1], "sa", 1)
        high = shifted(cur[0], "sa", -1)
        new = [None] * len(pieces)
        for todo in (inner, ends):
            if todo:
                got = call(
                    functools.partial(part_kernel, depth, pieces, todo, factor, old is None),
                    [field[k] for k in todo], table, behind, *cur, *([] if old is None else [old[k] for k in todo]),
                    ops=work * sum(len(pieces[k]) for k in todo),
                )
                for k, x in zip(todo, got):
                    new[k] = x
        sides = [(0, True, prior, low), (len(pieces) - 1, False, top_links, high)]
        for k in ends:
            used = [side for side in sides if side[0] == k]
            operands = [x for side in used for x in side[2:]]
            (new[k],) = call(
                functools.partial(close_kernel, factor, [side[1] for side in used]),
                [field[k]], *operands, new[k], ops=work / 6,
            )
        return new

    packed = shape_of(vecs, LANES)
    acc = [pltpu.VMEM((4 * vecs, 8 * vecs), F32)]

    def swapped(x):
        return flipped(x, "cfg", 1)

    def grams_of(planes, tasks, sofar):
        return call(
            functools.partial(gram_kernel, depth, [pieces[k] for k in planes], tasks, sofar is not None),
            packed, table, *[three[k] for k in planes], *([] if sofar is None else [sofar]),
            scratch=acc, ops=work * len(tasks) / 2,
        )

    one = advance(start, None)
    two = advance(one, start)
    three = advance(two, one)

    sofar = None
    if inner:
        middle = pieces[1]
        sofar = grams_of(inner, [(z, True, z + 1 in middle) for z in middle], None)
    above = shifted(three[0], "sa", -1)
    if len(ends) == 2:
        sofar = grams_of([0] + inner[:1], [(0, True, bool(inner))], sofar)
    tasks = [(depth - 1, True, False)]
    if depth > 1:
        tasks.append((depth - 2, False, True))
    sofar = grams_of(range(len(pieces)), tasks, sofar)
    sofar = call(
        last_hop_kernel, packed, top_links, three[-1], above, sofar,
        scratch=acc, ops=work / 4,
    )
    sum_mine, sum_other = summed(sofar)
    other = [swapped(x) for x in three]

    def scattered(planes):
        out = None
        for k in inner + ends:
            out = call(
                functools.partial(scatter_kernel, depth, pieces[k]), shape_of(many, LANES),
                planes[k], *([] if out is None else [out]), alias={} if out is None else {1: 0}, ops=1e5,
            )
        return out

    chunks = 4
    assert vecs % chunks == 0
    out, grams = call(
        functools.partial(final_kernel, chunks), [shape_of(2 * many, LANES), shape_of(2, 2, 2, vecs, vecs)],
        *sum_mine, scattered(three), *sum_other, scattered(other),
        pick=pick, far_out=(0,), ops=1e6,
        scratch=[pltpu.VMEM((vecs, LANES), F32), pltpu.VMEM((2, many, LANES), F32), sem((2, chunks))],
    )
    return from_rows(out, vectors.shape), grams


def solution(mesh):
    in_specs = (P(None, None, None, None, None, "sa", "ta"), P("ta", None, None, None, "sa", None))
    out_specs = (
        P(("cfg", "ta"), None, None, None, "sa", None),
        P(("cfg", "ta"), None, None, None, None),
    )
    return jax.shard_map(on_device, mesh=mesh, in_specs=in_specs, out_specs=out_specs, check_vma=False)
```

```python
import functools

import jax
import jax.numpy as jnp
from jax import lax
from jax.experimental import pallas as pl
from jax.experimental.pallas import tpu as pltpu
from jax.sharding import PartitionSpec as P


LX = 32
LANES = 128
DEG = 3
SCALE = 5.5
F32 = jnp.float32
BF16 = jnp.bfloat16
VMEM = pl.BlockSpec(memory_space=pltpu.VMEM)
FAR = pl.BlockSpec(memory_space=pltpu.HBM)
GRANT = 16 * 2**20


def shape_of(*dims, dtype=F32):
    return jax.ShapeDtypeStruct(dims, dtype)


def call(kernel, outs, *args, ops=1e6, scratch=(), pick=None, far=(), far_out=(), alias=None):
    size = sum(a.size * 4 for a in args) + sum(4 * o.size for o in jax.tree.leaves(outs))
    several = isinstance(outs, (list, tuple))
    params = dict(
        out_shape=outs,
        compiler_params=pltpu.CompilerParams(vmem_limit_bytes=GRANT),
        cost_estimate=pl.CostEstimate(flops=int(ops), bytes_accessed=int(size), transcendentals=0),
        input_output_aliases=alias or {},
    )
    in_specs = [FAR if k in far else VMEM for k in range(len(args))]
    out_specs = [VMEM] * len(outs) if several else VMEM
    if pick is None:
        return pl.pallas_call(
            kernel, in_specs=in_specs, out_specs=out_specs, scratch_shapes=scratch, **params
        )(*args)
    out_specs = [FAR if k in far_out else VMEM for k in range(len(outs))]
    spec = pltpu.PrefetchScalarGridSpec(
        num_scalar_prefetch=1, grid=(1,), in_specs=in_specs, out_specs=out_specs, scratch_shapes=scratch
    )
    return pl.pallas_call(kernel, grid_spec=spec, **params)(pick, *args)


def to_rows(x):
    depth, plane = x.shape[-2:]
    x = x.reshape(-1, depth, plane // LANES, LANES)
    return jnp.swapaxes(x, 1, 2).reshape(-1, LANES)


def from_rows(x, shape):
    depth, plane = shape[-2:]
    x = x.reshape(-1, plane // LANES, depth, LANES)
    return jnp.swapaxes(x, 1, 2).reshape(shape)


def pieces_of(depth):
    if depth == 1:
        return [[0]]
    if depth == 2:
        return [[0], [1]]
    return [[0], list(range(1, depth - 1)), [depth - 1]]


def plane_refs(refs, pieces):
    return {z: ref.at[k] for ref, planes in zip(refs, pieces) for k, z in enumerate(planes)}


def lane_index(shape):
    return lax.broadcasted_iota(jnp.int32, shape, len(shape) - 1)


def ahead_x(v, lane):
    wrap = (lane % LX) == LX - 1
    return jnp.where(wrap, pltpu.roll(v, LX - 1, v.ndim - 1), pltpu.roll(v, LANES - 1, v.ndim - 1))


def behind_x(v, lane):
    wrap = (lane % LX) == 0
    return jnp.where(wrap, pltpu.roll(v, LANES - LX + 1, v.ndim - 1), pltpu.roll(v, 1, v.ndim - 1))


def ahead_y(here, after, lane):
    ax = here.ndim - 1
    return jnp.where(lane < LANES - LX, pltpu.roll(here, LANES - LX, ax), pltpu.roll(after, LANES - LX, ax))


def behind_y(here, before, lane):
    ax = here.ndim - 1
    return jnp.where(lane < LX, pltpu.roll(before, LX, ax), pltpu.roll(here, LX, ax))


def take_planes(out, raw_ref, first, count, rows, depth):
    stride = 6 * rows * depth

    def body(c, _):
        for z in out:
            for q in range(6):
                start = first * stride + q * rows * depth + c * depth + z
                out[z][c, q, first : first + count, :] = raw_ref[pl.ds(start, count, stride=stride), :]
        return 0

    lax.fori_loop(0, rows, body, 0)


def planes_kernel(depth, pieces, pick_ref, far_ref, *refs):
    *out_refs, raw_ref, sems = refs
    out = plane_refs(out_refs, pieces)
    rows, _, vecs, _ = out[pieces[0][0]].shape
    size = raw_ref.shape[0]
    parts = 2
    copies = []
    for k in range(parts):
        block = pl.ds(k * (size // parts), size // parts)
        source = pl.ds(pick_ref[0] * size + k * (size // parts), size // parts)
        copies.append(pltpu.make_async_copy(far_ref.at[source], raw_ref.at[block], sems.at[k]))
        copies[-1].start()
    for k in range(parts):
        copies[k].wait()
        take_planes(out, raw_ref, k * (vecs // parts), vecs // parts, rows, depth)


def link_kernel(depth, half, pick_ref, far_ref, came_ref, table_ref, behind_ref, top_ref, sem):
    core = pick_ref[1]
    copy = pltpu.make_async_copy(far_ref.at[pick_ref[2]], table_ref.at[core], sem)
    copy.start()
    table_ref[1 - core] = came_ref[...]
    copy.wait()
    count = half * depth
    lane = lane_index((count, LANES))

    def shift(d, _):
        for h in range(2):
            behind_ref[h, d] = behind_x(table_ref[h, d], lane)
        low, high = table_ref[0, 18 + d], table_ref[1, 18 + d]
        for h, here, wrap in ((0, low, high), (1, high, low)):
            before = wrap[count - depth :]
            if half > 1:
                before = jnp.concatenate([before, here[: count - depth]], axis=0)
            behind_ref[h, 18 + d] = behind_y(here, before, lane)
        for h in range(2):
            top_ref[d, h * half : (h + 1) * half, :] = table_ref[h, 36 + d, pl.ds(depth - 1, half, stride=depth), :]
        return 0

    lax.fori_loop(0, 18, shift, 0)


def multiply_into(total, field, link, adjoint):
    for col in range(3):
        re, im = field(col), field(3 + col)
        for row in range(3):
            entry = col * 3 + row if adjoint else row * 3 + col
            a, b = link(entry), link(9 + entry)
            if adjoint:
                total[row] = total[row] + a * re + b * im
                total[3 + row] = total[3 + row] + a * im - b * re
            else:
                total[row] = total[row] + a * re - b * im
                total[3 + row] = total[3 + row] + a * im + b * re


def rows_of(ref, c, z, depth, first, vecs):
    half = ref.shape[2] // depth
    row = lax.rem(c, half) * depth + z

    def link(k):
        return jnp.broadcast_to(ref[c // half, first + k, pl.ds(row, 1), :], (vecs, LANES))

    return link


def edge_rows(ref, c, vecs):
    def link(k):
        return jnp.broadcast_to(ref[k, pl.ds(c, 1), :], (vecs, LANES))

    return link


def forward_hops(total, cur, up, table, c, z, depth, lane):
    rows, _, vecs, _ = cur.shape
    after = lax.rem(c + 1, rows)
    multiply_into(total, lambda q: ahead_x(cur[c, q], lane), rows_of(table, c, z, depth, 0, vecs), False)
    multiply_into(
        total, lambda q: ahead_y(cur[c, q], cur[after, q], lane), rows_of(table, c, z, depth, 18, vecs), False
    )
    if up is not None:
        multiply_into(total, lambda q: up[c, q], rows_of(table, c, z, depth, 36, vecs), False)


def backward_hops(total, cur, down, table, behind, c, z, depth, lane):
    rows, _, vecs, _ = cur.shape
    before = lax.rem(c + rows - 1, rows)
    multiply_into(total, lambda q: behind_x(cur[c, q], lane), rows_of(behind, c, z, depth, 0, vecs), True)
    multiply_into(
        total, lambda q: behind_y(cur[c, q], cur[before, q], lane), rows_of(behind, c, z, depth, 18, vecs), True
    )
    if down is not None:
        multiply_into(total, lambda q: down[c, q], rows_of(table, c, z - 1, depth, 36, vecs), True)


def part_kernel(depth, pieces, todo, factor, first, table_ref, behind_ref, *refs):
    refs = list(refs)
    cur = plane_refs([refs.pop(0) for _ in pieces], pieces)
    done = [pieces[k] for k in todo]
    old = None if first else plane_refs([refs.pop(0) for _ in todo], done)
    out = plane_refs(refs, done)
    rows, _, vecs, _ = cur[0].shape
    lane = lane_index((vecs, LANES))
    for z in out:

        def body(c, _, z=z):
            total = [cur[z][c, q] for q in range(6)]
            forward_hops(total, cur[z], cur.get(z + 1), table_ref, c, z, depth, lane)
            backward_hops(total, cur[z], cur.get(z - 1), table_ref, behind_ref, c, z, depth, lane)
            for q in range(6):
                value = total[q] * factor
                out[z][c, q] = value if first else value - old[z][c, q]
            return 0

        lax.fori_loop(0, rows, body, 0)


def whole_plane(message_ref, base_ref, links_ref, factor, back, c):
    plane = [message_ref[0, c, q] for q in range(6)]
    if base_ref is not None:
        total = [jnp.zeros_like(plane[0]) for _ in range(6)]
        multiply_into(total, lambda q: base_ref[0, c, q], edge_rows(links_ref, c, plane[0].shape[0]), back)
        plane = [p + t * factor for p, t in zip(plane, total)]
    return plane


def close_kernel(factor, factor_before, behind, based, *refs):
    refs = list(refs)
    part_ref, out_ref = refs[-2].at[0], refs[-1].at[0]
    rows, _, vecs, _ = out_ref.shape
    each = 3 if based else 2

    def body(c, _):
        total = [jnp.zeros((vecs, LANES), F32) for _ in range(6)]
        for k, back in enumerate(behind):
            links_ref, halo_ref, *base = refs[each * k : each * (k + 1)]
            halo = whole_plane(halo_ref, base[0] if based else None, links_ref, factor_before, not back, c)
            multiply_into(total, lambda q: halo[q], edge_rows(links_ref, c, vecs), back)
        for q in range(6):
            out_ref[c, q] = part_ref[c, q] + total[q] * factor
        return 0

    lax.fori_loop(0, rows, body, 0)


def halves(x):
    high = x.astype(BF16)
    return high, (x - high.astype(F32)).astype(BF16)


def high_low(tiles):
    pairs = [halves(jnp.concatenate(tiles[k : k + 3], axis=1)) for k in (0, 3)]
    return [pairs[0][0], pairs[1][0], pairs[0][1], pairs[1][1]]


def products(acc_ref, rows, own, sides):
    def body(pair, _):
        stacks = [[], []]
        for c in (2 * pair, 2 * pair + 1):
            for stack, tiles in zip(stacks, sides(c)):
                stack.append(jnp.concatenate(high_low(tiles), axis=0))
        left, right = [jnp.concatenate(s, axis=1) for s in stacks]
        right = jnp.concatenate([left if own else jnp.zeros_like(left), right], axis=0)
        acc_ref[...] += lax.dot_general(left, right, (((1,), (1,)), ((), ())), preferred_element_type=F32)
        return 0

    lax.fori_loop(0, rows // 2, body, 0)


def packed_product(acc, n):
    acc = acc[0 : 2 * n] + acc[2 * n : 4 * n]
    acc = acc + pltpu.roll(acc, LANES - 2 * n, 1)
    re, im = acc[0:n], acc[n : 2 * n]
    real = re + pltpu.roll(im, LANES - n, 1)
    imag = re - pltpu.roll(im, n, 1)
    return jnp.where(lane_index((n, LANES)) % (2 * n) < n, real, imag)


def gram_kernel(depth, pieces, tasks, more, table_ref, *refs):
    refs = list(refs)
    acc_ref, out_ref = refs.pop(), refs.pop()
    sofar_ref = refs.pop() if more else None
    cur = plane_refs(refs, pieces)
    rows, _, vecs, _ = cur[tasks[0][0]].shape
    lane = lane_index((vecs, LANES))
    acc_ref[...] = jnp.zeros_like(acc_ref)
    for z, own, depth_hop in tasks:

        def sides(c, z=z, own=own, depth_hop=depth_hop):
            total = [jnp.zeros((vecs, LANES), F32) for _ in range(6)]
            if own:
                forward_hops(total, cur[z], cur[z + 1] if depth_hop else None, table_ref, c, z, depth, lane)
            else:
                up = cur[z + 1]
                multiply_into(total, lambda q: up[c, q], rows_of(table_ref, c, z, depth, 36, vecs), False)
            return [cur[z][c, q] for q in range(6)], total

        products(acc_ref, rows, own, sides)
    part = packed_product(acc_ref[...], vecs)
    out_ref[...] = part + sofar_ref[...] if more else part


def last_hop_kernel(factor, links_ref, top_ref, above_ref, *refs):
    *base, sofar_ref, out_ref, acc_ref = refs
    rows, _, vecs, _ = top_ref.shape[1:]
    acc_ref[...] = jnp.zeros_like(acc_ref)

    def sides(c):
        total = [jnp.zeros((vecs, LANES), F32) for _ in range(6)]
        above = whole_plane(above_ref, base[0] if base else None, links_ref, factor, True, c)
        multiply_into(total, lambda q: above[q], edge_rows(links_ref, c, vecs), False)
        return [top_ref[0, c, q] for q in range(6)], total

    products(acc_ref, rows, False, sides)
    out_ref[...] = packed_product(acc_ref[...], vecs) + sofar_ref[...]


def norms_of(packed):
    n = packed.shape[0]
    diag = lane_index((n, LANES)) == lax.broadcasted_iota(jnp.int32, (n, LANES), 0)
    return jnp.where(diag, packed, 0.0)


def scatter_kernel(depth, planes, piece_ref, *refs):
    out_ref = refs[-1]
    rows, _, vecs, _ = piece_ref.shape[1:]
    stride = 6 * rows * depth

    def body(c, _):
        for k, z in enumerate(planes):
            for q in range(6):
                start = q * rows * depth + c * depth + z
                out_ref[pl.ds(start, vecs, stride=stride), :] = piece_ref[k, c, q]
        return 0

    lax.fori_loop(0, rows, body, 0)


def final_kernel(chunks, slot_ref, *refs):
    far_ref, grams_ref, scale_ref, ready_ref, sems = refs[-5:]
    copies = []
    for k in range(2):
        term0, term1, field_ref = refs[3 * k : 3 * k + 3]
        n = term0.shape[0]
        size = field_ref.shape[0] // n
        each = n // chunks
        slot = slot_ref[0] if k == 0 else 1 - slot_ref[0]
        packed = term0[...] + term1[...]
        norm = norms_of(packed)
        down = lax.rsqrt(jnp.sum(norm, axis=1, keepdims=True))
        scale_ref[...] = jnp.broadcast_to(down, (n, LANES))
        for j in range(chunks):

            def body(i, _, field_ref=field_ref, j=j, k=k):
                vec = j * each + i
                block = pl.ds(pl.multiple_of(vec * size, 8), size)
                ready_ref[k, block, :] = field_ref[block, :] * scale_ref[pl.ds(vec, 1), :]
                return 0

            lax.fori_loop(0, each, body, 0)
            part = pl.ds(j * each * size, each * size)
            target = pl.ds(slot * (n * size) + j * each * size, each * size)
            copies.append(pltpu.make_async_copy(ready_ref.at[k, part], far_ref.at[target], sems.at[k, j]))
            copies[-1].start()
        across = lax.rsqrt(jnp.sum(norm, axis=0, keepdims=True)[:, 0:n])
        scale = down * across
        over_re, over_im = packed[:, 0:n], packed[:, n : 2 * n]
        hop_re, hop_im = packed[:, 4 * n : 5 * n], packed[:, 5 * n : 6 * n]
        grams_ref[slot, 0, 0] = over_re * scale
        grams_ref[slot, 0, 1] = over_im * scale
        grams_ref[slot, 1, 0] = (6.0 * over_re - (hop_re + hop_re.T)) * scale
        grams_ref[slot, 1, 1] = (6.0 * over_im - (hop_im - hop_im.T)) * scale
    for copy in copies:
        copy.wait()


def shifted(x, axis, by):
    n = lax.axis_size(axis)
    return lax.ppermute(x, axis, [(i, (i + by) % n) for i in range(n)])


def flipped(x, axis, bit):
    return lax.ppermute(x, axis, [(i, i ^ bit) for i in range(lax.axis_size(axis))])


def summed(x):
    size = lax.axis_size("sa")
    count = size.bit_length() - 1
    assert size == 1 << count

    def across(x, cfg, bits):
        pairs = range(lax.axis_size("cfg") * size)
        return lax.ppermute(x, ("cfg", "sa"), [(i, i ^ (cfg * size + bits)) for i in pairs])

    bit = 1
    for _ in range((count - 1) // 2):
        x = x + flipped(x, "sa", bit) + flipped(x, "sa", 2 * bit) + flipped(x, "sa", 3 * bit)
        bit *= 4
    if count % 2 == 0:
        x = x + flipped(x, "sa", bit)
        bit *= 2
    return (x, flipped(x, "sa", bit)), (across(x, 1, 0), across(x, 1, bit))


def on_device(links, vectors):
    slices, vecs, _, _, depth, plane = vectors.shape
    rows = plane // LANES
    assert slices == 2 and lax.axis_size("cfg") % 2 == 0 and lax.axis_size("ta") == 2
    pieces = pieces_of(depth)
    ends = [0] if len(pieces) == 1 else [0, len(pieces) - 1]
    inner = [k for k in range(len(pieces)) if k not in ends]
    core = lax.axis_index("ta")
    mine = lax.axis_index("cfg") % 2
    pick = jnp.stack([mine, core, 2 * core + mine]).astype(jnp.int32)
    field = [shape_of(len(p), rows, 6, vecs, LANES) for p in pieces]
    work = 1000 * LANES * vecs * rows
    many = vecs * 6 * rows * depth
    half = rows // 2
    sem = pltpu.SemaphoreType.DMA

    view = pltpu.with_memory_space_constraint(to_rows(vectors), pltpu.HBM)

    def taken(todo):
        return call(
            functools.partial(planes_kernel, depth, [pieces[k] for k in todo]), [field[k] for k in todo],
            view, pick=pick, far=(0,), scratch=[pltpu.VMEM((many, LANES), F32), sem((2,))], ops=1e5,
        )

    first, rest = ends[-1:], [k for k in range(len(pieces)) if k != ends[-1]]
    start = [None] * len(pieces)
    for k, x in zip(first, taken(first)):
        start[k] = x
    flat = links.reshape((links.shape[0], 54) + links.shape[-2:])
    given = lax.dynamic_index_in_dim(flat, 2 * (1 - core) + mine, 0, keepdims=False)
    came = flipped(given, "ta", 1)
    if rest:
        for k, x in zip(rest, taken(rest)):
            start[k] = x
    table, behind, top_links = call(
        functools.partial(link_kernel, depth, half),
        [shape_of(2, 54, half * depth, LANES), shape_of(2, 36, half * depth, LANES), shape_of(18, rows, LANES)],
        pltpu.with_memory_space_constraint(to_rows(links).reshape(-1, 54, half * depth, LANES), pltpu.HBM),
        to_rows(came).reshape(54, half * depth, LANES),
        pick=pick, far=(0,), scratch=[sem], ops=1e6,
    )
    prior = shifted(top_links, "sa", 1)

    early = depth > 1

    def factor_of(step):
        return -(1.0 if step == 0 else 2.0) / SCALE

    def sent(planes, upwards=True):
        low = None
        if upwards:
            low = shifted(planes[-1], "sa", 1)
        return low, shifted(planes[0], "sa", -1)

    def advance(step, cur, old, messages):
        new = [None] * len(pieces)
        for todo in (inner, ends):
            if todo:
                got = call(
                    functools.partial(part_kernel, depth, pieces, todo, factor_of(step), old is None),
                    [field[k] for k in todo], table, behind, *cur,
                    *([] if old is None else [old[k] for k in todo]),
                    ops=work * sum(len(pieces[k]) for k in todo),
                )
                for k, x in zip(todo, got):
                    new[k] = x
        following = sent(new, step + 1 < DEG) if early else None
        based = early and old is not None
        sides = [(0, True, prior, messages[0]), (len(pieces) - 1, False, top_links, messages[1])]
        for k in ends:
            used = [side for side in sides if side[0] == k]
            operands = [x for side in used for x in (*side[2:], *([old[k]] if based else []))]
            (new[k],) = call(
                functools.partial(
                    close_kernel, factor_of(step), factor_of(step - 1), [side[1] for side in used], based
                ),
                [field[k]], *operands, new[k], ops=work / 6,
            )
        return new, following or sent(new, step + 1 < DEG)

    packed = shape_of(vecs, LANES)
    acc = [pltpu.VMEM((4 * vecs, 8 * vecs), F32)]

    def swapped(x):
        return flipped(x, "cfg", 1)

    def grams_of(planes, tasks, sofar):
        return call(
            functools.partial(gram_kernel, depth, [pieces[k] for k in planes], tasks, sofar is not None),
            packed, table, *[three[k] for k in planes], *([] if sofar is None else [sofar]),
            scratch=acc, ops=work * len(tasks) / 2,
        )

    old, three, messages = None, start, sent(start)
    for step in range(DEG):
        fresh, messages = advance(step, three, old, messages)
        old, three = three, fresh
    above = messages[1]

    sofar = None
    if inner:
        middle = pieces[1]
        sofar = grams_of(inner, [(z, True, z + 1 in middle) for z in middle], None)
    if len(ends) == 2:
        sofar = grams_of([0] + inner[:1], [(0, True, bool(inner))], sofar)
    tasks = [(depth - 1, True, False)]
    if depth > 1:
        tasks.append((depth - 2, False, True))
    sofar = grams_of(range(len(pieces)), tasks, sofar)
    sofar = call(
        functools.partial(last_hop_kernel, factor_of(DEG - 1)), packed,
        top_links, three[-1], above, *([old[-1]] if early else []), sofar,
        scratch=acc, ops=work / 4,
    )
    sum_mine, sum_other = summed(sofar)
    other = [swapped(x) for x in three]

    def scattered(planes):
        out = None
        for k in inner + ends:
            out = call(
                functools.partial(scatter_kernel, depth, pieces[k]), shape_of(many, LANES),
                planes[k], *([] if out is None else [out]), alias={} if out is None else {1: 0}, ops=1e5,
            )
        return out

    chunks = 4
    assert vecs % chunks == 0
    out, grams = call(
        functools.partial(final_kernel, chunks), [shape_of(2 * many, LANES), shape_of(2, 2, 2, vecs, vecs)],
        *sum_mine, scattered(three), *sum_other, scattered(other),
        pick=pick, far_out=(0,), ops=1e6,
        scratch=[pltpu.VMEM((vecs, LANES), F32), pltpu.VMEM((2, many, LANES), F32), sem((2, chunks))],
    )
    return from_rows(out, vectors.shape), grams


def solution(mesh):
    in_specs = (P(None, None, None, None, None, "sa", "ta"), P("ta", None, None, None, "sa", None))
    out_specs = (
        P(("cfg", "ta"), None, None, None, "sa", None),
        P(("cfg", "ta"), None, None, None, None),
    )
    return jax.shard_map(on_device, mesh=mesh, in_specs=in_specs, out_specs=out_specs, check_vma=False)
```

```python
import functools

import jax
import jax.numpy as jnp
from jax import lax
from jax.experimental import pallas as pl
from jax.experimental.pallas import tpu as pltpu
from jax.sharding import PartitionSpec as P


LX = 32
LANES = 128
SCALE = 5.5
F32 = jnp.float32
BF16 = jnp.bfloat16
VMEM = pl.BlockSpec(memory_space=pltpu.VMEM)
FAR = pl.BlockSpec(memory_space=pltpu.HBM)
GRANT = 16 * 2**20
GROUP = 8


def shape_of(*dims, dtype=F32):
    return jax.ShapeDtypeStruct(dims, dtype)


def call(kernel, outs, *args, ops=1e6, scratch=(), pick=None, far=(), far_out=(), alias=None):
    size = sum(a.size * 4 for a in args) + sum(4 * o.size for o in jax.tree.leaves(outs))
    several = isinstance(outs, (list, tuple))
    params = dict(
        out_shape=outs,
        compiler_params=pltpu.CompilerParams(vmem_limit_bytes=GRANT),
        cost_estimate=pl.CostEstimate(flops=int(ops), bytes_accessed=int(size), transcendentals=0),
        input_output_aliases=alias or {},
    )
    in_specs = [FAR if k in far else VMEM for k in range(len(args))]
    out_specs = [VMEM] * len(outs) if several else VMEM
    if pick is None:
        return pl.pallas_call(
            kernel, in_specs=in_specs, out_specs=out_specs, scratch_shapes=scratch, **params
        )(*args)
    out_specs = [FAR if k in far_out else VMEM for k in range(len(outs))]
    spec = pltpu.PrefetchScalarGridSpec(
        num_scalar_prefetch=1, grid=(1,), in_specs=in_specs, out_specs=out_specs, scratch_shapes=scratch
    )
    return pl.pallas_call(kernel, grid_spec=spec, **params)(pick, *args)


def to_rows(x):
    depth, plane = x.shape[-2:]
    x = x.reshape(-1, depth, plane // LANES, LANES)
    return jnp.swapaxes(x, 1, 2).reshape(-1, LANES)


def from_rows(x, shape):
    depth, plane = shape[-2:]
    x = x.reshape(-1, plane // LANES, depth, LANES)
    return jnp.swapaxes(x, 1, 2).reshape(shape)


def pieces_of(depth):
    if depth == 1:
        return [[0]]
    if depth == 2:
        return [[0], [1]]
    return [[0], list(range(1, depth - 1)), [depth - 1]]


def plane_refs(refs, pieces):
    return {z: ref.at[k] for ref, planes in zip(refs, pieces) for k, z in enumerate(planes)}


def lane_index(shape):
    return lax.broadcasted_iota(jnp.int32, shape, len(shape) - 1)


def ahead_x(v, lane):
    wrap = (lane % LX) == LX - 1
    return jnp.where(wrap, pltpu.roll(v, LX - 1, v.ndim - 1), pltpu.roll(v, LANES - 1, v.ndim - 1))


def behind_x(v, lane):
    wrap = (lane % LX) == 0
    return jnp.where(wrap, pltpu.roll(v, LANES - LX + 1, v.ndim - 1), pltpu.roll(v, 1, v.ndim - 1))


def ahead_y(here, after, lane):
    ax = here.ndim - 1
    return jnp.where(lane < LANES - LX, pltpu.roll(here, LANES - LX, ax), pltpu.roll(after, LANES - LX, ax))


def behind_y(here, before, lane):
    ax = here.ndim - 1
    return jnp.where(lane < LX, pltpu.roll(before, LX, ax), pltpu.roll(here, LX, ax))


def take_planes(out, raw_ref, first, count, rows, depth):
    stride = 6 * rows * depth

    def body(c, _):
        for z in out:
            for q in range(6):
                start = first * stride + q * rows * depth + c * depth + z
                out[z][c, q, first : first + count, :] = raw_ref[pl.ds(start, count, stride=stride), :]
        return 0

    lax.fori_loop(0, rows, body, 0)


def planes_kernel(depth, pieces, pick_ref, far_ref, *refs):
    *out_refs, raw_ref, sems = refs
    out = plane_refs(out_refs, pieces)
    rows, _, vecs, _ = out[pieces[0][0]].shape
    size = raw_ref.shape[0]
    parts = 2
    copies = []
    for k in range(parts):
        block = pl.ds(k * (size // parts), size // parts)
        source = pl.ds(pick_ref[0] * size + k * (size // parts), size // parts)
        copies.append(pltpu.make_async_copy(far_ref.at[source], raw_ref.at[block], sems.at[k]))
        copies[-1].start()
    for k in range(parts):
        copies[k].wait()
        take_planes(out, raw_ref, k * (vecs // parts), vecs // parts, rows, depth)


def link_kernel(depth, half, pick_ref, far_ref, came_ref, table_ref, behind_ref, top_ref, sem):
    core = pick_ref[1]
    copy = pltpu.make_async_copy(far_ref.at[pick_ref[2]], table_ref.at[core], sem)
    copy.start()
    table_ref[1 - core] = came_ref[...]
    copy.wait()
    count = half * depth
    lane = lane_index((count, LANES))

    def shift(d, _):
        for h in range(2):
            behind_ref[h, d] = behind_x(table_ref[h, d], lane)
        low, high = table_ref[0, 18 + d], table_ref[1, 18 + d]
        for h, here, wrap in ((0, low, high), (1, high, low)):
            before = wrap[count - depth :]
            if half > 1:
                before = jnp.concatenate([before, here[: count - depth]], axis=0)
            behind_ref[h, 18 + d] = behind_y(here, before, lane)
        for h in range(2):
            top_ref[d, h * half : (h + 1) * half, :] = table_ref[h, 36 + d, pl.ds(depth - 1, half, stride=depth), :]
        return 0

    lax.fori_loop(0, 18, shift, 0)


def multiply_into(total, field, link, adjoint):
    for col in range(3):
        re, im = field(col), field(3 + col)
        for row in range(3):
            entry = col * 3 + row if adjoint else row * 3 + col
            a, b = link(entry), link(9 + entry)
            if adjoint:
                total[row] = total[row] + a * re + b * im
                total[3 + row] = total[3 + row] + a * im - b * re
            else:
                total[row] = total[row] + a * re - b * im
                total[3 + row] = total[3 + row] + a * im + b * re


def rows_of(ref, c, z, depth, first, vecs):
    half = ref.shape[2] // depth
    row = lax.rem(c, half) * depth + z

    def link(k):
        return jnp.broadcast_to(ref[c // half, first + k, pl.ds(row, 1), :], (vecs, LANES))

    return link


def edge_rows(ref, c, vecs):
    def link(k):
        return jnp.broadcast_to(ref[k, pl.ds(c, 1), :], (vecs, LANES))

    return link


def forward_hops(total, cur, up, table, c, z, depth, lane):
    rows, _, vecs, _ = cur.shape
    after = lax.rem(c + 1, rows)
    multiply_into(total, lambda q: ahead_x(cur[c, q], lane), rows_of(table, c, z, depth, 0, vecs), False)
    multiply_into(
        total, lambda q: ahead_y(cur[c, q], cur[after, q], lane), rows_of(table, c, z, depth, 18, vecs), False
    )
    if up is not None:
        multiply_into(total, lambda q: up[c, q], rows_of(table, c, z, depth, 36, vecs), False)


def backward_hops(total, cur, down, table, behind, c, z, depth, lane):
    rows, _, vecs, _ = cur.shape
    before = lax.rem(c + rows - 1, rows)
    multiply_into(total, lambda q: behind_x(cur[c, q], lane), rows_of(behind, c, z, depth, 0, vecs), True)
    multiply_into(
        total, lambda q: behind_y(cur[c, q], cur[before, q], lane), rows_of(behind, c, z, depth, 18, vecs), True
    )
    if down is not None:
        multiply_into(total, lambda q: down[c, q], rows_of(table, c, z - 1, depth, 36, vecs), True)


def part_kernel(depth, pieces, todo, factor, first, table_ref, behind_ref, *refs):
    refs = list(refs)
    cur = plane_refs([refs.pop(0) for _ in pieces], pieces)
    done = [pieces[k] for k in todo]
    old = None if first else plane_refs([refs.pop(0) for _ in todo], done)
    out = plane_refs(refs, done)
    rows, _, vecs, _ = cur[0].shape
    lane = lane_index((vecs, LANES))
    for z in out:

        def body(c, _, z=z):
            total = [cur[z][c, q] for q in range(6)]
            forward_hops(total, cur[z], cur.get(z + 1), table_ref, c, z, depth, lane)
            backward_hops(total, cur[z], cur.get(z - 1), table_ref, behind_ref, c, z, depth, lane)
            for q in range(6):
                value = total[q] * factor
                out[z][c, q] = value if first else value - old[z][c, q]
            return 0

        lax.fori_loop(0, rows, body, 0)


def close_kernel(factor, behind, *refs):
    part_ref, out_ref = refs[-2].at[0], refs[-1].at[0]
    rows, _, vecs, _ = out_ref.shape

    def body(c, _):
        total = [jnp.zeros((vecs, LANES), F32) for _ in range(6)]
        for k, back in enumerate(behind):
            links_ref, halo_ref = refs[2 * k : 2 * k + 2]
            multiply_into(total, lambda q: halo_ref[0, c, q], edge_rows(links_ref, c, vecs), back)
        for q in range(6):
            out_ref[c, q] = part_ref[c, q] + total[q] * factor
        return 0

    lax.fori_loop(0, rows, body, 0)


def halves(x):
    high = x.astype(BF16)
    return high, (x - high.astype(F32)).astype(BF16)


def high_low(tiles):
    pairs = [halves(jnp.concatenate(tiles[k : k + 3], axis=1)) for k in (0, 3)]
    return [pairs[0][0], pairs[1][0], pairs[0][1], pairs[1][1]]


def products(acc_ref, rows, own, sides):
    group = min(rows, GROUP)
    assert rows % group == 0

    def body(step, _):
        stacks = [[], []]
        for k in range(group):
            for stack, tiles in zip(stacks, sides(group * step + k)):
                stack.append(jnp.concatenate(high_low(tiles), axis=0))
        left, right = [jnp.concatenate(s, axis=1) for s in stacks]
        right = jnp.concatenate([left if own else jnp.zeros_like(left), right], axis=0)
        acc_ref[...] += lax.dot_general(left, right, (((1,), (1,)), ((), ())), preferred_element_type=F32)
        return 0

    lax.fori_loop(0, rows // group, body, 0)


def packed_product(acc, n):
    acc = acc[0 : 2 * n] + acc[2 * n : 4 * n]
    acc = acc + pltpu.roll(acc, LANES - 2 * n, 1)
    re, im = acc[0:n], acc[n : 2 * n]
    real = re + pltpu.roll(im, LANES - n, 1)
    imag = re - pltpu.roll(im, n, 1)
    return jnp.where(lane_index((n, LANES)) % (2 * n) < n, real, imag)


def gram_kernel(depth, pieces, tasks, more, table_ref, *refs):
    refs = list(refs)
    acc_ref, out_ref = refs.pop(), refs.pop()
    sofar_ref = refs.pop() if more else None
    cur = plane_refs(refs, pieces)
    rows, _, vecs, _ = cur[tasks[0][0]].shape
    lane = lane_index((vecs, LANES))
    acc_ref[...] = jnp.zeros_like(acc_ref)
    for z, own, depth_hop in tasks:

        def sides(c, z=z, own=own, depth_hop=depth_hop):
            total = [jnp.zeros((vecs, LANES), F32) for _ in range(6)]
            if own:
                forward_hops(total, cur[z], cur[z + 1] if depth_hop else None, table_ref, c, z, depth, lane)
            else:
                up = cur[z + 1]
                multiply_into(total, lambda q: up[c, q], rows_of(table_ref, c, z, depth, 36, vecs), False)
            return [cur[z][c, q] for q in range(6)], total

        products(acc_ref, rows, own, sides)
    part = packed_product(acc_ref[...], vecs)
    out_ref[...] = part + sofar_ref[...] if more else part


def last_hop_kernel(links_ref, top_ref, above_ref, sofar_ref, out_ref, acc_ref):
    rows, _, vecs, _ = top_ref.shape[1:]
    acc_ref[...] = jnp.zeros_like(acc_ref)

    def sides(c):
        total = [jnp.zeros((vecs, LANES), F32) for _ in range(6)]
        multiply_into(total, lambda q: above_ref[0, c, q], edge_rows(links_ref, c, vecs), False)
        return [top_ref[0, c, q] for q in range(6)], total

    products(acc_ref, rows, False, sides)
    out_ref[...] = packed_product(acc_ref[...], vecs) + sofar_ref[...]


def norms_of(packed):
    n = packed.shape[0]
    diag = lane_index((n, LANES)) == lax.broadcasted_iota(jnp.int32, (n, LANES), 0)
    return jnp.where(diag, packed, 0.0)


def scatter_kernel(depth, planes, piece_ref, *refs):
    out_ref = refs[-1]
    rows, _, vecs, _ = piece_ref.shape[1:]
    stride = 6 * rows * depth

    def body(c, _):
        for k, z in enumerate(planes):
            for q in range(6):
                start = q * rows * depth + c * depth + z
                out_ref[pl.ds(start, vecs, stride=stride), :] = piece_ref[k, c, q]
        return 0

    lax.fori_loop(0, rows, body, 0)


def scale_out(field_ref, far_ref, slot, inverse, chunks, scale_ref, ready_ref, sems):
    n = inverse.shape[0]
    size = field_ref.shape[0] // n
    each = n // chunks
    scale_ref[...] = jnp.broadcast_to(inverse, (n, LANES))
    copies = []
    for j in range(chunks):

        def body(i, _, j=j):
            vec = j * each + i
            block = pl.ds(pl.multiple_of(vec * size, 8), size)
            ready_ref[block, :] = field_ref[block, :] * scale_ref[pl.ds(vec, 1), :]
            return 0

        lax.fori_loop(0, each, body, 0)
        part = pl.ds(j * each * size, each * size)
        target = pl.ds(slot * (n * size) + j * each * size, each * size)
        copies.append(pltpu.make_async_copy(ready_ref.at[part], far_ref.at[target], sems.at[j]))
        copies[-1].start()
    return copies


def mine_kernel(chunks, slot_ref, sum_ref, field_ref, far_ref, *scratch):
    inverse = lax.rsqrt(jnp.sum(norms_of(sum_ref[...]), axis=1, keepdims=True))
    for copy in scale_out(field_ref, far_ref, slot_ref[0], inverse, chunks, *scratch):
        copy.wait()


def other_kernel(chunks, slot_ref, mine_ref, other_ref, field_ref, _, far_ref, grams_ref, *scratch):
    parts = []
    for slot, ref in ((1 - slot_ref[0], other_ref), (slot_ref[0], mine_ref)):
        packed = ref[...]
        norm = norms_of(packed)
        parts.append((slot, packed, norm, lax.rsqrt(jnp.sum(norm, axis=1, keepdims=True))))
    copies = scale_out(field_ref, far_ref, 1 - slot_ref[0], parts[0][3], chunks, *scratch)
    n = mine_ref.shape[0]
    for slot, packed, norm, down in parts:
        across = lax.rsqrt(jnp.sum(norm, axis=0, keepdims=True)[:, 0:n])
        scale = down * across
        over_re, over_im = packed[:, 0:n], packed[:, n : 2 * n]
        hop_re, hop_im = packed[:, 4 * n : 5 * n], packed[:, 5 * n : 6 * n]
        grams_ref[slot, 0, 0] = over_re * scale
        grams_ref[slot, 0, 1] = over_im * scale
        grams_ref[slot, 1, 0] = (6.0 * over_re - (hop_re + hop_re.T)) * scale
        grams_ref[slot, 1, 1] = (6.0 * over_im - (hop_im - hop_im.T)) * scale
    for copy in copies:
        copy.wait()


def shifted(x, axis, by):
    n = lax.axis_size(axis)
    return lax.ppermute(x, axis, [(i, (i + by) % n) for i in range(n)])


def flipped(x, axis, bit):
    return lax.ppermute(x, axis, [(i, i ^ bit) for i in range(lax.axis_size(axis))])


def summed(x):
    size = lax.axis_size("sa")
    count = size.bit_length() - 1
    assert size == 1 << count
    bit = 1
    while bit < size:
        bits = (bit, 2 * bit, 3 * bit) if 4 * bit <= size else (bit,)
        x = sum([flipped(x, "sa", k) for k in bits], x)
        bit = bit * (4 if len(bits) == 3 else 2)
    return x


def on_device(links, vectors):
    slices, vecs, _, _, depth, plane = vectors.shape
    rows = plane // LANES
    assert slices == 2 and lax.axis_size("cfg") % 2 == 0 and lax.axis_size("ta") == 2
    pieces = pieces_of(depth)
    ends = [0] if len(pieces) == 1 else [0, len(pieces) - 1]
    inner = [k for k in range(len(pieces)) if k not in ends]
    core = lax.axis_index("ta")
    mine = lax.axis_index("cfg") % 2
    pick = jnp.stack([mine, core, 2 * core + mine]).astype(jnp.int32)
    field = [shape_of(len(p), rows, 6, vecs, LANES) for p in pieces]
    work = 1000 * LANES * vecs * rows
    many = vecs * 6 * rows * depth
    half = rows // 2
    sem = pltpu.SemaphoreType.DMA

    view = pltpu.with_memory_space_constraint(to_rows(vectors), pltpu.HBM)

    def taken(todo):
        return call(
            functools.partial(planes_kernel, depth, [pieces[k] for k in todo]), [field[k] for k in todo],
            view, pick=pick, far=(0,), scratch=[pltpu.VMEM((many, LANES), F32), sem((2,))], ops=1e5,
        )

    first, rest = ends[-1:], [k for k in range(len(pieces)) if k != ends[-1]]
    start = [None] * len(pieces)
    for k, x in zip(first, taken(first)):
        start[k] = x
    flat = links.reshape((links.shape[0], 54) + links.shape[-2:])
    given = lax.dynamic_index_in_dim(flat, 2 * (1 - core) + mine, 0, keepdims=False)
    came = flipped(given, "ta", 1)
    if rest:
        for k, x in zip(rest, taken(rest)):
            start[k] = x
    table, behind, top_links = call(
        functools.partial(link_kernel, depth, half),
        [shape_of(2, 54, half * depth, LANES), shape_of(2, 36, half * depth, LANES), shape_of(18, rows, LANES)],
        pltpu.with_memory_space_constraint(to_rows(links).reshape(-1, 54, half * depth, LANES), pltpu.HBM),
        to_rows(came).reshape(54, half * depth, LANES),
        pick=pick, far=(0,), scratch=[sem], ops=1e6,
    )
    prior = shifted(top_links, "sa", 1)

    def advance(cur, old):
        factor = -(1.0 if old is None else 2.0) / SCALE
        low = shifted(cur[-1], "sa", 1)
        high = shifted(cur[0], "sa", -1)
        new = [None] * len(pieces)
        for todo in (inner, ends):
            if todo:
                got = call(
                    functools.partial(part_kernel, depth, pieces, todo, factor, old is None),
                    [field[k] for k in todo], table, behind, *cur, *([] if old is None else [old[k] for k in todo]),
                    ops=work * sum(len(pieces[k]) for k in todo),
                )
                for k, x in zip(todo, got):
                    new[k] = x
        sides = [(0, True, prior, low), (len(pieces) - 1, False, top_links, high)]
        for k in ends:
            used = [side for side in sides if side[0] == k]
            operands = [x for side in used for x in side[2:]]
            (new[k],) = call(
                functools.partial(close_kernel, factor, [side[1] for side in used]),
                [field[k]], *operands, new[k], ops=work / 6,
            )
        return new

    packed = shape_of(vecs, LANES)
    acc = [pltpu.VMEM((4 * vecs, 8 * vecs), F32)]

    def swapped(x):
        return flipped(x, "cfg", 1)

    def grams_of(planes, tasks, sofar):
        return call(
            functools.partial(gram_kernel, depth, [pieces[k] for k in planes], tasks, sofar is not None),
            packed, table, *[three[k] for k in planes], *([] if sofar is None else [sofar]),
            scratch=acc, ops=work * len(tasks) / 2,
        )

    one = advance(start, None)
    two = advance(one, start)
    three = advance(two, one)

    sofar = None
    if inner:
        middle = pieces[1]
        sofar = grams_of(inner, [(z, True, z + 1 in middle) for z in middle], None)
    above = shifted(three[0], "sa", -1)
    if len(ends) == 2:
        sofar = grams_of([0] + inner[:1], [(0, True, bool(inner))], sofar)
    tasks = [(depth - 1, True, False)]
    if depth > 1:
        tasks.append((depth - 2, False, True))
    sofar = grams_of(range(len(pieces)), tasks, sofar)
    sofar = call(
        last_hop_kernel, packed, top_links, three[-1], above, sofar,
        scratch=acc, ops=work / 4,
    )
    sum_mine = summed(sofar)
    sum_other = flipped(sum_mine, "cfg", 1)
    other = [swapped(x) for x in three]

    def scattered(planes):
        out = None
        for k in inner + ends:
            out = call(
                functools.partial(scatter_kernel, depth, pieces[k]), shape_of(many, LANES),
                planes[k], *([] if out is None else [out]), alias={} if out is None else {1: 0}, ops=1e5,
            )
        return out

    chunks = 4
    assert vecs % chunks == 0
    scratch = [pltpu.VMEM((vecs, LANES), F32), pltpu.VMEM((many, LANES), F32), sem((chunks,))]
    ours, theirs = scattered(three), scattered(other)
    (out,) = call(
        functools.partial(mine_kernel, chunks), [shape_of(2 * many, LANES)],
        sum_mine, ours, pick=pick, far_out=(0,), ops=1e6, scratch=scratch,
    )
    out, grams = call(
        functools.partial(other_kernel, chunks), [shape_of(2 * many, LANES), shape_of(2, 2, 2, vecs, vecs)],
        sum_mine, sum_other, theirs, out, pick=pick, far=(3,), far_out=(0,), ops=1e6, scratch=scratch,
        alias={4: 0},
    )
    return from_rows(out, vectors.shape), grams


def solution(mesh):
    in_specs = (P(None, None, None, None, None, "sa", "ta"), P("ta", None, None, None, "sa", None))
    out_specs = (
        P(("cfg", "ta"), None, None, None, "sa", None),
        P(("cfg", "ta"), None, None, None, None),
    )
    return jax.shard_map(on_device, mesh=mesh, in_specs=in_specs, out_specs=out_specs, check_vma=False)
```

```python
import functools

import jax
import jax.numpy as jnp
from jax import lax
from jax.experimental import pallas as pl
from jax.experimental.pallas import tpu as pltpu
from jax.sharding import PartitionSpec as P


LX = 32
LANES = 128
SCALE = 5.5
F32 = jnp.float32
BF16 = jnp.bfloat16
VMEM = pl.BlockSpec(memory_space=pltpu.VMEM)
FAR = pl.BlockSpec(memory_space=pltpu.HBM)
GRANT = 16 * 2**20
GROUP = 8


def shape_of(*dims, dtype=F32):
    return jax.ShapeDtypeStruct(dims, dtype)


def call(kernel, outs, *args, ops=1e6, scratch=(), pick=None, far=(), far_out=(), alias=None):
    size = sum(a.size * 4 for a in args) + sum(4 * o.size for o in jax.tree.leaves(outs))
    several = isinstance(outs, (list, tuple))
    params = dict(
        out_shape=outs,
        compiler_params=pltpu.CompilerParams(vmem_limit_bytes=GRANT),
        cost_estimate=pl.CostEstimate(flops=int(ops), bytes_accessed=int(size), transcendentals=0),
        input_output_aliases=alias or {},
    )
    in_specs = [FAR if k in far else VMEM for k in range(len(args))]
    out_specs = [VMEM] * len(outs) if several else VMEM
    if pick is None:
        return pl.pallas_call(
            kernel, in_specs=in_specs, out_specs=out_specs, scratch_shapes=scratch, **params
        )(*args)
    out_specs = [FAR if k in far_out else VMEM for k in range(len(outs))]
    spec = pltpu.PrefetchScalarGridSpec(
        num_scalar_prefetch=1, grid=(1,), in_specs=in_specs, out_specs=out_specs, scratch_shapes=scratch
    )
    return pl.pallas_call(kernel, grid_spec=spec, **params)(pick, *args)


def to_rows(x):
    depth, plane = x.shape[-2:]
    x = x.reshape(-1, depth, plane // LANES, LANES)
    return jnp.swapaxes(x, 1, 2).reshape(-1, LANES)


def from_rows(x, shape):
    depth, plane = shape[-2:]
    x = x.reshape(-1, plane // LANES, depth, LANES)
    return jnp.swapaxes(x, 1, 2).reshape(shape)


def pieces_of(depth):
    if depth == 1:
        return [[0]]
    if depth == 2:
        return [[0], [1]]
    return [[0], list(range(1, depth - 1)), [depth - 1]]


def plane_refs(refs, pieces):
    return {z: ref.at[k] for ref, planes in zip(refs, pieces) for k, z in enumerate(planes)}


def lane_index(shape):
    return lax.broadcasted_iota(jnp.int32, shape, len(shape) - 1)


def ahead_x(v, lane):
    wrap = (lane % LX) == LX - 1
    return jnp.where(wrap, pltpu.roll(v, LX - 1, v.ndim - 1), pltpu.roll(v, LANES - 1, v.ndim - 1))


def behind_x(v, lane):
    wrap = (lane % LX) == 0
    return jnp.where(wrap, pltpu.roll(v, LANES - LX + 1, v.ndim - 1), pltpu.roll(v, 1, v.ndim - 1))


def ahead_y(here, after, lane):
    ax = here.ndim - 1
    return jnp.where(lane < LANES - LX, pltpu.roll(here, LANES - LX, ax), pltpu.roll(after, LANES - LX, ax))


def behind_y(here, before, lane):
    ax = here.ndim - 1
    return jnp.where(lane < LX, pltpu.roll(before, LX, ax), pltpu.roll(here, LX, ax))


def take_planes(out, raw_ref, first, count, rows, depth):
    stride = 6 * rows * depth

    def body(c, _):
        for z in out:
            for q in range(6):
                start = first * stride + q * rows * depth + c * depth + z
                out[z][c, q, first : first + count, :] = raw_ref[pl.ds(start, count, stride=stride), :]
        return 0

    lax.fori_loop(0, rows, body, 0, unroll=True)


def planes_kernel(depth, pieces, pick_ref, far_ref, *refs):
    *out_refs, raw_ref, sems = refs
    out = plane_refs(out_refs, pieces)
    rows, _, vecs, _ = out[pieces[0][0]].shape
    size = raw_ref.shape[0]
    parts = 2
    copies = []
    for k in range(parts):
        block = pl.ds(k * (size // parts), size // parts)
        source = pl.ds(pick_ref[0] * size + k * (size // parts), size // parts)
        copies.append(pltpu.make_async_copy(far_ref.at[source], raw_ref.at[block], sems.at[k]))
        copies[-1].start()
    for k in range(parts):
        copies[k].wait()
        take_planes(out, raw_ref, k * (vecs // parts), vecs // parts, rows, depth)


def link_kernel(depth, half, pick_ref, far_ref, came_ref, table_ref, top_ref, sem):
    core = pick_ref[1]
    copy = pltpu.make_async_copy(far_ref.at[pick_ref[2]], table_ref.at[core], sem)
    copy.start()
    table_ref[1 - core] = came_ref[...]
    copy.wait()

    def top(d, _):
        for h in range(2):
            top_ref[d, h * half : (h + 1) * half, :] = table_ref[h, 36 + d, pl.ds(depth - 1, half, stride=depth), :]
        return 0

    lax.fori_loop(0, 18, top, 0, unroll=6)


def shift_kernel(depth, table_ref, behind_ref):
    count = table_ref.shape[2]
    half = count // depth
    lane = lane_index((count, LANES))

    def shift(d, _):
        for h in range(2):
            behind_ref[h, d] = behind_x(table_ref[h, d], lane)
        low, high = table_ref[0, 18 + d], table_ref[1, 18 + d]
        for h, here, wrap in ((0, low, high), (1, high, low)):
            before = wrap[count - depth :]
            if half > 1:
                before = jnp.concatenate([before, here[: count - depth]], axis=0)
            behind_ref[h, 18 + d] = behind_y(here, before, lane)
        return 0

    lax.fori_loop(0, 18, shift, 0, unroll=3)


def multiply_into(total, field, link, adjoint):
    for col in range(3):
        re, im = field(col), field(3 + col)
        for row in range(3):
            entry = col * 3 + row if adjoint else row * 3 + col
            a, b = link(entry), link(9 + entry)
            if adjoint:
                total[row] = total[row] + a * re + b * im
                total[3 + row] = total[3 + row] + a * im - b * re
            else:
                total[row] = total[row] + a * re - b * im
                total[3 + row] = total[3 + row] + a * im + b * re


def rows_of(ref, c, z, depth, first, vecs):
    half = ref.shape[2] // depth
    row = lax.rem(c, half) * depth + z

    def link(k):
        return jnp.broadcast_to(ref[c // half, first + k, pl.ds(row, 1), :], (vecs, LANES))

    return link


def edge_rows(ref, c, vecs):
    def link(k):
        return jnp.broadcast_to(ref[k, pl.ds(c, 1), :], (vecs, LANES))

    return link


def forward_hops(total, cur, up, table, c, z, depth, lane):
    rows, _, vecs, _ = cur.shape
    after = lax.rem(c + 1, rows)
    multiply_into(total, lambda q: ahead_x(cur[c, q], lane), rows_of(table, c, z, depth, 0, vecs), False)
    multiply_into(
        total, lambda q: ahead_y(cur[c, q], cur[after, q], lane), rows_of(table, c, z, depth, 18, vecs), False
    )
    if up is not None:
        multiply_into(total, lambda q: up[c, q], rows_of(table, c, z, depth, 36, vecs), False)


def backward_hops(total, cur, down, table, behind, c, z, depth, lane):
    rows, _, vecs, _ = cur.shape
    before = lax.rem(c + rows - 1, rows)
    multiply_into(total, lambda q: behind_x(cur[c, q], lane), rows_of(behind, c, z, depth, 0, vecs), True)
    multiply_into(
        total, lambda q: behind_y(cur[c, q], cur[before, q], lane), rows_of(behind, c, z, depth, 18, vecs), True
    )
    if down is not None:
        multiply_into(total, lambda q: down[c, q], rows_of(table, c, z - 1, depth, 36, vecs), True)


def part_kernel(depth, pieces, todo, factor, first, table_ref, behind_ref, *refs):
    refs = list(refs)
    cur = plane_refs([refs.pop(0) for _ in pieces], pieces)
    done = [pieces[k] for k in todo]
    old = None if first else plane_refs([refs.pop(0) for _ in todo], done)
    out = plane_refs(refs, done)
    rows, _, vecs, _ = cur[0].shape
    lane = lane_index((vecs, LANES))
    for z in out:

        def body(c, _, z=z):
            total = [cur[z][c, q] for q in range(6)]
            forward_hops(total, cur[z], cur.get(z + 1), table_ref, c, z, depth, lane)
            backward_hops(total, cur[z], cur.get(z - 1), table_ref, behind_ref, c, z, depth, lane)
            for q in range(6):
                value = total[q] * factor
                out[z][c, q] = value if first else value - old[z][c, q]
            return 0

        lax.fori_loop(0, rows, body, 0)


def close_kernel(factor, behind, *refs):
    part_ref, out_ref = refs[-2].at[0], refs[-1].at[0]
    rows, _, vecs, _ = out_ref.shape

    def body(c, _):
        total = [jnp.zeros((vecs, LANES), F32) for _ in range(6)]
        for k, back in enumerate(behind):
            links_ref, halo_ref = refs[2 * k : 2 * k + 2]
            multiply_into(total, lambda q: halo_ref[0, c, q], edge_rows(links_ref, c, vecs), back)
        for q in range(6):
            out_ref[c, q] = part_ref[c, q] + total[q] * factor
        return 0

    lax.fori_loop(0, rows, body, 0)


def halves(x):
    high = x.astype(BF16)
    return high, (x - high.astype(F32)).astype(BF16)


def high_low(tiles):
    pairs = [halves(jnp.concatenate(tiles[k : k + 3], axis=1)) for k in (0, 3)]
    return [pairs[0][0], pairs[1][0], pairs[0][1], pairs[1][1]]


def products(acc_ref, rows, own, sides):
    group = min(rows, GROUP)
    assert rows % group == 0

    def body(step, _):
        stacks = [[], []]
        for k in range(group):
            for stack, tiles in zip(stacks, sides(group * step + k)):
                stack.append(jnp.concatenate(high_low(tiles), axis=0))
        left, right = [jnp.concatenate(s, axis=1) for s in stacks]
        right = jnp.concatenate([left if own else jnp.zeros_like(left), right], axis=0)
        acc_ref[...] += lax.dot_general(left, right, (((1,), (1,)), ((), ())), preferred_element_type=F32)
        return 0

    lax.fori_loop(0, rows // group, body, 0)


def packed_product(acc, n):
    acc = acc[0 : 2 * n] + acc[2 * n : 4 * n]
    acc = acc + pltpu.roll(acc, LANES - 2 * n, 1)
    re, im = acc[0:n], acc[n : 2 * n]
    real = re + pltpu.roll(im, LANES - n, 1)
    imag = re - pltpu.roll(im, n, 1)
    return jnp.where(lane_index((n, LANES)) % (2 * n) < n, real, imag)


def gram_kernel(depth, pieces, tasks, more, table_ref, *refs):
    refs = list(refs)
    acc_ref, out_ref = refs.pop(), refs.pop()
    sofar_ref = refs.pop() if more else None
    cur = plane_refs(refs, pieces)
    rows, _, vecs, _ = cur[tasks[0][0]].shape
    lane = lane_index((vecs, LANES))
    acc_ref[...] = jnp.zeros_like(acc_ref)
    for z, own, depth_hop in tasks:

        def sides(c, z=z, own=own, depth_hop=depth_hop):
            total = [jnp.zeros((vecs, LANES), F32) for _ in range(6)]
            if own:
                forward_hops(total, cur[z], cur[z + 1] if depth_hop else None, table_ref, c, z, depth, lane)
            else:
                up = cur[z + 1]
                multiply_into(total, lambda q: up[c, q], rows_of(table_ref, c, z, depth, 36, vecs), False)
            return [cur[z][c, q] for q in range(6)], total

        products(acc_ref, rows, own, sides)
    part = packed_product(acc_ref[...], vecs)
    out_ref[...] = part + sofar_ref[...] if more else part


def last_hop_kernel(links_ref, top_ref, above_ref, sofar_ref, out_ref, acc_ref):
    rows, _, vecs, _ = top_ref.shape[1:]
    acc_ref[...] = jnp.zeros_like(acc_ref)

    def sides(c):
        total = [jnp.zeros((vecs, LANES), F32) for _ in range(6)]
        multiply_into(total, lambda q: above_ref[0, c, q], edge_rows(links_ref, c, vecs), False)
        return [top_ref[0, c, q] for q in range(6)], total

    products(acc_ref, rows, False, sides)
    out_ref[...] = packed_product(acc_ref[...], vecs) + sofar_ref[...]


def norms_of(packed):
    n = packed.shape[0]
    diag = lane_index((n, LANES)) == lax.broadcasted_iota(jnp.int32, (n, LANES), 0)
    return jnp.where(diag, packed, 0.0)


def scatter_kernel(depth, planes, piece_ref, *refs):
    out_ref = refs[-1]
    rows, _, vecs, _ = piece_ref.shape[1:]
    stride = 6 * rows * depth

    def body(c, _):
        for k, z in enumerate(planes):
            for q in range(6):
                start = q * rows * depth + c * depth + z
                out_ref[pl.ds(start, vecs, stride=stride), :] = piece_ref[k, c, q]
        return 0

    lax.fori_loop(0, rows, body, 0, unroll=True)


def scale_out(field_ref, far_ref, slot, inverse, chunks, scale_ref, ready_ref, sems):
    n = inverse.shape[0]
    size = field_ref.shape[0] // n
    each = n // chunks
    scale_ref[...] = jnp.broadcast_to(inverse, (n, LANES))
    copies = []
    for j in range(chunks):

        def body(i, _, j=j):
            vec = j * each + i
            block = pl.ds(pl.multiple_of(vec * size, 8), size)
            ready_ref[block, :] = field_ref[block, :] * scale_ref[pl.ds(vec, 1), :]
            return 0

        lax.fori_loop(0, each, body, 0, unroll=4)
        part = pl.ds(j * each * size, each * size)
        target = pl.ds(slot * (n * size) + j * each * size, each * size)
        copies.append(pltpu.make_async_copy(ready_ref.at[part], far_ref.at[target], sems.at[j]))
        copies[-1].start()
    return copies


def mine_kernel(chunks, slot_ref, sum_ref, field_ref, far_ref, *scratch):
    inverse = lax.rsqrt(jnp.sum(norms_of(sum_ref[...]), axis=1, keepdims=True))
    for copy in scale_out(field_ref, far_ref, slot_ref[0], inverse, chunks, *scratch):
        copy.wait()


def other_kernel(chunks, slot_ref, mine_ref, other_ref, field_ref, _, far_ref, grams_ref, *scratch):
    parts = []
    for slot, ref in ((1 - slot_ref[0], other_ref), (slot_ref[0], mine_ref)):
        packed = ref[...]
        norm = norms_of(packed)
        parts.append((slot, packed, norm, lax.rsqrt(jnp.sum(norm, axis=1, keepdims=True))))
    copies = scale_out(field_ref, far_ref, 1 - slot_ref[0], parts[0][3], chunks, *scratch)
    n = mine_ref.shape[0]
    for slot, packed, norm, down in parts:
        across = lax.rsqrt(jnp.sum(norm, axis=0, keepdims=True)[:, 0:n])
        scale = down * across
        over_re, over_im = packed[:, 0:n], packed[:, n : 2 * n]
        hop_re, hop_im = packed[:, 4 * n : 5 * n], packed[:, 5 * n : 6 * n]
        grams_ref[slot, 0, 0] = over_re * scale
        grams_ref[slot, 0, 1] = over_im * scale
        grams_ref[slot, 1, 0] = (6.0 * over_re - (hop_re + hop_re.T)) * scale
        grams_ref[slot, 1, 1] = (6.0 * over_im - (hop_im - hop_im.T)) * scale
    for copy in copies:
        copy.wait()


def shifted(x, axis, by):
    n = lax.axis_size(axis)
    return lax.ppermute(x, axis, [(i, (i + by) % n) for i in range(n)])


def flipped(x, axis, bit):
    return lax.ppermute(x, axis, [(i, i ^ bit) for i in range(lax.axis_size(axis))])


def summed(x):
    size = lax.axis_size("sa")
    count = size.bit_length() - 1
    assert size == 1 << count
    bit = 1
    while bit < size:
        bits = (bit, 2 * bit, 3 * bit) if 4 * bit <= size else (bit,)
        x = sum([flipped(x, "sa", k) for k in bits], x)
        bit = bit * (4 if len(bits) == 3 else 2)
    return x


def on_device(links, vectors):
    slices, vecs, _, _, depth, plane = vectors.shape
    rows = plane // LANES
    assert slices == 2 and lax.axis_size("cfg") % 2 == 0 and lax.axis_size("ta") == 2
    pieces = pieces_of(depth)
    ends = [0] if len(pieces) == 1 else [0, len(pieces) - 1]
    inner = [k for k in range(len(pieces)) if k not in ends]
    core = lax.axis_index("ta")
    mine = lax.axis_index("cfg") % 2
    pick = jnp.stack([mine, core, 2 * core + mine]).astype(jnp.int32)
    field = [shape_of(len(p), rows, 6, vecs, LANES) for p in pieces]
    work = 1000 * LANES * vecs * rows
    many = vecs * 6 * rows * depth
    half = rows // 2
    sem = pltpu.SemaphoreType.DMA

    view = pltpu.with_memory_space_constraint(to_rows(vectors), pltpu.HBM)

    def taken(todo):
        return call(
            functools.partial(planes_kernel, depth, [pieces[k] for k in todo]), [field[k] for k in todo],
            view, pick=pick, far=(0,), scratch=[pltpu.VMEM((many, LANES), F32), sem((2,))], ops=1e5,
        )

    first, rest = ends[-1:], [k for k in range(len(pieces)) if k != ends[-1]]
    start = [None] * len(pieces)
    for k, x in zip(first, taken(first)):
        start[k] = x
    flat = links.reshape((links.shape[0], 54) + links.shape[-2:])
    given = lax.dynamic_index_in_dim(flat, 2 * (1 - core) + mine, 0, keepdims=False)
    came = flipped(given, "ta", 1)
    if rest:
        for k, x in zip(rest, taken(rest)):
            start[k] = x
    table, top_links = call(
        functools.partial(link_kernel, depth, half),
        [shape_of(2, 54, half * depth, LANES), shape_of(18, rows, LANES)],
        pltpu.with_memory_space_constraint(to_rows(links).reshape(-1, 54, half * depth, LANES), pltpu.HBM),
        to_rows(came).reshape(54, half * depth, LANES),
        pick=pick, far=(0,), scratch=[sem], ops=1e6,
    )
    prior = shifted(top_links, "sa", 1)
    behind = call(
        functools.partial(shift_kernel, depth), shape_of(2, 36, half * depth, LANES), table, ops=1e6
    )

    def advance(cur, old):
        factor = -(1.0 if old is None else 2.0) / SCALE
        low = shifted(cur[-1], "sa", 1)
        high = shifted(cur[0], "sa", -1)
        new = [None] * len(pieces)
        for todo in (inner, ends):
            if todo:
                got = call(
                    functools.partial(part_kernel, depth, pieces, todo, factor, old is None),
                    [field[k] for k in todo], table, behind, *cur, *([] if old is None else [old[k] for k in todo]),
                    ops=work * sum(len(pieces[k]) for k in todo),
                )
                for k, x in zip(todo, got):
                    new[k] = x
        sides = [(0, True, prior, low), (len(pieces) - 1, False, top_links, high)]
        for k in ends:
            used = [side for side in sides if side[0] == k]
            operands = [x for side in used for x in side[2:]]
            (new[k],) = call(
                functools.partial(close_kernel, factor, [side[1] for side in used]),
                [field[k]], *operands, new[k], ops=work / 6,
            )
        return new

    packed = shape_of(vecs, LANES)
    acc = [pltpu.VMEM((4 * vecs, 8 * vecs), F32)]

    def swapped(x):
        return flipped(x, "cfg", 1)

    def grams_of(planes, tasks, sofar):
        return call(
            functools.partial(gram_kernel, depth, [pieces[k] for k in planes], tasks, sofar is not None),
            packed, table, *[three[k] for k in planes], *([] if sofar is None else [sofar]),
            scratch=acc, ops=work * len(tasks) / 2,
        )

    one = advance(start, None)
    two = advance(one, start)
    three = advance(two, one)

    sofar = None
    if inner:
        middle = pieces[1]
        sofar = grams_of(inner, [(z, True, z + 1 in middle) for z in middle], None)
    above = shifted(three[0], "sa", -1)
    if len(ends) == 2:
        sofar = grams_of([0] + inner[:1], [(0, True, bool(inner))], sofar)
    tasks = [(depth - 1, True, False)]
    if depth > 1:
        tasks.append((depth - 2, False, True))
    sofar = grams_of(range(len(pieces)), tasks, sofar)
    sofar = call(
        last_hop_kernel, packed, top_links, three[-1], above, sofar,
        scratch=acc, ops=work / 4,
    )
    sum_mine = summed(sofar)
    sum_other = flipped(sum_mine, "cfg", 1)
    other = [swapped(x) for x in three]

    def scattered(planes):
        out = None
        for k in inner + ends:
            out = call(
                functools.partial(scatter_kernel, depth, pieces[k]), shape_of(many, LANES),
                planes[k], *([] if out is None else [out]), alias={} if out is None else {1: 0}, ops=1e5,
            )
        return out

    chunks = 2
    assert vecs % chunks == 0
    scratch = [pltpu.VMEM((vecs, LANES), F32), pltpu.VMEM((many, LANES), F32), sem((chunks,))]
    ours, theirs = scattered(three), scattered(other)
    (out,) = call(
        functools.partial(mine_kernel, chunks), [shape_of(2 * many, LANES)],
        sum_mine, ours, pick=pick, far_out=(0,), ops=1e6, scratch=scratch,
    )
    out, grams = call(
        functools.partial(other_kernel, chunks), [shape_of(2 * many, LANES), shape_of(2, 2, 2, vecs, vecs)],
        sum_mine, sum_other, theirs, out, pick=pick, far=(3,), far_out=(0,), ops=1e6, scratch=scratch,
        alias={4: 0},
    )
    return from_rows(out, vectors.shape), grams


def solution(mesh):
    in_specs = (P(None, None, None, None, None, "sa", "ta"), P("ta", None, None, None, "sa", None))
    out_specs = (
        P(("cfg", "ta"), None, None, None, "sa", None),
        P(("cfg", "ta"), None, None, None, None),
    )
    return jax.shard_map(on_device, mesh=mesh, in_specs=in_specs, out_specs=out_specs, check_vma=False)
```
